128 devices in a mesh: row: 8 (over y_hi, x), col: 16 (over z, y_lo, core).
Axes of the slice: x: 4, y: 4 (y_hi: 2, y_lo: 2; y = y_hi * 2 + y_lo), z: 4, core: 2. Of those that a mesh axis runs over, the one named last changes fastest.
Arguments:
- activations: float32 [4096, 8192], P('row', 'col')
- plan: int32 [3, 16], P(None, 'col'), may hold values 0 or 1
Outputs:
- rotated: float32 [4096, 8192], P('row', 'col')
- vectors: float32 [8192, 8192], P('row', 'col')
- spread: float32 [8192], P('col')
The draws below stay inside these ranges and needn't reach their ends.
All inputs are finite; a program needn't handle non-finite values. No bound on the sum of `plan` on one device may be relied on, other than what follows from the above.
Results may differ from the reference program's by a relative error of at most 0.0001.
Values sent between devices are 32-bit elements; how exact they have to be, the bound alone decides.
A program may use at most 64 MiB of HBM per device.

```python
import jax
import jax.numpy as jnp
from jax import lax

P_SIZE = 256
ROUNDS = 3
POLAR_STEPS = 3
PAIRS = 16
N = 8192
M = 4096


def draw_activations(key, part):
    keys = jax.random.split(jax.random.fold_in(key, 17), 4)
    noise = jax.random.normal(keys[0], (M, N), jnp.float32)
    left_factor = jax.random.normal(keys[1], (M, 8), jnp.float32)
    right_factor = jax.random.normal(keys[2], (8, N), jnp.float32)
    col_scale = jnp.exp(jax.random.uniform(keys[3], (N,), jnp.float32, 0.0, 2.302585))
    shared = jnp.dot(left_factor, right_factor) * (0.6 / 2.828427)
    values = (noise + shared) * col_scale[None, :]
    return values.astype(jnp.float32)


def place_ends(entries, key, smallest, top_value):
    dims = entries.shape
    spot = [jax.random.randint(jax.random.fold_in(key, axis), (), 0, dims[axis]) for axis in range(len(dims))]
    entries = entries.at[tuple(spot)].set(smallest)
    longest = dims.index(max(dims))
    spot[longest] = (spot[longest] + 1) % dims[longest]
    return entries.at[tuple(spot)].set(top_value)


def setup_inputs(seed: int = 0) -> dict:
    key_list = jax.random.split(jax.random.key(seed), 3)
    return {
        "activations": draw_activations(jax.random.fold_in(key_list[2], 71), 0),
        "plan": place_ends((jax.random.randint(key_list[1], (ROUNDS, PAIRS), 0, 2) < 1).astype(jnp.int32), jax.random.fold_in(key_list[1], 1), 0, 1),
    }


HIGH = lax.Precision.HIGHEST

def rotation(pair_gram):
    half_width = pair_gram.shape[0] // 2
    diagonal = jnp.diagonal(pair_gram) + 1e-06
    root_diag = jnp.sqrt(diagonal)
    coupling = pair_gram[:half_width, half_width:] / (root_diag[:half_width, None] * root_diag[None, half_width:])
    strength = jnp.sqrt(jnp.sum(coupling * coupling))
    scaled = coupling / (1.0 + strength)
    zeros_block = jnp.zeros((half_width, half_width), jnp.float32)
    generator = jnp.concatenate([jnp.concatenate([zeros_block, scaled], axis=1), jnp.concatenate([-scaled.T, zeros_block], axis=1)], axis=0)
    iterate = jnp.eye(2 * half_width, dtype=jnp.float32) + generator
    for polar_index in range(POLAR_STEPS):
        product = jnp.dot(iterate, iterate.T, precision=HIGH)
        iterate = 1.5 * iterate - 0.5 * jnp.dot(product, iterate, precision=HIGH)
    return iterate

def advance(turned, flags):
    chosen = (flags == 1)[None, :, None]
    first_panel = turned[:, :, :P_SIZE]
    second_panel = turned[:, :, P_SIZE:]
    moving = jnp.where(chosen, second_panel, first_panel)
    staying = jnp.where(chosen, first_panel, second_panel)
    arriving = jnp.roll(moving, 1, axis=1)
    return jnp.concatenate([staying, arriving], axis=2)

def reference(activations, plan):
    matrix = activations
    vectors = jnp.eye(N, dtype=jnp.float32)
    for round_index in range(ROUNDS):
        stacked = matrix.reshape(M, PAIRS, 2 * P_SIZE)
        grams = jnp.einsum('mpa,mpb->pab', stacked, stacked, precision=HIGH)
        rotations = jax.vmap(rotation)(grams)
        turned = jnp.einsum('mpa,pab->mpb', stacked, rotations, precision=HIGH)
        vec_stack = vectors.reshape(N, PAIRS, 2 * P_SIZE)
        turned_vec = jnp.einsum('mpa,pab->mpb', vec_stack, rotations, precision=HIGH)
        matrix = advance(turned, plan[round_index]).reshape(M, N)
        vectors = advance(turned_vec, plan[round_index]).reshape(N, N)
    squares = lax.optimization_barrier(jnp.sum(matrix * matrix, axis=0))
    spread = jnp.sqrt(squares / M)
    return (matrix, vectors, spread)
```

```python
import functools

import jax
import jax.numpy as jnp
from jax import lax
from jax.experimental import pallas as pl
from jax.experimental.pallas import tpu as pltpu
from jax.sharding import PartitionSpec as P

ROUNDS = 3
NY = 2
NCH = 2
MESH = pl.DeviceIdType.MESH
F32 = jnp.float32
BF16 = jnp.bfloat16


def split(x):
    hi = x.astype(BF16)
    lo = (x - hi.astype(F32)).astype(BF16)
    return hi, lo


def mm(a, b):
    return lax.dot_general(a, b, (((1,), (0,)), ((), ())), preferred_element_type=F32)


def mm3(a, b):
    ah, al = a
    bh, bl = b
    return mm(
        jnp.concatenate([ah, al, ah], axis=1), jnp.concatenate([bh, bh, bl], axis=0)
    )


def turn_blocks(b, bt, eye):
    bs, bts = split(b), split(bt)
    a = mm3(bs, bts)
    a_s = split(a)
    a2 = mm3(a_s, a_s)
    d1 = 0.25 * mm3(split(a2), a_s) - 0.75 * a2
    d1s = split(d1)
    w = 0.5 * a + 0.5 * d1 - 0.25 * mm3(d1s, a_s)
    e = mm3(d1s, d1s)
    ub = b - mm3(split(w), bs)
    d2 = 0.25 * mm3(split(e), d1s) - 0.75 * e
    d2s = split(d2)
    u = eye - w
    p = u - 0.5 * mm3(d2s, split(u))
    r = ub - 0.5 * mm3(d2s, split(ub))
    return p, r


def kernel(
    n_row, n_col, plan_ref, x_hbm, xo_hbm, vo_hbm, so_ref,
    stay, arr, mov, xh, xl, sth, stl, qm, qs, part, rs, ag, zbuf, nsend, nrecv,
    load_sem, arr_sem, varr_sem, xsend_sem, vsend_sem,
    rs_send, rs_recv, ag_send, ag_recv,
    vf_recv, vf_send, n_recv, n_send, out_sem,
):
    m, width = x_hbm.shape
    p = width // 2
    sl = p // n_row
    vr = width // n_row
    nv = 3 * vr
    qpr = n_col // n_row
    nx = n_row // NY
    rc = m // NCH
    r = lax.axis_index("row")
    c = lax.axis_index("col")
    y, x = r // nx, r % nx
    nxt, prv = (c + 1) % n_col, (c + n_col - 1) % n_col
    others = [(dy, dx) for dy in range(NY - 1, -1, -1) for dx in range(nx) if dy or dx]

    def peer(dy, dx):
        return ((y + dy) % NY) * nx + (x + dx) % nx

    barrier = pltpu.get_barrier_semaphore()
    for dy, dx in others:
        pl.semaphore_signal(barrier, inc=1, device_id={"row": peer(dy, dx), "col": c}, device_id_type=MESH)
    for rr in range(n_row):
        pl.semaphore_signal(barrier, inc=1, device_id={"row": rr, "col": nxt}, device_id_type=MESH)
        pl.semaphore_signal(barrier, inc=1, device_id={"row": rr, "col": prv}, device_id_type=MESH)

    load = pltpu.make_async_copy(x_hbm.at[:, pl.ds(0, p)], stay.at[pl.ds(0, m)], load_sem)
    load.start()
    for ch in range(NCH):
        pltpu.make_async_copy(
            x_hbm.at[pl.ds(ch * rc, rc), pl.ds(p, p)],
            arr.at[0, pl.ds(ch * rc, rc)],
            arr_sem.at[0, ch],
        ).start()

    lane = lax.broadcasted_iota(jnp.int32, (vr, p), 1)
    row_id = lax.broadcasted_iota(jnp.int32, (vr, p), 0) + r * vr
    stay[pl.ds(m, vr)] = jnp.where(row_id == lane, 1.0, 0.0).astype(F32)
    arr[0, pl.ds(m, vr)] = jnp.where(row_id == lane + p, 1.0, 0.0).astype(F32)
    stay[pl.ds(m + vr, 2 * vr)] = jnp.zeros((2 * vr, p), F32)
    arr[0, pl.ds(m + vr, 2 * vr)] = jnp.zeros((2 * vr, p), F32)
    for k in range(1, ROUNDS):
        arr[k, pl.ds(m, vr)] = jnp.zeros((vr, p), F32)
    zbuf[...] = jnp.zeros_like(zbuf)

    def zero_block(j, panel):
        return pltpu.make_async_copy(
            zbuf,
            vo_hbm.at[pl.ds(j * width, width), pl.ds(panel * p, p)],
            out_sem.at[1 + 2 * j + panel],
        )

    lag = [(c + n_col - (qpr * r + j)) % n_col for j in range(qpr)]
    for j in range(qpr):
        @pl.when(lag[j] > 2)
        def _():
            zero_block(j, 0).start()

        @pl.when((lag[j] < 1) | (lag[j] > 3))
        def _():
            zero_block(j, 1).start()

    load.wait()
    pl.semaphore_wait(barrier, len(others) + 2 * n_row)

    eye = jnp.where(
        lax.broadcasted_iota(jnp.int32, (p, p), 0) == lax.broadcasted_iota(jnp.int32, (p, p), 1), 1.0, 0.0
    ).astype(F32)

    def move_x(k, ch):
        return pltpu.make_async_remote_copy(
            src_ref=mov.at[k, pl.ds(ch * rc, rc)],
            dst_ref=arr.at[k + 1, pl.ds(ch * rc, rc)],
            send_sem=xsend_sem.at[k, ch],
            recv_sem=arr_sem.at[k + 1, ch],
            device_id={"row": r, "col": nxt},
            device_id_type=MESH,
        )

    def move_x_last(ch):
        return pltpu.make_async_remote_copy(
            src_ref=mov.at[ROUNDS - 1, pl.ds(ch * rc, rc)],
            dst_ref=xo_hbm.at[pl.ds(ch * rc, rc), pl.ds(p, p)],
            send_sem=xsend_sem.at[ROUNDS - 1, ch],
            recv_sem=arr_sem.at[ROUNDS, ch],
            device_id={"row": r, "col": nxt},
            device_id_type=MESH,
        )

    def move_v(k):
        return pltpu.make_async_remote_copy(
            src_ref=mov.at[k, pl.ds(m, 2 * vr)],
            dst_ref=arr.at[k + 1, pl.ds(m + vr, 2 * vr)],
            send_sem=vsend_sem.at[k],
            recv_sem=varr_sem.at[k + 1],
            device_id={"row": r, "col": nxt},
            device_id_type=MESH,
        )

    def scatter(k, i):
        dy, dx = others[i]
        to = peer(dy, dx)
        return pltpu.make_async_remote_copy(
            src_ref=part.at[to],
            dst_ref=rs.at[k, i],
            send_sem=rs_send.at[i],
            recv_sem=rs_recv.at[i],
            device_id={"row": to, "col": c},
            device_id_type=MESH,
        )

    def gather(k, i):
        dy, dx = others[i]
        mine = ag.at[k, pl.ds(pl.multiple_of(r * sl, sl), sl)]
        return pltpu.make_async_remote_copy(
            src_ref=mine,
            dst_ref=mine,
            send_sem=ag_send.at[i],
            recv_sem=ag_recv.at[i],
            device_id={"row": peer(dy, dx), "col": c},
            device_id_type=MESH,
        )

    def lhs_rows(start, size):
        h = xh[pl.ds(start, size), :]
        return jnp.concatenate([h, xl[pl.ds(start, size), :], h], axis=1)

    def one_round(k, carry):
        s = stay[...]
        sh, slo = split(s)
        xh[:, pl.ds(0, p)] = sh
        xl[:, pl.ds(0, p)] = slo
        sth[...] = sh[:m].T
        stl[...] = slo[:m].T
        n1 = jnp.sum(s[:m] * s[:m], axis=0, keepdims=True)
        n2 = jnp.zeros((1, p), F32)
        g = jnp.zeros((p, p), F32)
        for ch in range(NCH):
            rows = pl.ds(ch * rc, rc)
            block = arr.at[k, rows]
            pltpu.make_async_copy(block, block, arr_sem.at[k, ch]).wait()
            a = arr[k, rows]
            ah, al = split(a)
            xh[rows, pl.ds(p, p)] = ah
            xl[rows, pl.ds(p, p)] = al
            n2 = n2 + jnp.sum(a * a, axis=0, keepdims=True)
            th = sth[:, rows]
            g = g + mm3((th, stl[:, rows]), (ah, al))
        which = lax.broadcasted_iota(jnp.int32, (8, p), 0)
        norms = jnp.where(which == 0, n1, jnp.where(which == 1, n2, 0.0))
        for i in range(n_row):
            part[i, pl.ds(0, sl)] = g[i * sl:(i + 1) * sl]
            part[i, pl.ds(sl, 8)] = norms
        for i in range(len(others)):
            scatter(k, i).start()
        total = part[r]
        for i in range(len(others) - 1, -1, -1):
            scatter(k, i).wait_recv()
            total = total + rs[k, i]
        root = jnp.sqrt(total[sl:sl + 8] + 1e-06)
        root1, root2 = root[0:1], root[1:2]
        on_diag = lax.broadcasted_iota(jnp.int32, (sl, p), 1) == lax.broadcasted_iota(jnp.int32, (sl, p), 0) + r * sl
        root_col = jnp.sum(jnp.where(on_diag, root1, 0.0), axis=1, keepdims=True)
        ag[k, pl.ds(pl.multiple_of(r * sl, sl), sl)] = total[:sl] / (root_col * root2)
        for i in range(len(others)):
            gather(k, i).start()
        for i in range(len(others) - 1, -1, -1):
            gather(k, i).wait_recv()
        coupling = ag[k]
        strength = jnp.sqrt(jnp.sum(coupling * coupling, keepdims=True))
        b = coupling / (1.0 + strength)
        bt = b.T
        p1, q12 = turn_blocks(b, bt, eye)
        p2, q12t = turn_blocks(bt, b, eye)
        chosen = jnp.full((1, p), plan_ref[k, 0], jnp.int32) == 1
        for ref, top, bottom in (
            (qm, jnp.where(chosen, q12, p1), jnp.where(chosen, p2, -q12t)),
            (qs, jnp.where(chosen, p1, q12), jnp.where(chosen, -q12t, p2)),
        ):
            for at, piece in ((0, top), (p, bottom)):
                hi, lo = split(piece)
                ref[pl.ds(at, p)] = hi
                ref[pl.ds(2 * p + at, p)] = hi
                ref[pl.ds(4 * p + at, p)] = lo
        for ch in range(NCH):
            mov[k, pl.ds(ch * rc, rc)] = mm(lhs_rows(ch * rc, rc), qm[...])

            @pl.when(k < ROUNDS - 1)
            def _():
                move_x(k, ch).start()

            @pl.when(k == ROUNDS - 1)
            def _():
                move_x_last(ch).start()

        for ch in range(NCH):
            stay[pl.ds(ch * rc, rc)] = mm(lhs_rows(ch * rc, rc), qs[...])

        @pl.when(k > 0)
        def _():
            block = arr.at[k, pl.ds(m + vr, 2 * vr)]
            pltpu.make_async_copy(block, block, varr_sem.at[k]).wait()

        vh, vl = split(arr[k, pl.ds(m, nv)])
        xh[pl.ds(m, nv), pl.ds(p, p)] = vh
        xl[pl.ds(m, nv), pl.ds(p, p)] = vl
        v_lhs = lhs_rows(m, nv)
        mov[k, pl.ds(m, nv)] = mm(v_lhs, qm[...])
        stay[pl.ds(m, nv)] = mm(v_lhs, qs[...])

        @pl.when(k < ROUNDS - 1)
        def _():
            move_v(k).start()

        for i in range(len(others)):
            scatter(k, i).wait_send()
            gather(k, i).wait_send()
        return carry

    lax.fori_loop(0, ROUNDS, one_round, 0)

    for which, ref in ((0, stay[pl.ds(0, m)]), (1, mov[ROUNDS - 1, pl.ds(0, m)])):
        nsend[which] = jnp.broadcast_to(jnp.sum(ref * ref, axis=0, keepdims=True), (8, p))

    def norm_stay(i):
        dy, dx = others[i]
        return pltpu.make_async_remote_copy(
            src_ref=nsend.at[0], dst_ref=nrecv.at[0, r], send_sem=n_send.at[0, i], recv_sem=n_recv.at[0],
            device_id={"row": peer(dy, dx), "col": c}, device_id_type=MESH,
        )

    def norm_move(i):
        return pltpu.make_async_remote_copy(
            src_ref=nsend.at[1], dst_ref=nrecv.at[1, r], send_sem=n_send.at[1, i], recv_sem=n_recv.at[1],
            device_id={"row": (r + i) % n_row, "col": nxt}, device_id_type=MESH,
        )

    norm_own = pltpu.make_async_copy(nsend.at[0], nrecv.at[0, r], n_recv.at[0])
    for i in range(n_row):
        norm_move(i).start()
    for i in range(len(others)):
        norm_stay(i).start()
    norm_own.start()

    stay_out = pltpu.make_async_copy(stay.at[pl.ds(0, m)], xo_hbm.at[:, pl.ds(0, p)], out_sem.at[0])
    stay_out.start()

    def v_piece(d, panel):
        q = (c + n_col - d) % n_col
        owner, j = q // qpr, q % qpr
        src = (mov.at[ROUNDS - 1] if panel else stay).at[pl.ds(m + d * vr, vr)]
        dst = vo_hbm.at[pl.ds(pl.multiple_of(j * width + r * vr, vr), vr), pl.ds(panel * p, p)]
        local = pltpu.make_async_copy(src, dst, vf_recv.at[j, panel])
        far = pltpu.make_async_remote_copy(
            src_ref=src, dst_ref=dst, send_sem=vf_send.at[d, panel], recv_sem=vf_recv.at[j, panel],
            device_id={"row": owner, "col": nxt if panel else c}, device_id_type=MESH,
        )
        return owner, local, far

    for d in range(3):
        owner, local, far = v_piece(d, 0)

        @pl.when(owner == r)
        def _():
            local.start()

        @pl.when(owner != r)
        def _():
            far.start()

        v_piece(d, 1)[2].start()

    for panel in range(2):
        pltpu.make_async_copy(nrecv.at[panel], nrecv.at[panel], n_recv.at[panel]).wait()
        sums = nrecv[panel, 0]
        for i in range(1, n_row):
            sums = sums + nrecv[panel, i]
        so_ref[:, pl.ds(panel * p, p)] = jnp.sqrt(sums[0:1] / (m * n_row))

    for i in range(len(others)):
        norm_stay(i).wait_send()
    for i in range(n_row):
        norm_move(i).wait_send()
    for k in range(ROUNDS):
        for ch in range(NCH):
            if k < ROUNDS - 1:
                move_x(k, ch).wait_send()
            else:
                move_x_last(ch).wait_send()
                move_x_last(ch).wait_recv()
        if k < ROUNDS - 1:
            move_v(k).wait_send()
    for d in range(3):
        owner, local, far = v_piece(d, 0)

        @pl.when(owner != r)
        def _():
            far.wait_send()

        v_piece(d, 1)[2].wait_send()
    for j in range(qpr):
        for panel, there in ((0, lag[j] <= 2), (1, (lag[j] >= 1) & (lag[j] <= 3))):
            block = vo_hbm.at[pl.ds(j * width, width), pl.ds(panel * p, p)]

            @pl.when(there)
            def _():
                pltpu.make_async_copy(block, block, vf_recv.at[j, panel]).wait()

            @pl.when(jnp.logical_not(there))
            def _():
                zero_block(j, panel).wait()
    stay_out.wait()


def per_device(activations, plan):
    n_row, n_col = lax.axis_size("row"), lax.axis_size("col")
    m, width = activations.shape
    p = width // 2
    sl = p // n_row
    vr = width // n_row
    rows = m + 3 * vr
    qpr = n_col // n_row
    dma = pltpu.SemaphoreType.DMA
    rotated, vectors, spread = pl.pallas_call(
        functools.partial(kernel, n_row, n_col),
        out_shape=(
            jax.ShapeDtypeStruct((m, width), F32),
            jax.ShapeDtypeStruct((qpr * width, width), F32),
            jax.ShapeDtypeStruct((1, width), F32),
        ),
        in_specs=[
            pl.BlockSpec(memory_space=pltpu.SMEM),
            pl.BlockSpec(memory_space=pl.ANY),
        ],
        out_specs=(
            pl.BlockSpec(memory_space=pl.ANY),
            pl.BlockSpec(memory_space=pl.ANY),
            pl.BlockSpec(memory_space=pltpu.VMEM),
        ),
        scratch_shapes=[
            pltpu.VMEM((rows, p), F32),
            pltpu.VMEM((ROUNDS, rows, p), F32),
            pltpu.VMEM((ROUNDS, rows, p), F32),
            pltpu.VMEM((rows, width), BF16),
            pltpu.VMEM((rows, width), BF16),
            pltpu.VMEM((p, m), BF16),
            pltpu.VMEM((p, m), BF16),
            pltpu.VMEM((3 * width, p), BF16),
            pltpu.VMEM((3 * width, p), BF16),
            pltpu.VMEM((n_row, sl + 8, p), F32),
            pltpu.VMEM((ROUNDS, n_row - 1, sl + 8, p), F32),
            pltpu.VMEM((ROUNDS, p, p), F32),
            pltpu.VMEM((width, p), F32),
            pltpu.VMEM((2, 8, p), F32),
            pltpu.VMEM((2, n_row, 8, p), F32),
            dma,
            dma((ROUNDS + 1, NCH)),
            dma((ROUNDS,)),
            dma((ROUNDS, NCH)),
            dma((ROUNDS,)),
            dma((n_row - 1,)),
            dma((n_row - 1,)),
            dma((n_row - 1,)),
            dma((n_row - 1,)),
            dma((qpr, 2)),
            dma((3, 2)),
            dma((2,)),
            dma((2, n_row)),
            dma((1 + 2 * qpr,)),
        ],
        compiler_params=pltpu.CompilerParams(collective_id=0, has_side_effects=True, vmem_limit_bytes=48 * 2**20),
    )(plan, activations)
    return rotated, vectors, spread.reshape(width)


def solution(mesh):
    in_specs = (P("row", "col"), P(None, "col"))
    out_specs = (P("row", "col"), P("row", "col"), P("col"))
    return jax.shard_map(
        per_device, mesh=mesh, in_specs=in_specs, out_specs=out_specs, check_vma=False
    )
```

```python
import functools

import jax
import jax.numpy as jnp
from jax import lax
from jax.experimental import pallas as pl
from jax.experimental.pallas import tpu as pltpu
from jax.sharding import PartitionSpec as P

ROUNDS = 3
NY = 2
NCH = 2
MESH = pl.DeviceIdType.MESH
F32 = jnp.float32
BF16 = jnp.bfloat16


def split(x):
    hi = x.astype(BF16)
    lo = (x - hi.astype(F32)).astype(BF16)
    return hi, lo


def mm(a, b):
    return lax.dot_general(a, b, (((1,), (0,)), ((), ())), preferred_element_type=F32)


def mm3(a, b):
    ah, al = a
    bh, bl = b
    return mm(
        jnp.concatenate([ah, al, ah], axis=1), jnp.concatenate([bh, bh, bl], axis=0)
    )


def turn_blocks(b, bt, eye):
    bs, bts = split(b), split(bt)
    a = mm3(bs, bts)
    a_s = split(a)
    a2 = mm3(a_s, a_s)
    d1 = 0.25 * mm3(split(a2), a_s) - 0.75 * a2
    d1s = split(d1)
    w = 0.5 * a + 0.5 * d1 - 0.25 * mm3(d1s, a_s)
    e = mm3(d1s, d1s)
    ub = b - mm3(split(w), bs)
    d2 = 0.25 * mm3(split(e), d1s) - 0.75 * e
    d2s = split(d2)
    u = eye - w
    p = u - 0.5 * mm3(d2s, split(u))
    r = ub - 0.5 * mm3(d2s, split(ub))
    return p, r


def kernel(
    n_row, n_col, plan_ref, x_hbm, xo_ref, vo_ref, so_ref,
    stay, vst, arr, mov, xh, xl, sth, stl, qm, qs, part, rs, ag, vpre, vmov, nsend, nrecv,
    load_sem, arr_sem, varr_sem, xsend_sem, vsend_sem,
    rs_send, rs_recv, ag_send, ag_recv,
    vp_send, vp_recv, vf_send, vf_recv, vm_send, n_send, n_recv,
):
    m, width = x_hbm.shape
    p = width // 2
    sl = p // n_row
    vr = width // n_row
    nv = 3 * vr
    qpr = n_col // n_row
    nx = n_row // NY
    rc = m // NCH
    last = ROUNDS - 1
    r = lax.axis_index("row")
    c = lax.axis_index("col")
    y, x = r // nx, r % nx
    nxt, prv = (c + 1) % n_col, (c + n_col - 1) % n_col
    others = [(dy, dx) for dy in range(NY - 1, -1, -1) for dx in range(nx) if dy or dx]

    def peer(dy, dx):
        return ((y + dy) % NY) * nx + (x + dx) % nx

    def greet(row, col):
        pl.semaphore_signal(barrier, inc=1, device_id={"row": row, "col": col}, device_id_type=MESH)

    def remote(src, dst, send, recv, row, col):
        return pltpu.make_async_remote_copy(
            src_ref=src, dst_ref=dst, send_sem=send, recv_sem=recv,
            device_id={"row": row, "col": col}, device_id_type=MESH,
        )

    def await_bytes(ref, sem):
        pltpu.make_async_copy(ref, ref, sem).wait()

    barrier = pltpu.get_barrier_semaphore()
    for dy, dx in others:
        greet(peer(dy, dx), c)
    for rr in range(n_row):
        greet(rr, nxt)
        greet(rr, prv)

    load = pltpu.make_async_copy(x_hbm.at[:, pl.ds(0, p)], stay, load_sem)
    load.start()
    for ch in range(NCH):
        pltpu.make_async_copy(
            x_hbm.at[pl.ds(ch * rc, rc), pl.ds(p, p)],
            arr.at[0, pl.ds(ch * rc, rc)],
            arr_sem.at[0, ch],
        ).start()

    lane = lax.broadcasted_iota(jnp.int32, (vr, p), 1)
    row_id = lax.broadcasted_iota(jnp.int32, (vr, p), 0) + r * vr
    vst[0, pl.ds(0, vr)] = jnp.where(row_id == lane, 1.0, 0.0).astype(F32)
    arr[0, pl.ds(m, vr)] = jnp.where(row_id == lane + p, 1.0, 0.0).astype(F32)
    vst[0, pl.ds(vr, 2 * vr)] = jnp.zeros((2 * vr, p), F32)
    arr[0, pl.ds(m + vr, 2 * vr)] = jnp.zeros((2 * vr, p), F32)
    for k in range(1, ROUNDS):
        arr[k, pl.ds(m, vr)] = jnp.zeros((vr, p), F32)

    lag = [(c + n_col - (qpr * r + j)) % n_col for j in range(qpr)]
    for j in range(qpr):
        @pl.when(lag[j] > 2)
        def _():
            vo_ref[pl.ds(j * width, width), pl.ds(0, p)] = jnp.zeros((width, p), F32)

        @pl.when((lag[j] < 1) | (lag[j] > 3))
        def _():
            vo_ref[pl.ds(j * width, width), pl.ds(p, p)] = jnp.zeros((width, p), F32)

        @pl.when(lag[j] == 0)
        def _():
            vpre[j, 1] = jnp.zeros((width, p), F32)

        @pl.when(lag[j] == 2)
        def _():
            vpre[j, 0] = jnp.zeros((width, p), F32)

    eye = jnp.where(
        lax.broadcasted_iota(jnp.int32, (p, p), 0) == lax.broadcasted_iota(jnp.int32, (p, p), 1), 1.0, 0.0
    ).astype(F32)
    load.wait()

    def chunk(ch):
        return pl.ds(ch * rc, rc)

    def move_x(k, ch):
        return remote(
            mov.at[k, chunk(ch)], arr.at[k + 1, chunk(ch)], xsend_sem.at[k, ch], arr_sem.at[k + 1, ch], r, nxt
        )

    def move_x_last(ch):
        return remote(
            mov.at[last, chunk(ch)], xo_ref.at[chunk(ch), pl.ds(p, p)], xsend_sem.at[last, ch],
            arr_sem.at[ROUNDS, ch], r, nxt,
        )

    def move_v(k):
        return remote(
            mov.at[k, pl.ds(m, 2 * vr)], arr.at[k + 1, pl.ds(m + vr, 2 * vr)],
            vsend_sem.at[k], varr_sem.at[k + 1], r, nxt,
        )

    def scatter(k, i):
        to = peer(*others[i])
        return remote(part.at[to], rs.at[k, i], rs_send.at[i], rs_recv.at[i], to, c)

    def gather(k, i):
        mine = ag.at[k, pl.ds(pl.multiple_of(r * sl, sl), sl)]
        return remote(mine, mine, ag_send.at[i], ag_recv.at[i], peer(*others[i]), c)

    def norm_stay(i):
        return remote(nsend.at[0], nrecv.at[0, r], n_send.at[0, i], n_recv.at[0], peer(*others[i]), c)

    def norm_move(i):
        return remote(nsend.at[1], nrecv.at[1, r], n_send.at[1, i], n_recv.at[1], (r + i) % n_row, nxt)

    def home(d):
        q = (c + n_col - d) % n_col
        return q // qpr, q % qpr

    my_rows = pl.ds(pl.multiple_of(r * vr, vr), vr)

    def state_stay(d):
        owner, j = home(d)
        return vst.at[last, pl.ds(d * vr, vr)], vpre.at[j, 0, my_rows], vp_recv.at[j, 0], owner

    def state_stay_far(d):
        src, dst, sem, owner = state_stay(d)
        return remote(src, dst, vp_send.at[0, d], sem, owner, c)

    def state_move(d):
        owner, j = home(d)
        return remote(
            mov.at[last - 1, pl.ds(m + d * vr, vr)], vpre.at[j, 1, my_rows], vp_send.at[1, d], vp_recv.at[j, 1],
            owner, nxt,
        )

    def last_slice(d):
        owner, j = home(d)
        dst = vo_ref.at[pl.ds(pl.multiple_of(j * width + r * vr, vr), vr), pl.ds(p, p)]
        return remote(mov.at[last, pl.ds(m + d * vr, vr)], dst, vf_send.at[d], vf_recv.at[j], owner, nxt)

    def last_block(j):
        dst = vo_ref.at[pl.ds(j * width, width), pl.ds(p, p)]
        return remote(vmov.at[j], dst, vm_send.at[j], vf_recv.at[j], r, nxt)

    def lhs_rows(start, size):
        h = xh[pl.ds(start, size), :]
        return jnp.concatenate([h, xl[pl.ds(start, size), :], h], axis=1)

    def lhs_of(first, second):
        h1, l1 = split(first)
        h2, l2 = split(second)
        return jnp.concatenate([h1, h2, l1, l2, h1, h2], axis=1)

    def one_round(k, carry):
        s = stay[...]
        sh, slo = split(s)
        xh[:, pl.ds(0, p)] = sh
        xl[:, pl.ds(0, p)] = slo
        sth[...] = sh.T
        stl[...] = slo.T
        n1 = jnp.sum(s * s, axis=0, keepdims=True)
        n2 = jnp.zeros((1, p), F32)
        g = jnp.zeros((p, p), F32)
        for ch in range(NCH):
            rows = chunk(ch)
            await_bytes(arr.at[k, rows], arr_sem.at[k, ch])
            a = arr[k, rows]
            ah, al = split(a)
            xh[rows, pl.ds(p, p)] = ah
            xl[rows, pl.ds(p, p)] = al
            n2 = n2 + jnp.sum(a * a, axis=0, keepdims=True)
            th = sth[:, rows]
            g = g + mm3((th, stl[:, rows]), (ah, al))
        which = lax.broadcasted_iota(jnp.int32, (8, p), 0)
        norms = jnp.where(which == 0, n1, jnp.where(which == 1, n2, 0.0))
        for i in range(n_row):
            part[i, pl.ds(0, sl)] = g[i * sl:(i + 1) * sl]
            part[i, pl.ds(sl, 8)] = norms

        @pl.when(k == 0)
        def _():
            pl.semaphore_wait(barrier, len(others) + 2 * n_row)

        for i in range(len(others)):
            scatter(k, i).start()
        total = part[r]
        for i in range(len(others) - 1, -1, -1):
            scatter(k, i).wait_recv()
            total = total + rs[k, i]
        root = jnp.sqrt(total[sl:sl + 8] + 1e-06)
        root1, root2 = root[0:1], root[1:2]
        on_diag = lax.broadcasted_iota(jnp.int32, (sl, p), 1) == lax.broadcasted_iota(jnp.int32, (sl, p), 0) + r * sl
        root_col = jnp.sum(jnp.where(on_diag, root1, 0.0), axis=1, keepdims=True)
        ag[k, pl.ds(pl.multiple_of(r * sl, sl), sl)] = total[:sl] / (root_col * root2)
        for i in range(len(others)):
            gather(k, i).start()
        for i in range(len(others) - 1, -1, -1):
            gather(k, i).wait_recv()
        coupling = ag[k]
        strength = jnp.sqrt(jnp.sum(coupling * coupling, keepdims=True))
        b = coupling / (1.0 + strength)
        bt = b.T
        p1, q12 = turn_blocks(b, bt, eye)
        p2, q12t = turn_blocks(bt, b, eye)
        chosen = jnp.full((1, p), plan_ref[0, k], jnp.int32) == 1
        for ref, top, bottom in (
            (qm, jnp.where(chosen, q12, p1), jnp.where(chosen, p2, -q12t)),
            (qs, jnp.where(chosen, p1, q12), jnp.where(chosen, -q12t, p2)),
        ):
            for at, piece in ((0, top), (p, bottom)):
                hi, lo = split(piece)
                ref[pl.ds(at, p)] = hi
                ref[pl.ds(2 * p + at, p)] = hi
                ref[pl.ds(4 * p + at, p)] = lo
        moving = mm(lhs_rows(0, m), qm[...])
        mov[k, pl.ds(0, m)] = moving

        @pl.when(k < last)
        def _():
            for ch in range(NCH):
                move_x(k, ch).start()

        @pl.when(k == last)
        def _():
            t = mov[last, pl.ds(0, m)]
            nsend[1] = jnp.broadcast_to(jnp.sum(t * t, axis=0, keepdims=True), (8, p))
            for i in range(n_row):
                norm_move(i).start()
            for ch in range(NCH):
                move_x_last(ch).start()

        stay[...] = mm(lhs_rows(0, m), qs[...])

        @pl.when(k > 0)
        def _():
            await_bytes(arr.at[k, pl.ds(m + vr, 2 * vr)], varr_sem.at[k])

        v_lhs = lhs_of(vst[k], arr[k, pl.ds(m, nv)])
        mov[k, pl.ds(m, nv)] = mm(v_lhs, qm[...])

        @pl.when(k < last)
        def _():
            vst[k + 1] = mm(lhs_of(vst[k], arr[k, pl.ds(m, nv)]), qs[...])
            move_v(k).start()

        @pl.when(k == last - 1)
        def _():
            for d in range(2):
                src, dst, sem, owner = state_stay(d)
                state_move(d).start()

                @pl.when(owner == r)
                def _():
                    pltpu.make_async_copy(src, dst, sem).start()

                @pl.when(owner != r)
                def _():
                    state_stay_far(d).start()

        for i in range(len(others)):
            scatter(k, i).wait_send()
            gather(k, i).wait_send()
        return carry

    lax.fori_loop(0, ROUNDS, one_round, 0)

    even = c % 2 == 0

    @pl.when(jnp.logical_not(even))
    def _():
        for d in range(3):
            last_slice(d).start()

    t = stay[...]
    nsend[0] = jnp.broadcast_to(jnp.sum(t * t, axis=0, keepdims=True), (8, p))
    for i in range(len(others)):
        norm_stay(i).start()
    pltpu.make_async_copy(nsend.at[0], nrecv.at[0, r], n_recv.at[0]).start()
    xo_ref[:, pl.ds(0, p)] = t

    for j in range(qpr):
        @pl.when(lag[j] <= 1)
        def _():
            await_bytes(vpre.at[j, 0], vp_recv.at[j, 0])

        @pl.when((lag[j] >= 1) & (lag[j] <= 2))
        def _():
            await_bytes(vpre.at[j, 1], vp_recv.at[j, 1])

        @pl.when((lag[j] <= 2) & even)
        def _():
            vmov[j] = mm(lhs_of(vpre[j, 0], vpre[j, 1]), qm[...])
            last_block(j).start()

        @pl.when(lag[j] <= 2)
        def _():
            vo_ref[pl.ds(j * width, width), pl.ds(0, p)] = mm(lhs_of(vpre[j, 0], vpre[j, 1]), qs[...])

    for panel in range(2):
        await_bytes(nrecv.at[panel], n_recv.at[panel])
        sums = nrecv[panel, 0]
        for i in range(1, n_row):
            sums = sums + nrecv[panel, i]
        so_ref[:, pl.ds(panel * p, p)] = jnp.sqrt(sums[0:1] / (m * n_row))

    for i in range(len(others)):
        norm_stay(i).wait_send()
    for i in range(n_row):
        norm_move(i).wait_send()
    for k in range(last):
        for ch in range(NCH):
            move_x(k, ch).wait_send()
        move_v(k).wait_send()
    for d in range(2):
        state_move(d).wait_send()

        @pl.when(home(d)[0] != r)
        def _():
            state_stay_far(d).wait_send()

    @pl.when(jnp.logical_not(even))
    def _():
        for d in range(3):
            last_slice(d).wait_send()

    for j in range(qpr):
        @pl.when((lag[j] <= 2) & even)
        def _():
            last_block(j).wait_send()

        @pl.when((lag[j] >= 1) & (lag[j] <= 3))
        def _():
            await_bytes(vo_ref.at[pl.ds(j * width, width), pl.ds(p, p)], vf_recv.at[j])

    for ch in range(NCH):
        move_x_last(ch).wait_send()
        move_x_last(ch).wait_recv()


def write_out(x_ref, v_ref, s_ref, xo_hbm, vo_hbm, so_ref, sem):
    copies = []
    half = x_ref.shape[0] // 2
    for src, dst in ((v_ref, vo_hbm), (x_ref, xo_hbm)):
        for start in range(0, src.shape[0], half):
            rows = pl.ds(start, half)
            copies.append(pltpu.make_async_copy(src.at[rows], dst.at[rows], sem.at[len(copies)]))
    for copy in copies:
        copy.start()
    so_ref[...] = s_ref[...]
    for copy in copies:
        copy.wait()


def per_device(activations, plan):
    n_row, n_col = lax.axis_size("row"), lax.axis_size("col")
    m, width = activations.shape
    p = width // 2
    sl = p // n_row
    vr = width // n_row
    rows = m + 3 * vr
    qpr = n_col // n_row
    dma = pltpu.SemaphoreType.DMA
    vmem = pl.BlockSpec(memory_space=pltpu.VMEM)
    shapes = (
        jax.ShapeDtypeStruct((m, width), F32),
        jax.ShapeDtypeStruct((qpr * width, width), F32),
        jax.ShapeDtypeStruct((1, width), F32),
    )
    results = pl.pallas_call(
        functools.partial(kernel, n_row, n_col),
        out_shape=shapes,
        in_specs=[pl.BlockSpec(memory_space=pltpu.SMEM), pl.BlockSpec(memory_space=pltpu.HBM)],
        out_specs=(vmem, vmem, vmem),
        scratch_shapes=[
            pltpu.VMEM((m, p), F32),
            pltpu.VMEM((ROUNDS, 3 * vr, p), F32),
            pltpu.VMEM((ROUNDS, rows, p), F32),
            pltpu.VMEM((ROUNDS, rows, p), F32),
            pltpu.VMEM((m, width), BF16),
            pltpu.VMEM((m, width), BF16),
            pltpu.VMEM((p, m), BF16),
            pltpu.VMEM((p, m), BF16),
            pltpu.VMEM((3 * width, p), BF16),
            pltpu.VMEM((3 * width, p), BF16),
            pltpu.VMEM((n_row, sl + 8, p), F32),
            pltpu.VMEM((ROUNDS, n_row - 1, sl + 8, p), F32),
            pltpu.VMEM((ROUNDS, p, p), F32),
            pltpu.VMEM((qpr, 2, width, p), F32),
            pltpu.VMEM((qpr, width, p), F32),
            pltpu.VMEM((2, 8, p), F32),
            pltpu.VMEM((2, n_row, 8, p), F32),
            dma,
            dma((ROUNDS + 1, NCH)),
            dma((ROUNDS,)),
            dma((ROUNDS, NCH)),
            dma((ROUNDS,)),
            dma((n_row - 1,)),
            dma((n_row - 1,)),
            dma((n_row - 1,)),
            dma((n_row - 1,)),
            dma((2, 2)),
            dma((qpr, 2)),
            dma((3,)),
            dma((qpr,)),
            dma((qpr,)),
            dma((2, n_row)),
            dma((2,)),
        ],
        compiler_params=pltpu.CompilerParams(collective_id=0, has_side_effects=True, vmem_limit_bytes=48 * 2**20),
    )(plan.T, activations)
    hbm = pl.BlockSpec(memory_space=pltpu.HBM)
    anywhere = pl.BlockSpec(memory_space=pl.ANY)
    rotated, vectors, spread = pl.pallas_call(
        write_out,
        out_shape=shapes,
        in_specs=[anywhere, anywhere, vmem],
        out_specs=(hbm, hbm, vmem),
        scratch_shapes=[dma((2 * (qpr + 1),))],
        compiler_params=pltpu.CompilerParams(vmem_limit_bytes=2**20),
    )(*results)
    return rotated, vectors, spread.reshape(width)


def solution(mesh):
    in_specs = (P("row", "col"), P(None, "col"))
    out_specs = (P("row", "col"), P("row", "col"), P("col"))
    return jax.shard_map(
        per_device, mesh=mesh, in_specs=in_specs, out_specs=out_specs, check_vma=False
    )
```

```python
import functools

import jax
import jax.numpy as jnp
from jax import lax
from jax.experimental import pallas as pl
from jax.experimental.pallas import tpu as pltpu
from jax.sharding import PartitionSpec as P

ROUNDS = 3
NY = 2
NCH = 2
MESH = pl.DeviceIdType.MESH
F32 = jnp.float32
BF16 = jnp.bfloat16


def split(x):
    hi = x.astype(BF16)
    lo = (x - hi.astype(F32)).astype(BF16)
    return hi, lo


def mm(a, b):
    return lax.dot_general(a, b, (((1,), (0,)), ((), ())), preferred_element_type=F32)


def mm3(a, b):
    ah, al = a
    bh, bl = b
    return mm(
        jnp.concatenate([ah, al, ah], axis=1), jnp.concatenate([bh, bh, bl], axis=0)
    )


def turn_blocks(b, bt, eye):
    bs, bts = split(b), split(bt)
    a = mm3(bs, bts)
    a_s = split(a)
    a2 = mm3(a_s, a_s)
    d1 = 0.25 * mm3(split(a2), a_s) - 0.75 * a2
    d1s = split(d1)
    w = 0.5 * a + 0.5 * d1 - 0.25 * mm3(d1s, a_s)
    e = mm3(d1s, d1s)
    ub = b - mm3(split(w), bs)
    d2 = 0.25 * mm3(split(e), d1s) - 0.75 * e
    d2s = split(d2)
    u = eye - w
    p = u - 0.5 * mm3(d2s, split(u))
    r = ub - 0.5 * mm3(d2s, split(ub))
    return p, r


def kernel(
    n_row, n_col, plan_ref, x_hbm, xo_ref, vo_ref, so_ref,
    stay, vst, arr, mov, xh, xl, sth, stl, qm, qs, part, rs, ag, vpre, vmov, vfin, nsend, nrecv,
    load_sem, arr_sem, varr_sem, xsend_sem, vsend_sem,
    rs_send, rs_recv, ag_send, ag_recv,
    vp_send, vp_recv, vf_recv, vm_send, n_send, n_recv,
):
    m, width = x_hbm.shape
    p = width // 2
    sl = p // n_row
    vr = width // n_row
    nv = 3 * vr
    qpr = n_col // n_row
    nx = n_row // NY
    rc, wc = m // NCH, width // NCH
    last = ROUNDS - 1
    r = lax.axis_index("row")
    c = lax.axis_index("col")
    y, x = r // nx, r % nx
    nxt, prv = (c + 1) % n_col, (c + n_col - 1) % n_col
    others = [(dy, dx) for dy in range(NY - 1, -1, -1) for dx in range(nx) if dy or dx]

    def peer(dy, dx):
        return ((y + dy) % NY) * nx + (x + dx) % nx

    def greet(row, col):
        pl.semaphore_signal(barrier, inc=1, device_id={"row": row, "col": col}, device_id_type=MESH)

    def remote(src, dst, send, recv, row, col):
        return pltpu.make_async_remote_copy(
            src_ref=src, dst_ref=dst, send_sem=send, recv_sem=recv,
            device_id={"row": row, "col": col}, device_id_type=MESH,
        )

    def await_bytes(ref, sem):
        pltpu.make_async_copy(ref, ref, sem).wait()

    barrier = pltpu.get_barrier_semaphore()
    for dy, dx in others:
        greet(peer(dy, dx), c)
    for rr in range(n_row):
        greet(rr, nxt)
        greet(rr, prv)

    load = pltpu.make_async_copy(x_hbm.at[:, pl.ds(0, p)], stay, load_sem)
    load.start()
    for ch in range(NCH):
        pltpu.make_async_copy(
            x_hbm.at[pl.ds(ch * rc, rc), pl.ds(p, p)],
            arr.at[0, pl.ds(ch * rc, rc)],
            arr_sem.at[0, ch],
        ).start()

    lane = lax.broadcasted_iota(jnp.int32, (vr, p), 1)
    row_id = lax.broadcasted_iota(jnp.int32, (vr, p), 0) + r * vr
    vst[0, pl.ds(0, vr)] = jnp.where(row_id == lane, 1.0, 0.0).astype(F32)
    arr[0, pl.ds(m, vr)] = jnp.where(row_id == lane + p, 1.0, 0.0).astype(F32)
    vst[0, pl.ds(vr, 2 * vr)] = jnp.zeros((2 * vr, p), F32)
    arr[0, pl.ds(m + vr, 2 * vr)] = jnp.zeros((2 * vr, p), F32)
    for k in range(1, ROUNDS):
        arr[k, pl.ds(m, vr)] = jnp.zeros((vr, p), F32)

    lag = [(c + n_col - (qpr * r + j)) % n_col for j in range(qpr)]
    for j in range(qpr):
        @pl.when(lag[j] > 2)
        def _():
            vo_ref[pl.ds(j * width, width), pl.ds(0, p)] = jnp.zeros((width, p), F32)

        @pl.when((lag[j] < 1) | (lag[j] > 3))
        def _():
            vo_ref[pl.ds(j * width, width), pl.ds(p, p)] = jnp.zeros((width, p), F32)

        @pl.when(lag[j] == 0)
        def _():
            vpre[j, 1] = jnp.zeros((width, p), F32)

        @pl.when(lag[j] == 2)
        def _():
            vpre[j, 0] = jnp.zeros((width, p), F32)

    odd = c % 2 == 1
    even = c % 2 == 0
    eye = jnp.where(
        lax.broadcasted_iota(jnp.int32, (p, p), 0) == lax.broadcasted_iota(jnp.int32, (p, p), 1), 1.0, 0.0
    ).astype(F32)
    load.wait()

    def chunk(ch):
        return pl.ds(ch * rc, rc)

    def move_x(k, ch):
        return remote(
            mov.at[k, chunk(ch)], arr.at[k + 1, chunk(ch)], xsend_sem.at[k, ch], arr_sem.at[k + 1, ch], r, nxt
        )

    def move_x_last(ch):
        return remote(
            mov.at[last, chunk(ch)], xo_ref.at[chunk(ch), pl.ds(p, p)], xsend_sem.at[last, ch],
            arr_sem.at[ROUNDS, ch], r, nxt,
        )

    def move_v(k):
        return remote(
            mov.at[k, pl.ds(m, 2 * vr)], arr.at[k + 1, pl.ds(m + vr, 2 * vr)],
            vsend_sem.at[k], varr_sem.at[k + 1], r, nxt,
        )

    def scatter(k, i):
        to = peer(*others[i])
        return remote(part.at[to], rs.at[k, i], rs_send.at[i], rs_recv.at[i], to, c)

    def gather(k, i):
        mine = ag.at[k, pl.ds(pl.multiple_of(r * sl, sl), sl)]
        return remote(mine, mine, ag_send.at[i], ag_recv.at[i], peer(*others[i]), c)

    def norm_stay(i):
        return remote(nsend.at[0], nrecv.at[0, r], n_send.at[0, i], n_recv.at[0], peer(*others[i]), c)

    def norm_move(i):
        return remote(nsend.at[1], nrecv.at[1, r], n_send.at[1, i], n_recv.at[1], (r + i) % n_row, nxt)

    def home(d):
        q = (c + n_col - d) % n_col
        return q // qpr, q % qpr

    my_rows = pl.ds(pl.multiple_of(r * vr, vr), vr)

    last_slices = remote(mov.at[last, pl.ds(m, nv)], vfin, vsend_sem.at[last], varr_sem.at[ROUNDS], r, nxt)

    def to_owner(i):
        if i < 2:
            lagging, panel, src = i, 0, vst.at[last, pl.ds(i * vr, vr)]
        elif i < 4:
            lagging, panel, src = i - 1, 1, arr.at[last, pl.ds(m + (i - 1) * vr, vr)]
        else:
            lagging, panel, src = i - 3, None, vfin.at[pl.ds((i - 4) * vr, vr)]
        owner, j = home(lagging)
        if panel is None:
            dst = vo_ref.at[pl.ds(pl.multiple_of(j * width + r * vr, vr), vr), pl.ds(p, p)]
            sem = vf_recv.at[j]
        else:
            dst, sem = vpre.at[j, panel, my_rows], vp_recv.at[j, panel]
        return src, dst, sem, owner

    def send_to_owner(i):
        src, dst, sem, owner = to_owner(i)

        @pl.when(owner == r)
        def _():
            pltpu.make_async_copy(src, dst, sem).start()

        @pl.when(owner != r)
        def _():
            remote(src, dst, vp_send.at[i], sem, owner, c).start()

    def sent_to_owner(i):
        src, dst, sem, owner = to_owner(i)

        @pl.when(owner != r)
        def _():
            remote(src, dst, vp_send.at[i], sem, owner, c).wait_send()

    def last_block(j):
        dst = vo_ref.at[pl.ds(j * width, width), pl.ds(p, p)]
        return remote(vmov.at[j], dst, vm_send.at[j], vf_recv.at[j], r, nxt)

    def lhs_rows(start, size):
        h = xh[pl.ds(start, size), :]
        return jnp.concatenate([h, xl[pl.ds(start, size), :], h], axis=1)

    def lhs_of(first, second):
        h1, l1 = split(first)
        h2, l2 = split(second)
        return jnp.concatenate([h1, h2, l1, l2, h1, h2], axis=1)

    def one_round(k, carry):
        s = stay[...]
        sh, slo = split(s)
        xh[:, pl.ds(0, p)] = sh
        xl[:, pl.ds(0, p)] = slo
        sth[...] = sh.T
        stl[...] = slo.T
        n1 = jnp.sum(s * s, axis=0, keepdims=True)
        n2 = jnp.zeros((1, p), F32)
        g = jnp.zeros((p, p), F32)
        for ch in range(NCH):
            rows = chunk(ch)
            await_bytes(arr.at[k, rows], arr_sem.at[k, ch])
            a = arr[k, rows]
            ah, al = split(a)
            xh[rows, pl.ds(p, p)] = ah
            xl[rows, pl.ds(p, p)] = al
            n2 = n2 + jnp.sum(a * a, axis=0, keepdims=True)
            th = sth[:, rows]
            g = g + mm3((th, stl[:, rows]), (ah, al))
        which = lax.broadcasted_iota(jnp.int32, (8, p), 0)
        norms = jnp.where(which == 0, n1, jnp.where(which == 1, n2, 0.0))
        for i in range(n_row):
            part[i, pl.ds(0, sl)] = g[i * sl:(i + 1) * sl]
            part[i, pl.ds(sl, 8)] = norms

        @pl.when(k == 0)
        def _():
            pl.semaphore_wait(barrier, len(others) + 2 * n_row)

        for i in range(len(others)):
            scatter(k, i).start()
        total = part[r]
        for i in range(len(others) - 1, -1, -1):
            scatter(k, i).wait_recv()
            total = total + rs[k, i]
        root = jnp.sqrt(total[sl:sl + 8] + 1e-06)
        root1, root2 = root[0:1], root[1:2]
        on_diag = lax.broadcasted_iota(jnp.int32, (sl, p), 1) == lax.broadcasted_iota(jnp.int32, (sl, p), 0) + r * sl
        root_col = jnp.sum(jnp.where(on_diag, root1, 0.0), axis=1, keepdims=True)
        ag[k, pl.ds(pl.multiple_of(r * sl, sl), sl)] = total[:sl] / (root_col * root2)
        for i in range(len(others)):
            gather(k, i).start()
        for i in range(len(others) - 1, -1, -1):
            gather(k, i).wait_recv()

        @pl.when(k > 0)
        def _():
            await_bytes(arr.at[k, pl.ds(m + vr, 2 * vr)], varr_sem.at[k])

        @pl.when(k == last)
        def _():
            for i in range(4):
                send_to_owner(i)

        coupling = ag[k]
        strength = jnp.sqrt(jnp.sum(coupling * coupling, keepdims=True))
        b = coupling / (1.0 + strength)
        bt = b.T
        p1, q12 = turn_blocks(b, bt, eye)
        p2, q12t = turn_blocks(bt, b, eye)
        chosen = jnp.full((1, p), plan_ref[0, k], jnp.int32) == 1
        for ref, top, bottom in (
            (qm, jnp.where(chosen, q12, p1), jnp.where(chosen, p2, -q12t)),
            (qs, jnp.where(chosen, p1, q12), jnp.where(chosen, -q12t, p2)),
        ):
            for at, piece in ((0, top), (p, bottom)):
                hi, lo = split(piece)
                ref[pl.ds(at, p)] = hi
                ref[pl.ds(2 * p + at, p)] = hi
                ref[pl.ds(4 * p + at, p)] = lo
        for ch in range(NCH):
            mov[k, chunk(ch)] = mm(lhs_rows(ch * rc, rc), qm[...])

        @pl.when(k < last)
        def _():
            for ch in range(NCH):
                move_x(k, ch).start()

        @pl.when(k == last)
        def _():
            t = mov[last, pl.ds(0, m)]
            nsend[1] = jnp.broadcast_to(jnp.sum(t * t, axis=0, keepdims=True), (8, p))
            for i in range(n_row):
                norm_move(i).start()

            @pl.when(odd)
            def _():
                mov[last, pl.ds(m, nv)] = mm(lhs_of(vst[last], arr[last, pl.ds(m, nv)]), qm[...])
                last_slices.start()

            for ch in range(NCH):
                move_x_last(ch).start()

        for ch in range(NCH):
            stay[chunk(ch)] = mm(lhs_rows(ch * rc, rc), qs[...])

        @pl.when(k < last)
        def _():
            v_lhs = lhs_of(vst[k], arr[k, pl.ds(m, nv)])
            mov[k, pl.ds(m, nv)] = mm(v_lhs, qm[...])
            vst[k + 1] = mm(v_lhs, qs[...])
            move_v(k).start()

        for i in range(len(others)):
            scatter(k, i).wait_send()
            gather(k, i).wait_send()
        return carry

    lax.fori_loop(0, ROUNDS, one_round, 0)

    t = stay[...]
    nsend[0] = jnp.broadcast_to(jnp.sum(t * t, axis=0, keepdims=True), (8, p))
    for i in range(len(others)):
        norm_stay(i).start()
    pltpu.make_async_copy(nsend.at[0], nrecv.at[0, r], n_recv.at[0]).start()
    xo_ref[:, pl.ds(0, p)] = t

    for j in range(qpr):
        @pl.when(lag[j] <= 1)
        def _():
            await_bytes(vpre.at[j, 0], vp_recv.at[j, 0])

        @pl.when((lag[j] >= 1) & (lag[j] <= 2))
        def _():
            await_bytes(vpre.at[j, 1], vp_recv.at[j, 1])

        @pl.when((lag[j] <= 2) & even)
        def _():
            for ch in range(NCH):
                rows = pl.ds(ch * wc, wc)
                vmov[j, rows] = mm(lhs_of(vpre[j, 0, rows], vpre[j, 1, rows]), qm[...])
            last_block(j).start()

    @pl.when(even)
    def _():
        await_bytes(vfin, varr_sem.at[ROUNDS])
        for i in range(4, 7):
            send_to_owner(i)

    for j in range(qpr):
        @pl.when(lag[j] <= 2)
        def _():
            for ch in range(NCH):
                rows = pl.ds(ch * wc, wc)
                vo_ref[pl.ds(j * width + ch * wc, wc), pl.ds(0, p)] = mm(
                    lhs_of(vpre[j, 0, rows], vpre[j, 1, rows]), qs[...]
                )

    for panel in range(2):
        await_bytes(nrecv.at[panel], n_recv.at[panel])
        sums = nrecv[panel, 0]
        for i in range(1, n_row):
            sums = sums + nrecv[panel, i]
        so_ref[:, pl.ds(panel * p, p)] = jnp.sqrt(sums[0:1] / (m * n_row))

    for i in range(len(others)):
        norm_stay(i).wait_send()
    for i in range(n_row):
        norm_move(i).wait_send()
    for k in range(last):
        for ch in range(NCH):
            move_x(k, ch).wait_send()
        move_v(k).wait_send()
    for i in range(4):
        sent_to_owner(i)

    @pl.when(odd)
    def _():
        last_slices.wait_send()

    @pl.when(even)
    def _():
        for i in range(4, 7):
            sent_to_owner(i)

    for j in range(qpr):
        @pl.when((lag[j] <= 2) & even)
        def _():
            last_block(j).wait_send()

        @pl.when((lag[j] >= 1) & (lag[j] <= 3))
        def _():
            await_bytes(vo_ref.at[pl.ds(j * width, width), pl.ds(p, p)], vf_recv.at[j])

    for ch in range(NCH):
        move_x_last(ch).wait_send()
        move_x_last(ch).wait_recv()


def write_out(x_ref, v_ref, s_ref, xo_hbm, vo_hbm, so_ref, sem):
    copies = []
    half = x_ref.shape[0] // 2
    for src, dst in ((v_ref, vo_hbm), (x_ref, xo_hbm)):
        for start in range(0, src.shape[0], half):
            rows = pl.ds(start, half)
            copies.append(pltpu.make_async_copy(src.at[rows], dst.at[rows], sem.at[len(copies)]))
    for copy in copies:
        copy.start()
    so_ref[...] = s_ref[...]
    for copy in copies:
        copy.wait()


def per_device(activations, plan):
    n_row, n_col = lax.axis_size("row"), lax.axis_size("col")
    m, width = activations.shape
    p = width // 2
    sl = p // n_row
    vr = width // n_row
    rows = m + 3 * vr
    qpr = n_col // n_row
    dma = pltpu.SemaphoreType.DMA
    vmem = pl.BlockSpec(memory_space=pltpu.VMEM)
    shapes = (
        jax.ShapeDtypeStruct((m, width), F32),
        jax.ShapeDtypeStruct((qpr * width, width), F32),
        jax.ShapeDtypeStruct((1, width), F32),
    )
    results = pl.pallas_call(
        functools.partial(kernel, n_row, n_col),
        out_shape=shapes,
        in_specs=[pl.BlockSpec(memory_space=pltpu.SMEM), pl.BlockSpec(memory_space=pltpu.HBM)],
        out_specs=(vmem, vmem, vmem),
        scratch_shapes=[
            pltpu.VMEM((m, p), F32),
            pltpu.VMEM((ROUNDS, 3 * vr, p), F32),
            pltpu.VMEM((ROUNDS, rows, p), F32),
            pltpu.VMEM((ROUNDS, rows, p), F32),
            pltpu.VMEM((m, width), BF16),
            pltpu.VMEM((m, width), BF16),
            pltpu.VMEM((p, m), BF16),
            pltpu.VMEM((p, m), BF16),
            pltpu.VMEM((3 * width, p), BF16),
            pltpu.VMEM((3 * width, p), BF16),
            pltpu.VMEM((n_row, sl + 8, p), F32),
            pltpu.VMEM((ROUNDS, n_row - 1, sl + 8, p), F32),
            pltpu.VMEM((ROUNDS, p, p), F32),
            pltpu.VMEM((qpr, 2, width, p), F32),
            pltpu.VMEM((qpr, width, p), F32),
            pltpu.VMEM((3 * vr, p), F32),
            pltpu.VMEM((2, 8, p), F32),
            pltpu.VMEM((2, n_row, 8, p), F32),
            dma,
            dma((ROUNDS + 1, NCH)),
            dma((ROUNDS + 1,)),
            dma((ROUNDS, NCH)),
            dma((ROUNDS,)),
            dma((n_row - 1,)),
            dma((n_row - 1,)),
            dma((n_row - 1,)),
            dma((n_row - 1,)),
            dma((7,)),
            dma((qpr, 2)),
            dma((qpr,)),
            dma((qpr,)),
            dma((2, n_row)),
            dma((2,)),
        ],
        compiler_params=pltpu.CompilerParams(collective_id=0, has_side_effects=True, vmem_limit_bytes=48 * 2**20),
    )(plan.T, activations)
    hbm = pl.BlockSpec(memory_space=pltpu.HBM)
    anywhere = pl.BlockSpec(memory_space=pl.ANY)
    rotated, vectors, spread = pl.pallas_call(
        write_out,
        out_shape=shapes,
        in_specs=[anywhere, anywhere, vmem],
        out_specs=(hbm, hbm, vmem),
        scratch_shapes=[dma((2 * (qpr + 1),))],
        compiler_params=pltpu.CompilerParams(vmem_limit_bytes=2**20),
    )(*results)
    return rotated, vectors, spread.reshape(width)


def solution(mesh):
    in_specs = (P("row", "col"), P(None, "col"))
    out_specs = (P("row", "col"), P("row", "col"), P("col"))
    return jax.shard_map(
        per_device, mesh=mesh, in_specs=in_specs, out_specs=out_specs, check_vma=False
    )
```

```python
import functools

import jax
import jax.numpy as jnp
from jax import lax
from jax.experimental import pallas as pl
from jax.experimental.pallas import tpu as pltpu
from jax.sharding import PartitionSpec as P

ROUNDS = 3
NY = 2
NCH = 2
MESH = pl.DeviceIdType.MESH
F32 = jnp.float32
BF16 = jnp.bfloat16


def split(x):
    hi = x.astype(BF16)
    lo = (x - hi.astype(F32)).astype(BF16)
    return hi, lo


def mm(a, b):
    return lax.dot_general(a, b, (((1,), (0,)), ((), ())), preferred_element_type=F32)


def mm3(a, b):
    ah, al = a
    bh, bl = b
    return mm(
        jnp.concatenate([ah, al, ah], axis=1), jnp.concatenate([bh, bh, bl], axis=0)
    )


def turn_blocks(b, bt, eye):
    bs, bts = split(b), split(bt)
    a = mm3(bs, bts)
    a_s = split(a)
    a2 = mm3(a_s, a_s)
    d1 = 0.25 * mm3(split(a2), a_s) - 0.75 * a2
    d1s = split(d1)
    w = 0.5 * a + 0.5 * d1 - 0.25 * mm3(d1s, a_s)
    e = mm3(d1s, d1s)
    ub = b - mm3(split(w), bs)
    d2 = 0.25 * mm3(split(e), d1s) - 0.75 * e
    d2s = split(d2)
    u = eye - w
    p = u - 0.5 * mm3(d2s, split(u))
    r = ub - 0.5 * mm3(d2s, split(ub))
    return p, r


def kernel(
    n_row, n_col, plan_ref, x_hbm, xo_ref, vo_ref, so_ref,
    stay, vst, arr, mov, xh, xl, sth, stl, qm, qs, part, rs, ag, vs, va, vmov, vfin, nsend, nrecv,
    load_sem, arr_sem, varr_sem, xsend_sem, vsend_sem,
    rs_send, rs_recv, ag_send, ag_recv,
    fwd_send, fin_send, va_recv, vf_recv, vm_send, n_send, n_recv,
):
    m, width = x_hbm.shape
    p = width // 2
    sl = p // n_row
    vr = width // n_row
    nv = 3 * vr
    qpr = n_col // n_row
    nx = n_row // NY
    rc, wc = m // NCH, width // NCH
    last = ROUNDS - 1
    r = lax.axis_index("row")
    c = lax.axis_index("col")
    y, x = r // nx, r % nx
    nxt, prv = (c + 1) % n_col, (c + n_col - 1) % n_col
    others = [(dy, dx) for dy in range(NY - 1, -1, -1) for dx in range(nx) if dy or dx]

    def peer(dy, dx):
        return ((y + dy) % NY) * nx + (x + dx) % nx

    def greet(row, col):
        pl.semaphore_signal(barrier, inc=1, device_id={"row": row, "col": col}, device_id_type=MESH)

    def remote(src, dst, send, recv, row, col):
        return pltpu.make_async_remote_copy(
            src_ref=src, dst_ref=dst, send_sem=send, recv_sem=recv,
            device_id={"row": row, "col": col}, device_id_type=MESH,
        )

    def await_bytes(ref, sem):
        pltpu.make_async_copy(ref, ref, sem).wait()

    barrier = pltpu.get_barrier_semaphore()
    for dy, dx in others:
        greet(peer(dy, dx), c)
    for rr in range(n_row):
        greet(rr, nxt)
        greet(rr, prv)

    load = pltpu.make_async_copy(x_hbm.at[:, pl.ds(0, p)], stay, load_sem)
    load.start()
    for ch in range(NCH):
        pltpu.make_async_copy(
            x_hbm.at[pl.ds(ch * rc, rc), pl.ds(p, p)],
            arr.at[0, pl.ds(ch * rc, rc)],
            arr_sem.at[0, ch],
        ).start()

    lane = lax.broadcasted_iota(jnp.int32, (vr, p), 1)
    row_id = lax.broadcasted_iota(jnp.int32, (vr, p), 0) + r * vr
    vst[0, pl.ds(0, vr)] = jnp.where(row_id == lane, 1.0, 0.0).astype(F32)
    arr[0, pl.ds(m, vr)] = jnp.where(row_id == lane + p, 1.0, 0.0).astype(F32)
    vst[0, pl.ds(vr, 2 * vr)] = jnp.zeros((2 * vr, p), F32)
    arr[0, pl.ds(m + vr, 2 * vr)] = jnp.zeros((2 * vr, p), F32)
    for k in range(1, ROUNDS):
        arr[k, pl.ds(m, vr)] = jnp.zeros((vr, p), F32)

    lag = [(c + n_col - (qpr * r + j)) % n_col for j in range(qpr)]
    for j in range(qpr):
        @pl.when(lag[j] > 2)
        def _():
            vo_ref[pl.ds(j * width, width), pl.ds(0, p)] = jnp.zeros((width, p), F32)

        @pl.when((lag[j] < 1) | (lag[j] > 3))
        def _():
            vo_ref[pl.ds(j * width, width), pl.ds(p, p)] = jnp.zeros((width, p), F32)

        @pl.when(lag[j] == 0)
        def _():
            col_id = lax.broadcasted_iota(jnp.int32, (width, p), 1)
            at = lax.broadcasted_iota(jnp.int32, (width, p), 0)
            vs[j] = jnp.where(at == col_id, 1.0, 0.0).astype(F32)
            va[0, j] = jnp.where(at == col_id + p, 1.0, 0.0).astype(F32)
            for k in range(1, ROUNDS):
                va[k, j] = jnp.zeros((width, p), F32)

        @pl.when((lag[j] >= 1) & (lag[j] <= 2))
        def _():
            vs[j] = jnp.zeros((width, p), F32)

    odd = c % 2 == 1
    even = c % 2 == 0
    eye = jnp.where(
        lax.broadcasted_iota(jnp.int32, (p, p), 0) == lax.broadcasted_iota(jnp.int32, (p, p), 1), 1.0, 0.0
    ).astype(F32)
    load.wait()

    def chunk(ch):
        return pl.ds(ch * rc, rc)

    def move_x(k, ch):
        return remote(
            mov.at[k, chunk(ch)], arr.at[k + 1, chunk(ch)], xsend_sem.at[k, ch], arr_sem.at[k + 1, ch], r, nxt
        )

    def move_x_last(ch):
        return remote(
            mov.at[last, chunk(ch)], xo_ref.at[chunk(ch), pl.ds(p, p)], xsend_sem.at[last, ch],
            arr_sem.at[ROUNDS, ch], r, nxt,
        )

    def move_v(k):
        return remote(
            mov.at[k, pl.ds(m, 2 * vr)], arr.at[k + 1, pl.ds(m + vr, 2 * vr)],
            vsend_sem.at[k], varr_sem.at[k + 1], r, nxt,
        )

    def scatter(k, i):
        to = peer(*others[i])
        return remote(part.at[to], rs.at[k, i], rs_send.at[i], rs_recv.at[i], to, c)

    def gather(k, i):
        mine = ag.at[k, pl.ds(pl.multiple_of(r * sl, sl), sl)]
        return remote(mine, mine, ag_send.at[i], ag_recv.at[i], peer(*others[i]), c)

    def norm_stay(i):
        return remote(nsend.at[0], nrecv.at[0, r], n_send.at[0, i], n_recv.at[0], peer(*others[i]), c)

    def norm_move(i):
        return remote(nsend.at[1], nrecv.at[1, r], n_send.at[1, i], n_recv.at[1], (r + i) % n_row, nxt)

    def home(d):
        q = (c + n_col - d) % n_col
        return q // qpr, q % qpr

    last_slices = remote(mov.at[last, pl.ds(m, nv)], vfin, vsend_sem.at[last], varr_sem.at[ROUNDS], r, nxt)

    def to_owner(k, d):
        owner, j = home(d)
        if k is None:
            src = vfin.at[pl.ds((d - 1) * vr, vr)]
            dst = vo_ref.at[pl.ds(pl.multiple_of(j * width + r * vr, vr), vr), pl.ds(p, p)]
            send, sem = fin_send.at[d - 1], vf_recv.at[j]
        else:
            src = arr.at[k, pl.ds(m + d * vr, vr)]
            dst = va.at[k, j, pl.ds(pl.multiple_of(r * vr, vr), vr)]
            send, sem = fwd_send.at[k, d - 1], va_recv.at[k, j]
        return src, dst, send, sem, owner

    def send_to_owner(k, d):
        src, dst, send, sem, owner = to_owner(k, d)

        @pl.when(owner == r)
        def _():
            pltpu.make_async_copy(src, dst, sem).start()

        @pl.when(owner != r)
        def _():
            remote(src, dst, send, sem, owner, c).start()

    def sent_to_owner(k, d):
        src, dst, send, sem, owner = to_owner(k, d)

        @pl.when(owner != r)
        def _():
            remote(src, dst, send, sem, owner, c).wait_send()

    def pass_block(k, j):
        return remote(vmov.at[k, j], va.at[k + 1, j], vm_send.at[k, j], va_recv.at[k + 1, j], r, nxt)

    def last_block(j):
        dst = vo_ref.at[pl.ds(j * width, width), pl.ds(p, p)]
        return remote(vmov.at[last, j], dst, vm_send.at[last, j], vf_recv.at[j], r, nxt)

    def lhs_rows(start, size):
        h = xh[pl.ds(start, size), :]
        return jnp.concatenate([h, xl[pl.ds(start, size), :], h], axis=1)

    def lhs_of(first, second):
        h1, l1 = split(first)
        h2, l2 = split(second)
        return jnp.concatenate([h1, h2, l1, l2, h1, h2], axis=1)

    def one_round(k, carry):
        s = stay[...]
        sh, slo = split(s)
        xh[:, pl.ds(0, p)] = sh
        xl[:, pl.ds(0, p)] = slo
        sth[...] = sh.T
        stl[...] = slo.T
        n1 = jnp.sum(s * s, axis=0, keepdims=True)
        n2 = jnp.zeros((1, p), F32)
        g = jnp.zeros((p, p), F32)
        for ch in range(NCH):
            rows = chunk(ch)
            await_bytes(arr.at[k, rows], arr_sem.at[k, ch])
            a = arr[k, rows]
            ah, al = split(a)
            xh[rows, pl.ds(p, p)] = ah
            xl[rows, pl.ds(p, p)] = al
            n2 = n2 + jnp.sum(a * a, axis=0, keepdims=True)
            th = sth[:, rows]
            g = g + mm3((th, stl[:, rows]), (ah, al))
        which = lax.broadcasted_iota(jnp.int32, (8, p), 0)
        norms = jnp.where(which == 0, n1, jnp.where(which == 1, n2, 0.0))
        for i in range(n_row):
            part[i, pl.ds(0, sl)] = g[i * sl:(i + 1) * sl]
            part[i, pl.ds(sl, 8)] = norms

        @pl.when(k == 0)
        def _():
            pl.semaphore_wait(barrier, len(others) + 2 * n_row)

        for i in range(len(others)):
            scatter(k, i).start()
        total = part[r]
        for i in range(len(others) - 1, -1, -1):
            scatter(k, i).wait_recv()
            total = total + rs[k, i]
        root = jnp.sqrt(total[sl:sl + 8] + 1e-06)
        root1, root2 = root[0:1], root[1:2]
        on_diag = lax.broadcasted_iota(jnp.int32, (sl, p), 1) == lax.broadcasted_iota(jnp.int32, (sl, p), 0) + r * sl
        root_col = jnp.sum(jnp.where(on_diag, root1, 0.0), axis=1, keepdims=True)
        ag[k, pl.ds(pl.multiple_of(r * sl, sl), sl)] = total[:sl] / (root_col * root2)
        for i in range(len(others)):
            gather(k, i).start()
        for i in range(len(others) - 1, -1, -1):
            gather(k, i).wait_recv()

        @pl.when(k > 0)
        def _():
            await_bytes(arr.at[k, pl.ds(m + vr, 2 * vr)], varr_sem.at[k])

        for d in range(1, ROUNDS):
            @pl.when(even & (k >= d))
            def _():
                send_to_owner(k, d)

        coupling = ag[k]
        strength = jnp.sqrt(jnp.sum(coupling * coupling, keepdims=True))
        b = coupling / (1.0 + strength)
        bt = b.T
        p1, q12 = turn_blocks(b, bt, eye)
        p2, q12t = turn_blocks(bt, b, eye)
        chosen = jnp.full((1, p), plan_ref[0, k], jnp.int32) == 1
        for ref, top, bottom in (
            (qm, jnp.where(chosen, q12, p1), jnp.where(chosen, p2, -q12t)),
            (qs, jnp.where(chosen, p1, q12), jnp.where(chosen, -q12t, p2)),
        ):
            for at, piece in ((0, top), (p, bottom)):
                hi, lo = split(piece)
                ref[pl.ds(at, p)] = hi
                ref[pl.ds(2 * p + at, p)] = hi
                ref[pl.ds(4 * p + at, p)] = lo
        for ch in range(NCH):
            mov[k, chunk(ch)] = mm(lhs_rows(ch * rc, rc), qm[...])

        @pl.when(k < last)
        def _():
            for ch in range(NCH):
                move_x(k, ch).start()

        @pl.when(k == last)
        def _():
            t = mov[last, pl.ds(0, m)]
            nsend[1] = jnp.broadcast_to(jnp.sum(t * t, axis=0, keepdims=True), (8, p))
            for i in range(n_row):
                norm_move(i).start()

            @pl.when(odd)
            def _():
                mov[last, pl.ds(m, nv)] = mm(lhs_of(vst[last], arr[last, pl.ds(m, nv)]), qm[...])
                last_slices.start()

            for ch in range(NCH):
                move_x_last(ch).start()

        for ch in range(NCH):
            stay[chunk(ch)] = mm(lhs_rows(ch * rc, rc), qs[...])

        @pl.when(k < last)
        def _():
            v_lhs = lhs_of(vst[k], arr[k, pl.ds(m, nv)])
            mov[k, pl.ds(m, nv)] = mm(v_lhs, qm[...])
            vst[k + 1] = mm(v_lhs, qs[...])
            move_v(k).start()

        for j in range(qpr):
            @pl.when((lag[j] <= k) & (k < last))
            def _():
                @pl.when(lag[j] >= 1)
                def _():
                    await_bytes(va.at[k, j], va_recv.at[k, j])

                for ch in range(NCH):
                    rows = pl.ds(ch * wc, wc)
                    block = lhs_of(vs[j, rows], va[k, j, rows])
                    vmov[k, j, rows] = mm(block, qm[...])
                    vs[j, rows] = mm(block, qs[...])

                @pl.when(even)
                def _():
                    pass_block(k, j).start()

        for i in range(len(others)):
            scatter(k, i).wait_send()
            gather(k, i).wait_send()
        return carry

    lax.fori_loop(0, ROUNDS, one_round, 0)

    t = stay[...]
    nsend[0] = jnp.broadcast_to(jnp.sum(t * t, axis=0, keepdims=True), (8, p))
    for i in range(len(others)):
        norm_stay(i).start()
    pltpu.make_async_copy(nsend.at[0], nrecv.at[0, r], n_recv.at[0]).start()
    xo_ref[:, pl.ds(0, p)] = t

    for j in range(qpr):
        @pl.when((lag[j] >= 1) & (lag[j] <= 2))
        def _():
            await_bytes(va.at[last, j], va_recv.at[last, j])

        @pl.when((lag[j] <= 2) & even)
        def _():
            for ch in range(NCH):
                rows = pl.ds(ch * wc, wc)
                vmov[last, j, rows] = mm(lhs_of(vs[j, rows], va[last, j, rows]), qm[...])
            last_block(j).start()

    @pl.when(even)
    def _():
        await_bytes(vfin, varr_sem.at[ROUNDS])
        for d in range(1, 4):
            send_to_owner(None, d)

    for j in range(qpr):
        @pl.when(lag[j] <= 2)
        def _():
            for ch in range(NCH):
                rows = pl.ds(ch * wc, wc)
                vo_ref[pl.ds(j * width + ch * wc, wc), pl.ds(0, p)] = mm(
                    lhs_of(vs[j, rows], va[last, j, rows]), qs[...]
                )

    for panel in range(2):
        await_bytes(nrecv.at[panel], n_recv.at[panel])
        sums = nrecv[panel, 0]
        for i in range(1, n_row):
            sums = sums + nrecv[panel, i]
        so_ref[:, pl.ds(panel * p, p)] = jnp.sqrt(sums[0:1] / (m * n_row))

    for i in range(len(others)):
        norm_stay(i).wait_send()
    for i in range(n_row):
        norm_move(i).wait_send()
    for k in range(last):
        for ch in range(NCH):
            move_x(k, ch).wait_send()
        move_v(k).wait_send()
    @pl.when(odd)
    def _():
        last_slices.wait_send()

    @pl.when(even)
    def _():
        for k in range(1, ROUNDS):
            for d in range(1, k + 1):
                sent_to_owner(k, d)
        for d in range(1, 4):
            sent_to_owner(None, d)

    for k in range(last):
        for j in range(qpr):
            @pl.when(even & (lag[j] <= k))
            def _():
                pass_block(k, j).wait_send()

    for j in range(qpr):
        @pl.when((lag[j] <= 2) & even)
        def _():
            last_block(j).wait_send()

        @pl.when((lag[j] >= 1) & (lag[j] <= 3))
        def _():
            await_bytes(vo_ref.at[pl.ds(j * width, width), pl.ds(p, p)], vf_recv.at[j])

    for ch in range(NCH):
        move_x_last(ch).wait_send()
        move_x_last(ch).wait_recv()


def write_out(x_ref, v_ref, s_ref, xo_hbm, vo_hbm, so_ref, sem):
    copies = []
    half = x_ref.shape[0] // 2
    for src, dst in ((v_ref, vo_hbm), (x_ref, xo_hbm)):
        for start in range(0, src.shape[0], half):
            rows = pl.ds(start, half)
            copies.append(pltpu.make_async_copy(src.at[rows], dst.at[rows], sem.at[len(copies)]))
    for copy in copies:
        copy.start()
    so_ref[...] = s_ref[...]
    for copy in copies:
        copy.wait()


def per_device(activations, plan):
    n_row, n_col = lax.axis_size("row"), lax.axis_size("col")
    m, width = activations.shape
    p = width // 2
    sl = p // n_row
    vr = width // n_row
    rows = m + 3 * vr
    qpr = n_col // n_row
    dma = pltpu.SemaphoreType.DMA
    vmem = pl.BlockSpec(memory_space=pltpu.VMEM)
    shapes = (
        jax.ShapeDtypeStruct((m, width), F32),
        jax.ShapeDtypeStruct((qpr * width, width), F32),
        jax.ShapeDtypeStruct((1, width), F32),
    )
    results = pl.pallas_call(
        functools.partial(kernel, n_row, n_col),
        out_shape=shapes,
        in_specs=[pl.BlockSpec(memory_space=pltpu.SMEM), pl.BlockSpec(memory_space=pltpu.HBM)],
        out_specs=(vmem, vmem, vmem),
        scratch_shapes=[
            pltpu.VMEM((m, p), F32),
            pltpu.VMEM((ROUNDS, 3 * vr, p), F32),
            pltpu.VMEM((ROUNDS, rows, p), F32),
            pltpu.VMEM((ROUNDS, rows, p), F32),
            pltpu.VMEM((m, width), BF16),
            pltpu.VMEM((m, width), BF16),
            pltpu.VMEM((p, m), BF16),
            pltpu.VMEM((p, m), BF16),
            pltpu.VMEM((3 * width, p), BF16),
            pltpu.VMEM((3 * width, p), BF16),
            pltpu.VMEM((n_row, sl + 8, p), F32),
            pltpu.VMEM((ROUNDS, n_row - 1, sl + 8, p), F32),
            pltpu.VMEM((ROUNDS, p, p), F32),
            pltpu.VMEM((qpr, width, p), F32),
            pltpu.VMEM((ROUNDS, qpr, width, p), F32),
            pltpu.VMEM((ROUNDS, qpr, width, p), F32),
            pltpu.VMEM((3 * vr, p), F32),
            pltpu.VMEM((2, 8, p), F32),
            pltpu.VMEM((2, n_row, 8, p), F32),
            dma,
            dma((ROUNDS + 1, NCH)),
            dma((ROUNDS + 1,)),
            dma((ROUNDS, NCH)),
            dma((ROUNDS,)),
            dma((n_row - 1,)),
            dma((n_row - 1,)),
            dma((n_row - 1,)),
            dma((n_row - 1,)),
            dma((ROUNDS, 2)),
            dma((3,)),
            dma((ROUNDS, qpr)),
            dma((qpr,)),
            dma((ROUNDS, qpr)),
            dma((2, n_row)),
            dma((2,)),
        ],
        compiler_params=pltpu.CompilerParams(collective_id=0, has_side_effects=True, vmem_limit_bytes=48 * 2**20),
    )(plan.T, activations)
    hbm = pl.BlockSpec(memory_space=pltpu.HBM)
    anywhere = pl.BlockSpec(memory_space=pl.ANY)
    rotated, vectors, spread = pl.pallas_call(
        write_out,
        out_shape=shapes,
        in_specs=[anywhere, anywhere, vmem],
        out_specs=(hbm, hbm, vmem),
        scratch_shapes=[dma((2 * (qpr + 1),))],
        compiler_params=pltpu.CompilerParams(vmem_limit_bytes=2**20),
    )(*results)
    return rotated, vectors, spread.reshape(width)


def solution(mesh):
    in_specs = (P("row", "col"), P(None, "col"))
    out_specs = (P("row", "col"), P("row", "col"), P("col"))
    return jax.shard_map(
        per_device, mesh=mesh, in_specs=in_specs, out_specs=out_specs, check_vma=False
    )
```

```python
import functools

import jax
import jax.numpy as jnp
from jax import lax
from jax.experimental import pallas as pl
from jax.experimental.pallas import tpu as pltpu
from jax.sharding import PartitionSpec as P

ROUNDS = 3
NY = 2
NCH = 2
MESH = pl.DeviceIdType.MESH
F32 = jnp.float32
BF16 = jnp.bfloat16


def split(x):
    hi = x.astype(BF16)
    lo = (x - hi.astype(F32)).astype(BF16)
    return hi, lo


def mm(a, b):
    return lax.dot_general(a, b, (((1,), (0,)), ((), ())), preferred_element_type=F32)


def mm3(a, b):
    ah, al = a
    bh, bl = b
    return mm(
        jnp.concatenate([ah, al, ah], axis=1), jnp.concatenate([bh, bh, bl], axis=0)
    )


def turn_blocks(b, bt, eye):
    bs, bts = split(b), split(bt)
    a = mm3(bs, bts)
    a_s = split(a)
    a2 = mm3(a_s, a_s)
    d1 = 0.25 * mm3(split(a2), a_s) - 0.75 * a2
    d1s = split(d1)
    w = 0.5 * a + 0.5 * d1 - 0.25 * mm3(d1s, a_s)
    e = mm3(d1s, d1s)
    ub = b - mm3(split(w), bs)
    d2 = 0.25 * mm3(split(e), d1s) - 0.75 * e
    d2s = split(d2)
    u = eye - w
    p = u - 0.5 * mm3(d2s, split(u))
    r = ub - 0.5 * mm3(d2s, split(ub))
    return p, r


def kernel(
    n_row, n_col, plan_ref, x_hbm, xo_ref, vo_ref, so_ref,
    stay, vst, arr, mov, xh, xl, sth, stl, qm, qs, part, rs, ag, vs, va, vmov, vfin, nsend, nrecv,
    load_sem, arr_sem, varr_sem, xsend_sem, vsend_sem,
    rs_send, rs_recv, ag_send, ag_recv,
    fwd_send, fin_send, x_send, va_recv, vf_recv, vm_send, n_send, n_recv,
):
    m, width = x_hbm.shape
    p = width // 2
    sl = p // n_row
    vr = width // n_row
    nv = 3 * vr
    qpr = n_col // n_row
    nx = n_row // NY
    rc, wc = m // NCH, width // NCH
    last = ROUNDS - 1
    r = lax.axis_index("row")
    c = lax.axis_index("col")
    y, x = r // nx, r % nx
    nxt, prv = (c + 1) % n_col, (c + n_col - 1) % n_col
    others = [(dy, dx) for dy in range(NY - 1, -1, -1) for dx in range(nx) if dy or dx]

    def peer(dy, dx):
        return ((y + dy) % NY) * nx + (x + dx) % nx

    def greet(row, col):
        pl.semaphore_signal(barrier, inc=1, device_id={"row": row, "col": col}, device_id_type=MESH)

    def remote(src, dst, send, recv, row, col):
        return pltpu.make_async_remote_copy(
            src_ref=src, dst_ref=dst, send_sem=send, recv_sem=recv,
            device_id={"row": row, "col": col}, device_id_type=MESH,
        )

    def await_bytes(ref, sem):
        pltpu.make_async_copy(ref, ref, sem).wait()

    barrier = pltpu.get_barrier_semaphore()
    for dy, dx in others:
        greet(peer(dy, dx), c)
    for rr in range(n_row):
        greet(rr, nxt)
        greet(rr, prv)

    load = pltpu.make_async_copy(x_hbm.at[:, pl.ds(0, p)], stay, load_sem)
    load.start()
    for ch in range(NCH):
        pltpu.make_async_copy(
            x_hbm.at[pl.ds(ch * rc, rc), pl.ds(p, p)],
            arr.at[0, pl.ds(ch * rc, rc)],
            arr_sem.at[0, ch],
        ).start()

    lane = lax.broadcasted_iota(jnp.int32, (vr, p), 1)
    row_id = lax.broadcasted_iota(jnp.int32, (vr, p), 0) + r * vr
    vst[0, pl.ds(0, vr)] = jnp.where(row_id == lane, 1.0, 0.0).astype(F32)
    arr[0, pl.ds(m, vr)] = jnp.where(row_id == lane + p, 1.0, 0.0).astype(F32)
    vst[0, pl.ds(vr, 2 * vr)] = jnp.zeros((2 * vr, p), F32)
    arr[0, pl.ds(m + vr, 2 * vr)] = jnp.zeros((2 * vr, p), F32)
    for k in range(1, ROUNDS):
        arr[k, pl.ds(m, vr)] = jnp.zeros((vr, p), F32)

    lag = [(c + n_col - (qpr * r + j)) % n_col for j in range(qpr)]
    for j in range(qpr):
        @pl.when(lag[j] > 2)
        def _():
            vo_ref[pl.ds(j * width, width), pl.ds(0, p)] = jnp.zeros((width, p), F32)

        @pl.when((lag[j] < 1) | (lag[j] > 3))
        def _():
            vo_ref[pl.ds(j * width, width), pl.ds(p, p)] = jnp.zeros((width, p), F32)

        @pl.when(lag[j] == 0)
        def _():
            col_id = lax.broadcasted_iota(jnp.int32, (width, p), 1)
            at = lax.broadcasted_iota(jnp.int32, (width, p), 0)
            vs[j] = jnp.where(at == col_id, 1.0, 0.0).astype(F32)
            va[0, j] = jnp.where(at == col_id + p, 1.0, 0.0).astype(F32)
            for k in range(1, ROUNDS):
                va[k, j] = jnp.zeros((width, p), F32)

        @pl.when((lag[j] >= 1) & (lag[j] <= 2))
        def _():
            vs[j] = jnp.zeros((width, p), F32)

    odd = c % 2 == 1
    even = c % 2 == 0
    eye = jnp.where(
        lax.broadcasted_iota(jnp.int32, (p, p), 0) == lax.broadcasted_iota(jnp.int32, (p, p), 1), 1.0, 0.0
    ).astype(F32)
    load.wait()

    def chunk(ch):
        return pl.ds(ch * rc, rc)

    def move_x(k, ch):
        return remote(
            mov.at[k, chunk(ch)], arr.at[k + 1, chunk(ch)], xsend_sem.at[k, ch], arr_sem.at[k + 1, ch], r, nxt
        )

    def move_x_last(ch):
        return remote(
            mov.at[last, chunk(ch)], xo_ref.at[chunk(ch), pl.ds(p, p)], xsend_sem.at[last, ch],
            arr_sem.at[ROUNDS, ch], r, nxt,
        )

    def move_v(k):
        return remote(
            mov.at[k, pl.ds(m, 2 * vr)], arr.at[k + 1, pl.ds(m + vr, 2 * vr)],
            vsend_sem.at[k], varr_sem.at[k + 1], r, nxt,
        )

    def scatter(k, i):
        to = peer(*others[i])
        return remote(part.at[to], rs.at[k, i], rs_send.at[i], rs_recv.at[i], to, c)

    def gather(k, i):
        mine = ag.at[k, pl.ds(pl.multiple_of(r * sl, sl), sl)]
        return remote(mine, mine, ag_send.at[i], ag_recv.at[i], peer(*others[i]), c)

    def norm_stay(i):
        return remote(nsend.at[0], nrecv.at[0, r], n_send.at[0, i], n_recv.at[0], peer(*others[i]), c)

    def norm_move(i):
        return remote(nsend.at[1], nrecv.at[1, r], n_send.at[1, i], n_recv.at[1], (r + i) % n_row, nxt)

    def home(d):
        q = (c + n_col - d) % n_col
        return q // qpr, q % qpr

    last_slices = remote(mov.at[last, pl.ds(m, nv)], vfin, vsend_sem.at[last], varr_sem.at[ROUNDS], r, nxt)

    def to_owner(k, d):
        owner, j = home(d)
        if k is None:
            src = vfin.at[pl.ds((d - 1) * vr, vr)]
            dst = vo_ref.at[pl.ds(pl.multiple_of(j * width + r * vr, vr), vr), pl.ds(p, p)]
            send, sem = fin_send.at[d - 1], vf_recv.at[j]
        else:
            src = arr.at[k, pl.ds(m + d * vr, vr)]
            dst = va.at[k, j, pl.ds(pl.multiple_of(r * vr, vr), vr)]
            send, sem = fwd_send.at[k, d - 1], va_recv.at[k, j]
        return src, dst, send, sem, owner

    def send_to_owner(k, d):
        src, dst, send, sem, owner = to_owner(k, d)

        @pl.when(owner == r)
        def _():
            pltpu.make_async_copy(src, dst, sem).start()

        @pl.when((owner != r) & (owner // nx == y))
        def _():
            remote(src, dst, send, sem, owner, c).start()

    def sent_to_owner(k, d):
        src, dst, send, sem, owner = to_owner(k, d)

        @pl.when((owner != r) & (owner // nx == y))
        def _():
            remote(src, dst, send, sem, owner, c).wait_send()

    def across(k, d):
        owner, j = home(d)
        src = mov.at[k, pl.ds(m + d * vr, vr)]
        if isinstance(k, int) and k == last:
            dst = vo_ref.at[pl.ds(pl.multiple_of(j * width + r * vr, vr), vr), pl.ds(p, p)]
            sem = vf_recv.at[j]
        else:
            dst = va.at[k + 1, j, pl.ds(pl.multiple_of(r * vr, vr), vr)]
            sem = va_recv.at[k + 1, j]
        return odd & (owner // nx != y), remote(src, dst, x_send.at[k, d], sem, owner, nxt)

    def pass_block(k, j):
        return remote(vmov.at[k, j], va.at[k + 1, j], vm_send.at[k, j], va_recv.at[k + 1, j], r, nxt)

    def last_block(j):
        dst = vo_ref.at[pl.ds(j * width, width), pl.ds(p, p)]
        return remote(vmov.at[last, j], dst, vm_send.at[last, j], vf_recv.at[j], r, nxt)

    def lhs_rows(start, size):
        h = xh[pl.ds(start, size), :]
        return jnp.concatenate([h, xl[pl.ds(start, size), :], h], axis=1)

    def lhs_of(first, second):
        h1, l1 = split(first)
        h2, l2 = split(second)
        return jnp.concatenate([h1, h2, l1, l2, h1, h2], axis=1)

    def one_round(k, carry):
        s = stay[...]
        sh, slo = split(s)
        xh[:, pl.ds(0, p)] = sh
        xl[:, pl.ds(0, p)] = slo
        sth[...] = sh.T
        stl[...] = slo.T
        n1 = jnp.sum(s * s, axis=0, keepdims=True)
        n2 = jnp.zeros((1, p), F32)
        g = jnp.zeros((p, p), F32)
        for ch in range(NCH):
            rows = chunk(ch)
            await_bytes(arr.at[k, rows], arr_sem.at[k, ch])
            a = arr[k, rows]
            ah, al = split(a)
            xh[rows, pl.ds(p, p)] = ah
            xl[rows, pl.ds(p, p)] = al
            n2 = n2 + jnp.sum(a * a, axis=0, keepdims=True)
            th = sth[:, rows]
            g = g + mm3((th, stl[:, rows]), (ah, al))
        which = lax.broadcasted_iota(jnp.int32, (8, p), 0)
        norms = jnp.where(which == 0, n1, jnp.where(which == 1, n2, 0.0))
        for i in range(n_row):
            part[i, pl.ds(0, sl)] = g[i * sl:(i + 1) * sl]
            part[i, pl.ds(sl, 8)] = norms

        @pl.when(k == 0)
        def _():
            pl.semaphore_wait(barrier, len(others) + 2 * n_row)

        for i in range(len(others)):
            scatter(k, i).start()
        total = part[r]
        for i in range(len(others) - 1, -1, -1):
            scatter(k, i).wait_recv()
            total = total + rs[k, i]
        root = jnp.sqrt(total[sl:sl + 8] + 1e-06)
        root1, root2 = root[0:1], root[1:2]
        on_diag = lax.broadcasted_iota(jnp.int32, (sl, p), 1) == lax.broadcasted_iota(jnp.int32, (sl, p), 0) + r * sl
        root_col = jnp.sum(jnp.where(on_diag, root1, 0.0), axis=1, keepdims=True)
        ag[k, pl.ds(pl.multiple_of(r * sl, sl), sl)] = total[:sl] / (root_col * root2)
        for i in range(len(others)):
            gather(k, i).start()
        for i in range(len(others) - 1, -1, -1):
            gather(k, i).wait_recv()

        @pl.when(k > 0)
        def _():
            await_bytes(arr.at[k, pl.ds(m + vr, 2 * vr)], varr_sem.at[k])

        for d in range(1, ROUNDS):
            @pl.when(even & (k >= d))
            def _():
                send_to_owner(k, d)

        coupling = ag[k]
        strength = jnp.sqrt(jnp.sum(coupling * coupling, keepdims=True))
        b = coupling / (1.0 + strength)
        bt = b.T
        p1, q12 = turn_blocks(b, bt, eye)
        p2, q12t = turn_blocks(bt, b, eye)
        chosen = jnp.full((1, p), plan_ref[0, k], jnp.int32) == 1
        for ref, top, bottom in (
            (qm, jnp.where(chosen, q12, p1), jnp.where(chosen, p2, -q12t)),
            (qs, jnp.where(chosen, p1, q12), jnp.where(chosen, -q12t, p2)),
        ):
            for at, piece in ((0, top), (p, bottom)):
                hi, lo = split(piece)
                ref[pl.ds(at, p)] = hi
                ref[pl.ds(2 * p + at, p)] = hi
                ref[pl.ds(4 * p + at, p)] = lo
        for ch in range(NCH):
            mov[k, chunk(ch)] = mm(lhs_rows(ch * rc, rc), qm[...])

        @pl.when(k < last)
        def _():
            for ch in range(NCH):
                move_x(k, ch).start()

        @pl.when(k == last)
        def _():
            t = mov[last, pl.ds(0, m)]
            nsend[1] = jnp.broadcast_to(jnp.sum(t * t, axis=0, keepdims=True), (8, p))
            for i in range(n_row):
                norm_move(i).start()

            @pl.when(odd)
            def _():
                mov[last, pl.ds(m, nv)] = mm(lhs_of(vst[last], arr[last, pl.ds(m, nv)]), qm[...])
                last_slices.start()
                for d in range(3):
                    there, copy = across(last, d)

                    @pl.when(there)
                    def _():
                        copy.start()

            for ch in range(NCH):
                move_x_last(ch).start()

        for ch in range(NCH):
            stay[chunk(ch)] = mm(lhs_rows(ch * rc, rc), qs[...])

        @pl.when(k < last)
        def _():
            v_lhs = lhs_of(vst[k], arr[k, pl.ds(m, nv)])
            mov[k, pl.ds(m, nv)] = mm(v_lhs, qm[...])
            vst[k + 1] = mm(v_lhs, qs[...])
            move_v(k).start()

        for d in range(last):
            there, copy = across(k, d)

            @pl.when(there & (k >= d) & (k < last))
            def _():
                copy.start()

        for j in range(qpr):
            @pl.when((lag[j] <= k) & (k < last))
            def _():
                @pl.when(lag[j] >= 1)
                def _():
                    await_bytes(va.at[k, j], va_recv.at[k, j])

                for ch in range(NCH):
                    rows = pl.ds(ch * wc, wc)
                    block = lhs_of(vs[j, rows], va[k, j, rows])
                    vmov[k, j, rows] = mm(block, qm[...])
                    vs[j, rows] = mm(block, qs[...])

                @pl.when(even)
                def _():
                    pass_block(k, j).start()

        for i in range(len(others)):
            scatter(k, i).wait_send()
            gather(k, i).wait_send()
        return carry

    lax.fori_loop(0, ROUNDS, one_round, 0)

    t = stay[...]
    nsend[0] = jnp.broadcast_to(jnp.sum(t * t, axis=0, keepdims=True), (8, p))
    for i in range(len(others)):
        norm_stay(i).start()
    pltpu.make_async_copy(nsend.at[0], nrecv.at[0, r], n_recv.at[0]).start()
    xo_ref[:, pl.ds(0, p)] = t

    for j in range(qpr):
        @pl.when((lag[j] >= 1) & (lag[j] <= 2))
        def _():
            await_bytes(va.at[last, j], va_recv.at[last, j])

        @pl.when((lag[j] <= 2) & even)
        def _():
            for ch in range(NCH):
                rows = pl.ds(ch * wc, wc)
                vmov[last, j, rows] = mm(lhs_of(vs[j, rows], va[last, j, rows]), qm[...])
            last_block(j).start()

    @pl.when(even)
    def _():
        await_bytes(vfin, varr_sem.at[ROUNDS])
        for d in range(1, 4):
            send_to_owner(None, d)

    for j in range(qpr):
        @pl.when(lag[j] <= 2)
        def _():
            for ch in range(NCH):
                rows = pl.ds(ch * wc, wc)
                vo_ref[pl.ds(j * width + ch * wc, wc), pl.ds(0, p)] = mm(
                    lhs_of(vs[j, rows], va[last, j, rows]), qs[...]
                )

    for panel in range(2):
        await_bytes(nrecv.at[panel], n_recv.at[panel])
        sums = nrecv[panel, 0]
        for i in range(1, n_row):
            sums = sums + nrecv[panel, i]
        so_ref[:, pl.ds(panel * p, p)] = jnp.sqrt(sums[0:1] / (m * n_row))

    for i in range(len(others)):
        norm_stay(i).wait_send()
    for i in range(n_row):
        norm_move(i).wait_send()
    for k in range(last):
        for ch in range(NCH):
            move_x(k, ch).wait_send()
        move_v(k).wait_send()
    @pl.when(odd)
    def _():
        last_slices.wait_send()

    for k in range(ROUNDS):
        for d in range(k + 1):
            there, copy = across(k, d)

            @pl.when(there)
            def _():
                copy.wait_send()

    @pl.when(even)
    def _():
        for k in range(1, ROUNDS):
            for d in range(1, k + 1):
                sent_to_owner(k, d)
        for d in range(1, 4):
            sent_to_owner(None, d)

    for k in range(last):
        for j in range(qpr):
            @pl.when(even & (lag[j] <= k))
            def _():
                pass_block(k, j).wait_send()

    for j in range(qpr):
        @pl.when((lag[j] <= 2) & even)
        def _():
            last_block(j).wait_send()

        @pl.when((lag[j] >= 1) & (lag[j] <= 3))
        def _():
            await_bytes(vo_ref.at[pl.ds(j * width, width), pl.ds(p, p)], vf_recv.at[j])

    for ch in range(NCH):
        move_x_last(ch).wait_send()
        move_x_last(ch).wait_recv()


def write_out(x_ref, v_ref, s_ref, xo_hbm, vo_hbm, so_ref, sem):
    copies = []
    half = x_ref.shape[0] // 2
    for src, dst in ((v_ref, vo_hbm), (x_ref, xo_hbm)):
        for start in range(0, src.shape[0], half):
            rows = pl.ds(start, half)
            copies.append(pltpu.make_async_copy(src.at[rows], dst.at[rows], sem.at[len(copies)]))
    for copy in copies:
        copy.start()
    so_ref[...] = s_ref[...]
    for copy in copies:
        copy.wait()


def per_device(activations, plan):
    n_row, n_col = lax.axis_size("row"), lax.axis_size("col")
    m, width = activations.shape
    p = width // 2
    sl = p // n_row
    vr = width // n_row
    rows = m + 3 * vr
    qpr = n_col // n_row
    dma = pltpu.SemaphoreType.DMA
    vmem = pl.BlockSpec(memory_space=pltpu.VMEM)
    shapes = (
        jax.ShapeDtypeStruct((m, width), F32),
        jax.ShapeDtypeStruct((qpr * width, width), F32),
        jax.ShapeDtypeStruct((1, width), F32),
    )
    results = pl.pallas_call(
        functools.partial(kernel, n_row, n_col),
        out_shape=shapes,
        in_specs=[pl.BlockSpec(memory_space=pltpu.SMEM), pl.BlockSpec(memory_space=pltpu.HBM)],
        out_specs=(vmem, vmem, vmem),
        scratch_shapes=[
            pltpu.VMEM((m, p), F32),
            pltpu.VMEM((ROUNDS, 3 * vr, p), F32),
            pltpu.VMEM((ROUNDS, rows, p), F32),
            pltpu.VMEM((ROUNDS, rows, p), F32),
            pltpu.VMEM((m, width), BF16),
            pltpu.VMEM((m, width), BF16),
            pltpu.VMEM((p, m), BF16),
            pltpu.VMEM((p, m), BF16),
            pltpu.VMEM((3 * width, p), BF16),
            pltpu.VMEM((3 * width, p), BF16),
            pltpu.VMEM((n_row, sl + 8, p), F32),
            pltpu.VMEM((ROUNDS, n_row - 1, sl + 8, p), F32),
            pltpu.VMEM((ROUNDS, p, p), F32),
            pltpu.VMEM((qpr, width, p), F32),
            pltpu.VMEM((ROUNDS, qpr, width, p), F32),
            pltpu.VMEM((ROUNDS, qpr, width, p), F32),
            pltpu.VMEM((3 * vr, p), F32),
            pltpu.VMEM((2, 8, p), F32),
            pltpu.VMEM((2, n_row, 8, p), F32),
            dma,
            dma((ROUNDS + 1, NCH)),
            dma((ROUNDS + 1,)),
            dma((ROUNDS, NCH)),
            dma((ROUNDS,)),
            dma((n_row - 1,)),
            dma((n_row - 1,)),
            dma((n_row - 1,)),
            dma((n_row - 1,)),
            dma((ROUNDS, 2)),
            dma((3,)),
            dma((ROUNDS, 3)),
            dma((ROUNDS, qpr)),
            dma((qpr,)),
            dma((ROUNDS, qpr)),
            dma((2, n_row)),
            dma((2,)),
        ],
        compiler_params=pltpu.CompilerParams(collective_id=0, has_side_effects=True, vmem_limit_bytes=48 * 2**20),
    )(plan.T, activations)
    hbm = pl.BlockSpec(memory_space=pltpu.HBM)
    anywhere = pl.BlockSpec(memory_space=pl.ANY)
    rotated, vectors, spread = pl.pallas_call(
        write_out,
        out_shape=shapes,
        in_specs=[anywhere, anywhere, vmem],
        out_specs=(hbm, hbm, vmem),
        scratch_shapes=[dma((2 * (qpr + 1),))],
        compiler_params=pltpu.CompilerParams(vmem_limit_bytes=2**20),
    )(*results)
    return rotated, vectors, spread.reshape(width)


def solution(mesh):
    in_specs = (P("row", "col"), P(None, "col"))
    out_specs = (P("row", "col"), P("row", "col"), P("col"))
    return jax.shard_map(
        per_device, mesh=mesh, in_specs=in_specs, out_specs=out_specs, check_vma=False
    )
```

```python
import functools

import jax
import jax.numpy as jnp
from jax import lax
from jax.experimental import pallas as pl
from jax.experimental.pallas import tpu as pltpu
from jax.sharding import PartitionSpec as P

ROUNDS = 3
NY = 2
NCH = 2
MESH = pl.DeviceIdType.MESH
F32 = jnp.float32
BF16 = jnp.bfloat16


def split(x):
    hi = x.astype(BF16)
    lo = (x - hi.astype(F32)).astype(BF16)
    return hi, lo


def mm(a, b):
    return lax.dot_general(a, b, (((1,), (0,)), ((), ())), preferred_element_type=F32)


def mm3(a, b):
    ah, al = a
    bh, bl = b
    return mm(
        jnp.concatenate([ah, al, ah], axis=1), jnp.concatenate([bh, bh, bl], axis=0)
    )


def turn_blocks(b, bt, eye):
    bs, bts = split(b), split(bt)
    a = mm3(bs, bts)
    a_s = split(a)
    a2 = mm3(a_s, a_s)
    d1 = 0.25 * mm3(split(a2), a_s) - 0.75 * a2
    d1s = split(d1)
    w = 0.5 * a + 0.5 * d1 - 0.25 * mm3(d1s, a_s)
    e = mm3(d1s, d1s)
    ub = b - mm3(split(w), bs)
    d2 = 0.25 * mm3(split(e), d1s) - 0.75 * e
    d2s = split(d2)
    u = eye - w
    p = u - 0.5 * mm3(d2s, split(u))
    r = ub - 0.5 * mm3(d2s, split(ub))
    return p, r


def kernel(
    n_row, n_col, plan_ref, x_hbm, xo_ref, vo_ref, so_ref,
    stay, vst, arr, mov, xh, xl, sth, stl, qm, qs, part, rs, ag, vs, va, vmov, vfin, nsend, nrecv,
    load_sem, arr_sem, varr_sem, xsend_sem, vsend_sem,
    rs_send, rs_recv, ag_send, ag_recv,
    fwd_send, fin_send, x_send, va_recv, vf_recv, vm_send, n_send, n_recv,
):
    m, width = x_hbm.shape
    p = width // 2
    sl = p // n_row
    vr = width // n_row
    nv = 3 * vr
    qpr = n_col // n_row
    nx = n_row // NY
    rc, wc = m // NCH, width // NCH
    last = ROUNDS - 1
    r = lax.axis_index("row")
    c = lax.axis_index("col")
    y, x = r // nx, r % nx
    nxt, prv = (c + 1) % n_col, (c + n_col - 1) % n_col
    others = [(dy, dx) for dy in range(NY - 1, -1, -1) for dx in range(nx) if dy or dx]

    def peer(dy, dx):
        return ((y + dy) % NY) * nx + (x + dx) % nx

    def greet(row, col):
        pl.semaphore_signal(barrier, inc=1, device_id={"row": row, "col": col}, device_id_type=MESH)

    def remote(src, dst, send, recv, row, col):
        return pltpu.make_async_remote_copy(
            src_ref=src, dst_ref=dst, send_sem=send, recv_sem=recv,
            device_id={"row": row, "col": col}, device_id_type=MESH,
        )

    def await_bytes(ref, sem):
        pltpu.make_async_copy(ref, ref, sem).wait()

    barrier = pltpu.get_barrier_semaphore()
    for dy, dx in others:
        greet(peer(dy, dx), c)
    for rr in range(n_row):
        greet(rr, nxt)
        greet(rr, prv)

    load = pltpu.make_async_copy(x_hbm.at[:, pl.ds(0, p)], stay, load_sem)
    load.start()
    for ch in range(NCH):
        pltpu.make_async_copy(
            x_hbm.at[pl.ds(ch * rc, rc), pl.ds(p, p)],
            arr.at[0, pl.ds(ch * rc, rc)],
            arr_sem.at[0, ch],
        ).start()

    lane = lax.broadcasted_iota(jnp.int32, (vr, p), 1)
    row_id = lax.broadcasted_iota(jnp.int32, (vr, p), 0) + r * vr
    vst[0, pl.ds(0, vr)] = jnp.where(row_id == lane, 1.0, 0.0).astype(F32)
    arr[0, pl.ds(m, vr)] = jnp.where(row_id == lane + p, 1.0, 0.0).astype(F32)
    vst[0, pl.ds(vr, 2 * vr)] = jnp.zeros((2 * vr, p), F32)
    arr[0, pl.ds(m + vr, 2 * vr)] = jnp.zeros((2 * vr, p), F32)
    for k in range(1, ROUNDS):
        arr[k, pl.ds(m, vr)] = jnp.zeros((vr, p), F32)

    lag = [(c + n_col - (qpr * r + j)) % n_col for j in range(qpr)]
    for j in range(qpr):
        @pl.when(lag[j] > 2)
        def _():
            vo_ref[pl.ds(j * width, width), pl.ds(0, p)] = jnp.zeros((width, p), F32)

        @pl.when((lag[j] < 1) | (lag[j] > 3))
        def _():
            vo_ref[pl.ds(j * width, width), pl.ds(p, p)] = jnp.zeros((width, p), F32)

        @pl.when(lag[j] == 0)
        def _():
            col_id = lax.broadcasted_iota(jnp.int32, (width, p), 1)
            at = lax.broadcasted_iota(jnp.int32, (width, p), 0)
            vs[j] = jnp.where(at == col_id, 1.0, 0.0).astype(F32)
            va[0, j] = jnp.where(at == col_id + p, 1.0, 0.0).astype(F32)
            for k in range(1, ROUNDS):
                va[k, j] = jnp.zeros((width, p), F32)

        @pl.when((lag[j] >= 1) & (lag[j] <= 2))
        def _():
            vs[j] = jnp.zeros((width, p), F32)

    odd = c % 2 == 1
    even = c % 2 == 0
    eye = jnp.where(
        lax.broadcasted_iota(jnp.int32, (p, p), 0) == lax.broadcasted_iota(jnp.int32, (p, p), 1), 1.0, 0.0
    ).astype(F32)
    load.wait()

    def chunk(ch):
        return pl.ds(ch * rc, rc)

    def move_x(k, ch):
        return remote(
            mov.at[k, chunk(ch)], arr.at[k + 1, chunk(ch)], xsend_sem.at[k, ch], arr_sem.at[k + 1, ch], r, nxt
        )

    def move_x_last(ch):
        return remote(
            mov.at[last, chunk(ch)], xo_ref.at[chunk(ch), pl.ds(p, p)], xsend_sem.at[last, ch],
            arr_sem.at[ROUNDS, ch], r, nxt,
        )

    def move_v(k):
        return remote(
            mov.at[k, pl.ds(m, 2 * vr)], arr.at[k + 1, pl.ds(m + vr, 2 * vr)],
            vsend_sem.at[k], varr_sem.at[k + 1], r, nxt,
        )

    def scatter(k, i):
        to = peer(*others[i])
        return remote(part.at[to], rs.at[k, i], rs_send.at[i], rs_recv.at[i], to, c)

    def gather(k, i):
        mine = ag.at[k, pl.ds(pl.multiple_of(r * sl, sl), sl)]
        return remote(mine, mine, ag_send.at[i], ag_recv.at[i], peer(*others[i]), c)

    def norm_stay(i):
        return remote(nsend.at[0], nrecv.at[0, r], n_send.at[0, i], n_recv.at[0], peer(*others[i]), c)

    def norm_move(i):
        return remote(nsend.at[1], nrecv.at[1, r], n_send.at[1, i], n_recv.at[1], (r + i) % n_row, nxt)

    def home(d):
        q = (c + n_col - d) % n_col
        return q // qpr, q % qpr

    last_slices = remote(mov.at[last, pl.ds(m, nv)], vfin, vsend_sem.at[last], varr_sem.at[ROUNDS], r, nxt)

    def to_owner(k, d):
        owner, j = home(d)
        if k is None:
            src = vfin.at[pl.ds((d - 1) * vr, vr)]
            dst = vo_ref.at[pl.ds(pl.multiple_of(j * width + r * vr, vr), vr), pl.ds(p, p)]
            send, sem = fin_send.at[d - 1], vf_recv.at[j]
        else:
            src = arr.at[k, pl.ds(m + d * vr, vr)]
            dst = va.at[k, j, pl.ds(pl.multiple_of(r * vr, vr), vr)]
            send, sem = fwd_send.at[k, d - 1], va_recv.at[k, j]
        return src, dst, send, sem, owner

    def send_to_owner(k, d):
        src, dst, send, sem, owner = to_owner(k, d)

        @pl.when(owner == r)
        def _():
            pltpu.make_async_copy(src, dst, sem).start()

        @pl.when((owner != r) & (owner // nx == y))
        def _():
            remote(src, dst, send, sem, owner, c).start()

    def sent_to_owner(k, d):
        src, dst, send, sem, owner = to_owner(k, d)

        @pl.when((owner != r) & (owner // nx == y))
        def _():
            remote(src, dst, send, sem, owner, c).wait_send()

    def across(k, d):
        owner, j = home(d)
        src = mov.at[k, pl.ds(m + d * vr, vr)]
        if isinstance(k, int) and k == last:
            dst = vo_ref.at[pl.ds(pl.multiple_of(j * width + r * vr, vr), vr), pl.ds(p, p)]
            sem = vf_recv.at[j]
        else:
            dst = va.at[k + 1, j, pl.ds(pl.multiple_of(r * vr, vr), vr)]
            sem = va_recv.at[k + 1, j]
        return odd & (owner // nx != y), remote(src, dst, x_send.at[k, d], sem, owner, nxt)

    def pass_block(k, j):
        return remote(vmov.at[k, j], va.at[k + 1, j], vm_send.at[k, j], va_recv.at[k + 1, j], r, nxt)

    def last_block(j):
        dst = vo_ref.at[pl.ds(j * width, width), pl.ds(p, p)]
        return remote(vmov.at[last, j], dst, vm_send.at[last, j], vf_recv.at[j], r, nxt)

    def lhs_rows(start, size):
        h = xh[pl.ds(start, size), :]
        return jnp.concatenate([h, xl[pl.ds(start, size), :], h], axis=1)

    def lhs_of(first, second):
        h1, l1 = split(first)
        h2, l2 = split(second)
        return jnp.concatenate([h1, h2, l1, l2, h1, h2], axis=1)

    def one_round(k, carry):
        s = stay[...]
        sh, slo = split(s)
        xh[:, pl.ds(0, p)] = sh
        xl[:, pl.ds(0, p)] = slo
        sth[...] = sh.T
        stl[...] = slo.T
        n1 = jnp.sum(s * s, axis=0, keepdims=True)
        n2 = jnp.zeros((1, p), F32)
        g = jnp.zeros((p, p), F32)
        for ch in range(NCH):
            rows = chunk(ch)
            await_bytes(arr.at[k, rows], arr_sem.at[k, ch])
            a = arr[k, rows]
            ah, al = split(a)
            xh[rows, pl.ds(p, p)] = ah
            xl[rows, pl.ds(p, p)] = al
            n2 = n2 + jnp.sum(a * a, axis=0, keepdims=True)
            th = sth[:, rows]
            g = g + mm3((th, stl[:, rows]), (ah, al))
        which = lax.broadcasted_iota(jnp.int32, (8, p), 0)
        norms = jnp.where(which == 0, n1, jnp.where(which == 1, n2, 0.0))
        for i in range(n_row):
            part[i, pl.ds(0, sl)] = g[i * sl:(i + 1) * sl]
            part[i, pl.ds(sl, 8)] = norms

        @pl.when(k == 0)
        def _():
            pl.semaphore_wait(barrier, len(others) + 2 * n_row)

        for i in range(len(others)):
            scatter(k, i).start()
        total = part[r]
        for i in range(len(others) - 1, -1, -1):
            scatter(k, i).wait_recv()
            total = total + rs[k, i]
        root = jnp.sqrt(total[sl:sl + 8] + 1e-06)
        root1, root2 = root[0:1], root[1:2]
        on_diag = lax.broadcasted_iota(jnp.int32, (sl, p), 1) == lax.broadcasted_iota(jnp.int32, (sl, p), 0) + r * sl
        root_col = jnp.sum(jnp.where(on_diag, root1, 0.0), axis=1, keepdims=True)
        ag[k, pl.ds(pl.multiple_of(r * sl, sl), sl)] = total[:sl] / (root_col * root2)
        for i in range(len(others)):
            gather(k, i).start()
        for i in range(len(others) - 1, -1, -1):
            gather(k, i).wait_recv()

        @pl.when(k > 0)
        def _():
            await_bytes(arr.at[k, pl.ds(m + vr, 2 * vr)], varr_sem.at[k])

        for d in range(1, ROUNDS):
            there, copy = across(k - 1, d - 1)

            @pl.when(there & (k >= d))
            def _():
                copy.start()

            @pl.when(even & (k >= d))
            def _():
                send_to_owner(k, d)

        coupling = ag[k]
        strength = jnp.sqrt(jnp.sum(coupling * coupling, keepdims=True))
        b = coupling / (1.0 + strength)
        bt = b.T
        p1, q12 = turn_blocks(b, bt, eye)
        p2, q12t = turn_blocks(bt, b, eye)
        chosen = jnp.full((1, p), plan_ref[0, k], jnp.int32) == 1
        for ref, top, bottom in (
            (qm, jnp.where(chosen, q12, p1), jnp.where(chosen, p2, -q12t)),
            (qs, jnp.where(chosen, p1, q12), jnp.where(chosen, -q12t, p2)),
        ):
            for at, piece in ((0, top), (p, bottom)):
                hi, lo = split(piece)
                ref[pl.ds(at, p)] = hi
                ref[pl.ds(2 * p + at, p)] = hi
                ref[pl.ds(4 * p + at, p)] = lo
        for ch in range(NCH):
            mov[k, chunk(ch)] = mm(lhs_rows(ch * rc, rc), qm[...])

        @pl.when(k < last)
        def _():
            for ch in range(NCH):
                move_x(k, ch).start()

        @pl.when(k == last)
        def _():
            t = mov[last, pl.ds(0, m)]
            nsend[1] = jnp.broadcast_to(jnp.sum(t * t, axis=0, keepdims=True), (8, p))
            for i in range(n_row):
                norm_move(i).start()

            @pl.when(odd)
            def _():
                mov[last, pl.ds(m, nv)] = mm(lhs_of(vst[last], arr[last, pl.ds(m, nv)]), qm[...])
                last_slices.start()
                for d in range(3):
                    there, copy = across(last, d)

                    @pl.when(there)
                    def _():
                        copy.start()

            for ch in range(NCH):
                move_x_last(ch).start()

        for ch in range(NCH):
            stay[chunk(ch)] = mm(lhs_rows(ch * rc, rc), qs[...])

        @pl.when(k < last)
        def _():
            v_lhs = lhs_of(vst[k], arr[k, pl.ds(m, nv)])
            mov[k, pl.ds(m, nv)] = mm(v_lhs, qm[...])
            vst[k + 1] = mm(v_lhs, qs[...])
            move_v(k).start()

        for j in range(qpr):
            @pl.when((lag[j] <= k) & (k < last))
            def _():
                @pl.when(lag[j] >= 1)
                def _():
                    await_bytes(va.at[k, j], va_recv.at[k, j])

                for ch in range(NCH):
                    rows = pl.ds(ch * wc, wc)
                    block = lhs_of(vs[j, rows], va[k, j, rows])
                    vmov[k, j, rows] = mm(block, qm[...])
                    vs[j, rows] = mm(block, qs[...])

                @pl.when(even)
                def _():
                    pass_block(k, j).start()

        for i in range(len(others)):
            scatter(k, i).wait_send()
            gather(k, i).wait_send()
        return carry

    lax.fori_loop(0, ROUNDS, one_round, 0)

    t = stay[...]
    nsend[0] = jnp.broadcast_to(jnp.sum(t * t, axis=0, keepdims=True), (8, p))
    for i in range(len(others)):
        norm_stay(i).start()
    pltpu.make_async_copy(nsend.at[0], nrecv.at[0, r], n_recv.at[0]).start()
    xo_ref[:, pl.ds(0, p)] = t

    for j in range(qpr):
        @pl.when((lag[j] >= 1) & (lag[j] <= 2))
        def _():
            await_bytes(va.at[last, j], va_recv.at[last, j])

        @pl.when((lag[j] <= 2) & even)
        def _():
            for ch in range(NCH):
                rows = pl.ds(ch * wc, wc)
                vmov[last, j, rows] = mm(lhs_of(vs[j, rows], va[last, j, rows]), qm[...])
            last_block(j).start()

    @pl.when(even)
    def _():
        await_bytes(vfin, varr_sem.at[ROUNDS])
        for d in range(1, 4):
            send_to_owner(None, d)

    for j in range(qpr):
        @pl.when(lag[j] <= 2)
        def _():
            for ch in range(NCH):
                rows = pl.ds(ch * wc, wc)
                vo_ref[pl.ds(j * width + ch * wc, wc), pl.ds(0, p)] = mm(
                    lhs_of(vs[j, rows], va[last, j, rows]), qs[...]
                )

    for panel in range(2):
        await_bytes(nrecv.at[panel], n_recv.at[panel])
        sums = nrecv[panel, 0]
        for i in range(1, n_row):
            sums = sums + nrecv[panel, i]
        so_ref[:, pl.ds(panel * p, p)] = jnp.sqrt(sums[0:1] / (m * n_row))

    for i in range(len(others)):
        norm_stay(i).wait_send()
    for i in range(n_row):
        norm_move(i).wait_send()
    for k in range(last):
        for ch in range(NCH):
            move_x(k, ch).wait_send()
        move_v(k).wait_send()
    @pl.when(odd)
    def _():
        last_slices.wait_send()

    for k in range(ROUNDS):
        for d in range(k + 1):
            there, copy = across(k, d)

            @pl.when(there)
            def _():
                copy.wait_send()

    @pl.when(even)
    def _():
        for k in range(1, ROUNDS):
            for d in range(1, k + 1):
                sent_to_owner(k, d)
        for d in range(1, 4):
            sent_to_owner(None, d)

    for k in range(last):
        for j in range(qpr):
            @pl.when(even & (lag[j] <= k))
            def _():
                pass_block(k, j).wait_send()

    for j in range(qpr):
        @pl.when((lag[j] <= 2) & even)
        def _():
            last_block(j).wait_send()

        @pl.when((lag[j] >= 1) & (lag[j] <= 3))
        def _():
            await_bytes(vo_ref.at[pl.ds(j * width, width), pl.ds(p, p)], vf_recv.at[j])

    for ch in range(NCH):
        move_x_last(ch).wait_send()
        move_x_last(ch).wait_recv()


def write_out(x_ref, v_ref, s_ref, xo_hbm, vo_hbm, so_ref, sem):
    copies = []
    half = x_ref.shape[0] // 2
    for src, dst in ((v_ref, vo_hbm), (x_ref, xo_hbm)):
        for start in range(0, src.shape[0], half):
            rows = pl.ds(start, half)
            copies.append(pltpu.make_async_copy(src.at[rows], dst.at[rows], sem.at[len(copies)]))
    for copy in copies:
        copy.start()
    so_ref[...] = s_ref[...]
    for copy in copies:
        copy.wait()


def per_device(activations, plan):
    n_row, n_col = lax.axis_size("row"), lax.axis_size("col")
    m, width = activations.shape
    p = width // 2
    sl = p // n_row
    vr = width // n_row
    rows = m + 3 * vr
    qpr = n_col // n_row
    dma = pltpu.SemaphoreType.DMA
    vmem = pl.BlockSpec(memory_space=pltpu.VMEM)
    shapes = (
        jax.ShapeDtypeStruct((m, width), F32),
        jax.ShapeDtypeStruct((qpr * width, width), F32),
        jax.ShapeDtypeStruct((1, width), F32),
    )
    results = pl.pallas_call(
        functools.partial(kernel, n_row, n_col),
        out_shape=shapes,
        in_specs=[pl.BlockSpec(memory_space=pltpu.SMEM), pl.BlockSpec(memory_space=pltpu.HBM)],
        out_specs=(vmem, vmem, vmem),
        scratch_shapes=[
            pltpu.VMEM((m, p), F32),
            pltpu.VMEM((ROUNDS, 3 * vr, p), F32),
            pltpu.VMEM((ROUNDS, rows, p), F32),
            pltpu.VMEM((ROUNDS, rows, p), F32),
            pltpu.VMEM((m, width), BF16),
            pltpu.VMEM((m, width), BF16),
            pltpu.VMEM((p, m), BF16),
            pltpu.VMEM((p, m), BF16),
            pltpu.VMEM((3 * width, p), BF16),
            pltpu.VMEM((3 * width, p), BF16),
            pltpu.VMEM((n_row, sl + 8, p), F32),
            pltpu.VMEM((ROUNDS, n_row - 1, sl + 8, p), F32),
            pltpu.VMEM((ROUNDS, p, p), F32),
            pltpu.VMEM((qpr, width, p), F32),
            pltpu.VMEM((ROUNDS, qpr, width, p), F32),
            pltpu.VMEM((ROUNDS, qpr, width, p), F32),
            pltpu.VMEM((3 * vr, p), F32),
            pltpu.VMEM((2, 8, p), F32),
            pltpu.VMEM((2, n_row, 8, p), F32),
            dma,
            dma((ROUNDS + 1, NCH)),
            dma((ROUNDS + 1,)),
            dma((ROUNDS, NCH)),
            dma((ROUNDS,)),
            dma((n_row - 1,)),
            dma((n_row - 1,)),
            dma((n_row - 1,)),
            dma((n_row - 1,)),
            dma((ROUNDS, 2)),
            dma((3,)),
            dma((ROUNDS, 3)),
            dma((ROUNDS, qpr)),
            dma((qpr,)),
            dma((ROUNDS, qpr)),
            dma((2, n_row)),
            dma((2,)),
        ],
        compiler_params=pltpu.CompilerParams(collective_id=0, has_side_effects=True, vmem_limit_bytes=48 * 2**20),
    )(plan.T, activations)
    hbm = pl.BlockSpec(memory_space=pltpu.HBM)
    anywhere = pl.BlockSpec(memory_space=pl.ANY)
    rotated, vectors, spread = pl.pallas_call(
        write_out,
        out_shape=shapes,
        in_specs=[anywhere, anywhere, vmem],
        out_specs=(hbm, hbm, vmem),
        scratch_shapes=[dma((2 * (qpr + 1),))],
        compiler_params=pltpu.CompilerParams(vmem_limit_bytes=2**20),
    )(*results)
    return rotated, vectors, spread.reshape(width)


def solution(mesh):
    in_specs = (P("row", "col"), P(None, "col"))
    out_specs = (P("row", "col"), P("row", "col"), P("col"))
    return jax.shard_map(
        per_device, mesh=mesh, in_specs=in_specs, out_specs=out_specs, check_vma=False
    )
```

```python
import functools

import jax
import jax.numpy as jnp
from jax import lax
from jax.experimental import pallas as pl
from jax.experimental.pallas import tpu as pltpu
from jax.sharding import PartitionSpec as P

ROUNDS = 3
NY = 2
NCH = 2
MESH = pl.DeviceIdType.MESH
F32 = jnp.float32
BF16 = jnp.bfloat16


def split(x):
    hi = x.astype(BF16)
    lo = (x - hi.astype(F32)).astype(BF16)
    return hi, lo


def mm(a, b):
    return lax.dot_general(a, b, (((1,), (0,)), ((), ())), preferred_element_type=F32)


def mm3(a, b):
    ah, al = a
    bh, bl = b
    return mm(
        jnp.concatenate([ah, al, ah], axis=1), jnp.concatenate([bh, bh, bl], axis=0)
    )


def turn_blocks(b, bt, eye):
    bs, bts = split(b), split(bt)
    a = mm3(bs, bts)
    a_s = split(a)
    f1 = 0.25 * mm3(a_s, a_s) - 0.75 * a
    f1s = split(f1)
    d1 = mm3(a_s, f1s)
    d1s = split(d1)
    g = 0.25 * mm3(d1s, d1s) - 0.75 * d1
    w = 0.5 * a + 0.5 * d1 - 0.25 * mm3(d1s, a_s)
    h = mm3(f1s, split(g))
    q = 0.25 * d1 - 0.5 * (eye + f1 + h - mm3(split(w), split(h)))
    q_s = split(q)
    t = split(mm3(q_s, bs))
    tt = split(mm3(bts, q_s))
    return eye + mm3(a_s, q_s), b + mm3(a_s, t), bt + mm3(tt, a_s), eye + mm3(bts, t)


def kernel(
    n_row, n_col, plan_ref, x_hbm, xo_ref, vo_ref, so_ref,
    stay, vst, arr, mov, xh, xl, sth, stl, qm, qs, part, rs, ag, vs, va, vmov, vfin, nsend, nrecv,
    load_sem, arr_sem, varr_sem, xsend_sem, vsend_sem,
    rs_send, rs_recv, ag_send, ag_recv,
    fwd_send, fin_send, x_send, va_recv, vf_recv, vm_send, n_send, n_recv,
):
    m, width = x_hbm.shape
    p = width // 2
    sl = p // n_row
    vr = width // n_row
    nv = 3 * vr
    qpr = n_col // n_row
    nx = n_row // NY
    rc, wc = m // NCH, width // NCH
    last = ROUNDS - 1
    r = lax.axis_index("row")
    c = lax.axis_index("col")
    y, x = r // nx, r % nx
    nxt, prv = (c + 1) % n_col, (c + n_col - 1) % n_col
    others = [(dy, dx) for dy in range(NY - 1, -1, -1) for dx in range(nx) if dy or dx]

    def peer(dy, dx):
        return ((y + dy) % NY) * nx + (x + dx) % nx

    def greet(row, col):
        pl.semaphore_signal(barrier, inc=1, device_id={"row": row, "col": col}, device_id_type=MESH)

    def remote(src, dst, send, recv, row, col):
        return pltpu.make_async_remote_copy(
            src_ref=src, dst_ref=dst, send_sem=send, recv_sem=recv,
            device_id={"row": row, "col": col}, device_id_type=MESH,
        )

    def await_bytes(ref, sem):
        pltpu.make_async_copy(ref, ref, sem).wait()

    barrier = pltpu.get_barrier_semaphore()
    for dy, dx in others:
        greet(peer(dy, dx), c)
    for rr in range(n_row):
        greet(rr, nxt)
        greet(rr, prv)

    load = pltpu.make_async_copy(x_hbm.at[:, pl.ds(0, p)], stay, load_sem)
    load.start()
    for ch in range(NCH):
        pltpu.make_async_copy(
            x_hbm.at[pl.ds(ch * rc, rc), pl.ds(p, p)],
            arr.at[0, pl.ds(ch * rc, rc)],
            arr_sem.at[0, ch],
        ).start()

    lane = lax.broadcasted_iota(jnp.int32, (vr, p), 1)
    row_id = lax.broadcasted_iota(jnp.int32, (vr, p), 0) + r * vr
    vst[0, pl.ds(0, vr)] = jnp.where(row_id == lane, 1.0, 0.0).astype(F32)
    arr[0, pl.ds(m, vr)] = jnp.where(row_id == lane + p, 1.0, 0.0).astype(F32)
    vst[0, pl.ds(vr, 2 * vr)] = jnp.zeros((2 * vr, p), F32)
    arr[0, pl.ds(m + vr, 2 * vr)] = jnp.zeros((2 * vr, p), F32)
    for k in range(1, ROUNDS):
        arr[k, pl.ds(m, vr)] = jnp.zeros((vr, p), F32)

    lag = [(c + n_col - (qpr * r + j)) % n_col for j in range(qpr)]
    for j in range(qpr):
        @pl.when(lag[j] > 2)
        def _():
            vo_ref[pl.ds(j * width, width), pl.ds(0, p)] = jnp.zeros((width, p), F32)

        @pl.when((lag[j] < 1) | (lag[j] > 3))
        def _():
            vo_ref[pl.ds(j * width, width), pl.ds(p, p)] = jnp.zeros((width, p), F32)

        @pl.when(lag[j] == 0)
        def _():
            col_id = lax.broadcasted_iota(jnp.int32, (width, p), 1)
            at = lax.broadcasted_iota(jnp.int32, (width, p), 0)
            vs[j] = jnp.where(at == col_id, 1.0, 0.0).astype(F32)
            va[0, j] = jnp.where(at == col_id + p, 1.0, 0.0).astype(F32)
            for k in range(1, ROUNDS):
                va[k, j] = jnp.zeros((width, p), F32)

        @pl.when((lag[j] >= 1) & (lag[j] <= 2))
        def _():
            vs[j] = jnp.zeros((width, p), F32)

    odd = c % 2 == 1
    even = c % 2 == 0
    eye = jnp.where(
        lax.broadcasted_iota(jnp.int32, (p, p), 0) == lax.broadcasted_iota(jnp.int32, (p, p), 1), 1.0, 0.0
    ).astype(F32)
    load.wait()

    def chunk(ch):
        return pl.ds(ch * rc, rc)

    def move_x(k, ch):
        return remote(
            mov.at[k, chunk(ch)], arr.at[k + 1, chunk(ch)], xsend_sem.at[k, ch], arr_sem.at[k + 1, ch], r, nxt
        )

    def move_x_last(ch):
        return remote(
            mov.at[last, chunk(ch)], xo_ref.at[chunk(ch), pl.ds(p, p)], xsend_sem.at[last, ch],
            arr_sem.at[ROUNDS, ch], r, nxt,
        )

    def move_v(k):
        return remote(
            mov.at[k, pl.ds(m, 2 * vr)], arr.at[k + 1, pl.ds(m + vr, 2 * vr)],
            vsend_sem.at[k], varr_sem.at[k + 1], r, nxt,
        )

    def scatter(k, i):
        to = peer(*others[i])
        return remote(part.at[to], rs.at[k, i], rs_send.at[i], rs_recv.at[i], to, c)

    def gather(k, i):
        mine = ag.at[k, pl.ds(pl.multiple_of(r * sl, sl), sl)]
        return remote(mine, mine, ag_send.at[i], ag_recv.at[i], peer(*others[i]), c)

    def norm_stay(i):
        return remote(nsend.at[0], nrecv.at[0, r], n_send.at[0, i], n_recv.at[0], peer(*others[i]), c)

    def norm_move(i):
        return remote(nsend.at[1], nrecv.at[1, r], n_send.at[1, i], n_recv.at[1], (r + i) % n_row, nxt)

    def home(d):
        q = (c + n_col - d) % n_col
        return q // qpr, q % qpr

    last_slices = remote(mov.at[last, pl.ds(m, nv)], vfin, vsend_sem.at[last], varr_sem.at[ROUNDS], r, nxt)

    def to_owner(k, d):
        owner, j = home(d)
        if k is None:
            src = vfin.at[pl.ds((d - 1) * vr, vr)]
            dst = vo_ref.at[pl.ds(pl.multiple_of(j * width + r * vr, vr), vr), pl.ds(p, p)]
            send, sem = fin_send.at[d - 1], vf_recv.at[j]
        else:
            src = arr.at[k, pl.ds(m + d * vr, vr)]
            dst = va.at[k, j, pl.ds(pl.multiple_of(r * vr, vr), vr)]
            send, sem = fwd_send.at[k, d - 1], va_recv.at[k, j]
        return src, dst, send, sem, owner

    def send_to_owner(k, d):
        src, dst, send, sem, owner = to_owner(k, d)

        @pl.when(owner == r)
        def _():
            pltpu.make_async_copy(src, dst, sem).start()

        @pl.when((owner != r) & (owner // nx == y))
        def _():
            remote(src, dst, send, sem, owner, c).start()

    def sent_to_owner(k, d):
        src, dst, send, sem, owner = to_owner(k, d)

        @pl.when((owner != r) & (owner // nx == y))
        def _():
            remote(src, dst, send, sem, owner, c).wait_send()

    def across(k, d):
        owner, j = home(d)
        src = mov.at[k, pl.ds(m + d * vr, vr)]
        if isinstance(k, int) and k == last:
            dst = vo_ref.at[pl.ds(pl.multiple_of(j * width + r * vr, vr), vr), pl.ds(p, p)]
            sem = vf_recv.at[j]
        else:
            dst = va.at[k + 1, j, pl.ds(pl.multiple_of(r * vr, vr), vr)]
            sem = va_recv.at[k + 1, j]
        return odd & (owner // nx != y), remote(src, dst, x_send.at[k, d], sem, owner, nxt)

    def pass_block(k, j):
        return remote(vmov.at[k, j], va.at[k + 1, j], vm_send.at[k, j], va_recv.at[k + 1, j], r, nxt)

    def last_block(j):
        dst = vo_ref.at[pl.ds(j * width, width), pl.ds(p, p)]
        return remote(vmov.at[last, j], dst, vm_send.at[last, j], vf_recv.at[j], r, nxt)

    def lhs_rows(start, size):
        h = xh[pl.ds(start, size), :]
        return jnp.concatenate([h, xl[pl.ds(start, size), :], h], axis=1)

    def lhs_of(first, second):
        h1, l1 = split(first)
        h2, l2 = split(second)
        return jnp.concatenate([h1, h2, l1, l2, h1, h2], axis=1)

    def one_round(k, carry):
        s = stay[...]
        sh, slo = split(s)
        xh[:, pl.ds(0, p)] = sh
        xl[:, pl.ds(0, p)] = slo
        sth[...] = sh.T
        stl[...] = slo.T
        n1 = jnp.sum(s * s, axis=0, keepdims=True)
        n2 = jnp.zeros((1, p), F32)
        g = jnp.zeros((p, p), F32)
        for ch in range(NCH):
            rows = chunk(ch)
            await_bytes(arr.at[k, rows], arr_sem.at[k, ch])
            a = arr[k, rows]
            ah, al = split(a)
            xh[rows, pl.ds(p, p)] = ah
            xl[rows, pl.ds(p, p)] = al
            n2 = n2 + jnp.sum(a * a, axis=0, keepdims=True)
            th = sth[:, rows]
            g = g + mm3((th, stl[:, rows]), (ah, al))
        which = lax.broadcasted_iota(jnp.int32, (8, p), 0)
        norms = jnp.where(which == 0, n1, jnp.where(which == 1, n2, 0.0))
        for i in range(n_row):
            part[i, pl.ds(0, sl)] = g[i * sl:(i + 1) * sl]
            part[i, pl.ds(sl, 8)] = norms

        @pl.when(k == 0)
        def _():
            pl.semaphore_wait(barrier, len(others) + 2 * n_row)

        for i in range(len(others)):
            scatter(k, i).start()
        total = part[r]
        for i in range(len(others) - 1, -1, -1):
            scatter(k, i).wait_recv()
            total = total + rs[k, i]
        root = jnp.sqrt(total[sl:sl + 8] + 1e-06)
        root1, root2 = root[0:1], root[1:2]
        on_diag = lax.broadcasted_iota(jnp.int32, (sl, p), 1) == lax.broadcasted_iota(jnp.int32, (sl, p), 0) + r * sl
        root_col = jnp.sum(jnp.where(on_diag, root1, 0.0), axis=1, keepdims=True)
        ag[k, pl.ds(pl.multiple_of(r * sl, sl), sl)] = total[:sl] / (root_col * root2)
        for i in range(len(others)):
            gather(k, i).start()
        for d in range(1, ROUNDS):
            there, copy = across(k - 1, d - 1)

            @pl.when(there & (k >= d))
            def _():
                copy.start()

        for i in range(len(others) - 1, -1, -1):
            gather(k, i).wait_recv()

        @pl.when(k > 0)
        def _():
            await_bytes(arr.at[k, pl.ds(m + vr, 2 * vr)], varr_sem.at[k])

        for d in range(1, ROUNDS):
            @pl.when(even & (k >= d))
            def _():
                send_to_owner(k, d)

        coupling = ag[k]
        strength = jnp.sqrt(jnp.sum(coupling * coupling, keepdims=True))
        flipped = coupling.T
        p1, q12, q12t, p2 = turn_blocks(coupling / (1.0 + strength), flipped / (1.0 + strength), eye)
        chosen = jnp.full((1, p), plan_ref[0, k], jnp.int32) == 1
        for ref, top, bottom in (
            (qm, jnp.where(chosen, q12, p1), jnp.where(chosen, p2, -q12t)),
            (qs, jnp.where(chosen, p1, q12), jnp.where(chosen, -q12t, p2)),
        ):
            for at, piece in ((0, top), (p, bottom)):
                hi, lo = split(piece)
                ref[pl.ds(at, p)] = hi
                ref[pl.ds(2 * p + at, p)] = hi
                ref[pl.ds(4 * p + at, p)] = lo
        for ch in range(NCH):
            mov[k, chunk(ch)] = mm(lhs_rows(ch * rc, rc), qm[...])

        @pl.when(k < last)
        def _():
            for ch in range(NCH):
                move_x(k, ch).start()

        @pl.when(k == last)
        def _():
            t = mov[last, pl.ds(0, m)]
            nsend[1] = jnp.broadcast_to(jnp.sum(t * t, axis=0, keepdims=True), (8, p))
            for i in range(n_row):
                norm_move(i).start()

            @pl.when(odd)
            def _():
                mov[last, pl.ds(m, nv)] = mm(lhs_of(vst[last], arr[last, pl.ds(m, nv)]), qm[...])
                last_slices.start()
                for d in range(3):
                    there, copy = across(last, d)

                    @pl.when(there)
                    def _():
                        copy.start()

            for ch in range(NCH):
                move_x_last(ch).start()

        for ch in range(NCH):
            stay[chunk(ch)] = mm(lhs_rows(ch * rc, rc), qs[...])

        @pl.when(k < last)
        def _():
            v_lhs = lhs_of(vst[k], arr[k, pl.ds(m, nv)])
            mov[k, pl.ds(m, nv)] = mm(v_lhs, qm[...])
            vst[k + 1] = mm(v_lhs, qs[...])
            move_v(k).start()

        for j in range(qpr):
            @pl.when((lag[j] <= k) & (k < last))
            def _():
                @pl.when(lag[j] >= 1)
                def _():
                    await_bytes(va.at[k, j], va_recv.at[k, j])

                for ch in range(NCH):
                    rows = pl.ds(ch * wc, wc)
                    block = lhs_of(vs[j, rows], va[k, j, rows])
                    vmov[k, j, rows] = mm(block, qm[...])
                    vs[j, rows] = mm(block, qs[...])

                @pl.when(even)
                def _():
                    pass_block(k, j).start()

        for i in range(len(others)):
            scatter(k, i).wait_send()
            gather(k, i).wait_send()
        return carry

    lax.fori_loop(0, ROUNDS, one_round, 0)

    t = stay[...]
    nsend[0] = jnp.broadcast_to(jnp.sum(t * t, axis=0, keepdims=True), (8, p))
    for i in range(len(others)):
        norm_stay(i).start()
    pltpu.make_async_copy(nsend.at[0], nrecv.at[0, r], n_recv.at[0]).start()
    xo_ref[:, pl.ds(0, p)] = t

    for j in range(qpr):
        @pl.when((lag[j] >= 1) & (lag[j] <= 2))
        def _():
            await_bytes(va.at[last, j], va_recv.at[last, j])

        @pl.when((lag[j] <= 2) & even)
        def _():
            for ch in range(NCH):
                rows = pl.ds(ch * wc, wc)
                vmov[last, j, rows] = mm(lhs_of(vs[j, rows], va[last, j, rows]), qm[...])
            last_block(j).start()

    @pl.when(even)
    def _():
        await_bytes(vfin, varr_sem.at[ROUNDS])
        for d in range(1, 4):
            send_to_owner(None, d)

    for j in range(qpr):
        @pl.when(lag[j] <= 2)
        def _():
            for ch in range(NCH):
                rows = pl.ds(ch * wc, wc)
                vo_ref[pl.ds(j * width + ch * wc, wc), pl.ds(0, p)] = mm(
                    lhs_of(vs[j, rows], va[last, j, rows]), qs[...]
                )

    for panel in range(2):
        await_bytes(nrecv.at[panel], n_recv.at[panel])
        sums = nrecv[panel, 0]
        for i in range(1, n_row):
            sums = sums + nrecv[panel, i]
        so_ref[:, pl.ds(panel * p, p)] = jnp.sqrt(sums[0:1] / (m * n_row))

    for i in range(len(others)):
        norm_stay(i).wait_send()
    for i in range(n_row):
        norm_move(i).wait_send()
    for k in range(last):
        for ch in range(NCH):
            move_x(k, ch).wait_send()
        move_v(k).wait_send()
    @pl.when(odd)
    def _():
        last_slices.wait_send()

    for k in range(ROUNDS):
        for d in range(k + 1):
            there, copy = across(k, d)

            @pl.when(there)
            def _():
                copy.wait_send()

    @pl.when(even)
    def _():
        for k in range(1, ROUNDS):
            for d in range(1, k + 1):
                sent_to_owner(k, d)
        for d in range(1, 4):
            sent_to_owner(None, d)

    for k in range(last):
        for j in range(qpr):
            @pl.when(even & (lag[j] <= k))
            def _():
                pass_block(k, j).wait_send()

    for j in range(qpr):
        @pl.when((lag[j] <= 2) & even)
        def _():
            last_block(j).wait_send()

        @pl.when((lag[j] >= 1) & (lag[j] <= 3))
        def _():
            await_bytes(vo_ref.at[pl.ds(j * width, width), pl.ds(p, p)], vf_recv.at[j])

    for ch in range(NCH):
        move_x_last(ch).wait_send()
        move_x_last(ch).wait_recv()


def write_out(x_ref, v_ref, s_ref, xo_hbm, vo_hbm, so_ref, sem):
    copies = []
    half = x_ref.shape[0] // 2
    for src, dst in ((v_ref, vo_hbm), (x_ref, xo_hbm)):
        for start in range(0, src.shape[0], half):
            rows = pl.ds(start, half)
            copies.append(pltpu.make_async_copy(src.at[rows], dst.at[rows], sem.at[len(copies)]))
    for copy in copies:
        copy.start()
    so_ref[...] = s_ref[...]
    for copy in copies:
        copy.wait()


def per_device(activations, plan):
    n_row, n_col = lax.axis_size("row"), lax.axis_size("col")
    m, width = activations.shape
    p = width // 2
    sl = p // n_row
    vr = width // n_row
    rows = m + 3 * vr
    qpr = n_col // n_row
    dma = pltpu.SemaphoreType.DMA
    vmem = pl.BlockSpec(memory_space=pltpu.VMEM)
    shapes = (
        jax.ShapeDtypeStruct((m, width), F32),
        jax.ShapeDtypeStruct((qpr * width, width), F32),
        jax.ShapeDtypeStruct((1, width), F32),
    )
    results = pl.pallas_call(
        functools.partial(kernel, n_row, n_col),
        out_shape=shapes,
        in_specs=[pl.BlockSpec(memory_space=pltpu.SMEM), pl.BlockSpec(memory_space=pltpu.HBM)],
        out_specs=(vmem, vmem, vmem),
        scratch_shapes=[
            pltpu.VMEM((m, p), F32),
            pltpu.VMEM((ROUNDS, 3 * vr, p), F32),
            pltpu.VMEM((ROUNDS, rows, p), F32),
            pltpu.VMEM((ROUNDS, rows, p), F32),
            pltpu.VMEM((m, width), BF16),
            pltpu.VMEM((m, width), BF16),
            pltpu.VMEM((p, m), BF16),
            pltpu.VMEM((p, m), BF16),
            pltpu.VMEM((3 * width, p), BF16),
            pltpu.VMEM((3 * width, p), BF16),
            pltpu.VMEM((n_row, sl + 8, p), F32),
            pltpu.VMEM((ROUNDS, n_row - 1, sl + 8, p), F32),
            pltpu.VMEM((ROUNDS, p, p), F32),
            pltpu.VMEM((qpr, width, p), F32),
            pltpu.VMEM((ROUNDS, qpr, width, p), F32),
            pltpu.VMEM((ROUNDS, qpr, width, p), F32),
            pltpu.VMEM((3 * vr, p), F32),
            pltpu.VMEM((2, 8, p), F32),
            pltpu.VMEM((2, n_row, 8, p), F32),
            dma,
            dma((ROUNDS + 1, NCH)),
            dma((ROUNDS + 1,)),
            dma((ROUNDS, NCH)),
            dma((ROUNDS,)),
            dma((n_row - 1,)),
            dma((n_row - 1,)),
            dma((n_row - 1,)),
            dma((n_row - 1,)),
            dma((ROUNDS, 2)),
            dma((3,)),
            dma((ROUNDS, 3)),
            dma((ROUNDS, qpr)),
            dma((qpr,)),
            dma((ROUNDS, qpr)),
            dma((2, n_row)),
            dma((2,)),
        ],
        compiler_params=pltpu.CompilerParams(collective_id=0, has_side_effects=True, vmem_limit_bytes=48 * 2**20),
    )(plan.T, activations)
    hbm = pl.BlockSpec(memory_space=pltpu.HBM)
    anywhere = pl.BlockSpec(memory_space=pl.ANY)
    rotated, vectors, spread = pl.pallas_call(
        write_out,
        out_shape=shapes,
        in_specs=[anywhere, anywhere, vmem],
        out_specs=(hbm, hbm, vmem),
        scratch_shapes=[dma((2 * (qpr + 1),))],
        compiler_params=pltpu.CompilerParams(vmem_limit_bytes=2**20),
    )(*results)
    return rotated, vectors, spread.reshape(width)


def solution(mesh):
    in_specs = (P("row", "col"), P(None, "col"))
    out_specs = (P("row", "col"), P("row", "col"), P("col"))
    return jax.shard_map(
        per_device, mesh=mesh, in_specs=in_specs, out_specs=out_specs, check_vma=False
    )
```

```python
import functools

import jax
import jax.numpy as jnp
from jax import lax
from jax.experimental import pallas as pl
from jax.experimental.pallas import tpu as pltpu
from jax.sharding import PartitionSpec as P

ROUNDS = 3
NY = 2
NCH = 2
MESH = pl.DeviceIdType.MESH
F32 = jnp.float32
BF16 = jnp.bfloat16


def split(x):
    hi = x.astype(BF16)
    lo = (x - hi.astype(F32)).astype(BF16)
    return hi, lo


def mm(a, b):
    return lax.dot_general(a, b, (((1,), (0,)), ((), ())), preferred_element_type=F32)


def mm3(a, b):
    ah, al = a
    bh, bl = b
    return mm(
        jnp.concatenate([ah, al, ah], axis=1), jnp.concatenate([bh, bh, bl], axis=0)
    )


def turn_blocks(b, bt, eye):
    bs, bts = split(b), split(bt)
    a = mm3(bs, bts)
    a_s = split(a)
    f1 = 0.25 * mm3(a_s, a_s) - 0.75 * a
    f1s = split(f1)
    d1 = mm3(a_s, f1s)
    d1s = split(d1)
    g = 0.25 * mm3(d1s, d1s) - 0.75 * d1
    w = 0.5 * a + 0.5 * d1 - 0.25 * mm3(d1s, a_s)
    h = mm3(f1s, split(g))
    q = 0.25 * d1 - 0.5 * (eye + f1 + h - mm3(split(w), split(h)))
    q_s = split(q)
    t = split(mm3(q_s, bs))
    tt = split(mm3(bts, q_s))
    return eye + mm3(a_s, q_s), b + mm3(a_s, t), bt + mm3(tt, a_s), eye + mm3(bts, t)


def kernel(
    n_row, n_col, plan_ref, x_hbm, xo_ref, vo_ref, so_ref,
    stay, vst, arr, mov, xh, xl, sth, stl, qm, qs, part, rs, ag, vs, va, vmov, vfin, nsend, nrecv,
    load_sem, arr_sem, varr_sem, xsend_sem, vsend_sem,
    rs_send, rs_recv, ag_send, ag_recv,
    fwd_send, fin_send, x_send, va_recv, vf_recv, vm_send, n_send, n_recv,
):
    m, width = x_hbm.shape
    p = width // 2
    sl = p // n_row
    vr = width // n_row
    nv = 3 * vr
    qpr = n_col // n_row
    nx = n_row // NY
    rc, wc = m // NCH, width // NCH
    last = ROUNDS - 1
    r = lax.axis_index("row")
    c = lax.axis_index("col")
    y, x = r // nx, r % nx
    nxt, prv = (c + 1) % n_col, (c + n_col - 1) % n_col
    others = [(dy, dx) for dy in range(NY - 1, -1, -1) for dx in range(nx) if dy or dx]

    def peer(dy, dx):
        return ((y + dy) % NY) * nx + (x + dx) % nx

    def greet(row, col):
        pl.semaphore_signal(barrier, inc=1, device_id={"row": row, "col": col}, device_id_type=MESH)

    def remote(src, dst, send, recv, row, col):
        return pltpu.make_async_remote_copy(
            src_ref=src, dst_ref=dst, send_sem=send, recv_sem=recv,
            device_id={"row": row, "col": col}, device_id_type=MESH,
        )

    def await_bytes(ref, sem):
        pltpu.make_async_copy(ref, ref, sem).wait()

    barrier = pltpu.get_barrier_semaphore()
    for dy, dx in others:
        greet(peer(dy, dx), c)
    for rr in range(n_row):
        greet(rr, nxt)
        greet(rr, prv)

    load = pltpu.make_async_copy(x_hbm.at[:, pl.ds(0, p)], stay, load_sem)
    load.start()
    for ch in range(NCH):
        pltpu.make_async_copy(
            x_hbm.at[pl.ds(ch * rc, rc), pl.ds(p, p)],
            arr.at[0, pl.ds(ch * rc, rc)],
            arr_sem.at[0, ch],
        ).start()

    lane = lax.broadcasted_iota(jnp.int32, (vr, p), 1)
    row_id = lax.broadcasted_iota(jnp.int32, (vr, p), 0) + r * vr
    vst[0, pl.ds(0, vr)] = jnp.where(row_id == lane, 1.0, 0.0).astype(F32)
    arr[0, pl.ds(m, vr)] = jnp.where(row_id == lane + p, 1.0, 0.0).astype(F32)
    vst[0, pl.ds(vr, 2 * vr)] = jnp.zeros((2 * vr, p), F32)
    arr[0, pl.ds(m + vr, 2 * vr)] = jnp.zeros((2 * vr, p), F32)
    for k in range(1, ROUNDS):
        arr[k, pl.ds(m, vr)] = jnp.zeros((vr, p), F32)

    lag = [(c + n_col - (qpr * r + j)) % n_col for j in range(qpr)]
    for j in range(qpr):
        @pl.when(lag[j] > 2)
        def _():
            vo_ref[pl.ds(j * width, width), pl.ds(0, p)] = jnp.zeros((width, p), F32)

        @pl.when((lag[j] < 1) | (lag[j] > 3))
        def _():
            vo_ref[pl.ds(j * width, width), pl.ds(p, p)] = jnp.zeros((width, p), F32)

        @pl.when(lag[j] == 0)
        def _():
            col_id = lax.broadcasted_iota(jnp.int32, (width, p), 1)
            at = lax.broadcasted_iota(jnp.int32, (width, p), 0)
            vs[j] = jnp.where(at == col_id, 1.0, 0.0).astype(F32)
            va[0, j] = jnp.where(at == col_id + p, 1.0, 0.0).astype(F32)
            for k in range(1, ROUNDS):
                va[k, j] = jnp.zeros((width, p), F32)

        @pl.when((lag[j] >= 1) & (lag[j] <= 2))
        def _():
            vs[j] = jnp.zeros((width, p), F32)

    odd = c % 2 == 1
    even = c % 2 == 0
    eye = jnp.where(
        lax.broadcasted_iota(jnp.int32, (p, p), 0) == lax.broadcasted_iota(jnp.int32, (p, p), 1), 1.0, 0.0
    ).astype(F32)
    load.wait()

    def chunk(ch):
        return pl.ds(ch * rc, rc)

    def move_x(k, ch):
        return remote(
            mov.at[k, chunk(ch)], arr.at[k + 1, chunk(ch)], xsend_sem.at[k, ch], arr_sem.at[k + 1, ch], r, nxt
        )

    def move_x_last(ch):
        return remote(
            mov.at[last, chunk(ch)], xo_ref.at[chunk(ch), pl.ds(p, p)], xsend_sem.at[last, ch],
            arr_sem.at[ROUNDS, ch], r, nxt,
        )

    def move_v(k):
        return remote(
            mov.at[k, pl.ds(m, 2 * vr)], arr.at[k + 1, pl.ds(m + vr, 2 * vr)],
            vsend_sem.at[k], varr_sem.at[k + 1], r, nxt,
        )

    def scatter(k, i):
        to = peer(*others[i])
        return remote(part.at[to], rs.at[k, i], rs_send.at[i], rs_recv.at[i], to, c)

    def gather(k, i):
        mine = ag.at[k, pl.ds(pl.multiple_of(r * sl, sl), sl)]
        return remote(mine, mine, ag_send.at[i], ag_recv.at[i], peer(*others[i]), c)

    def norm_stay(i):
        return remote(nsend.at[0], nrecv.at[0, r], n_send.at[0, i], n_recv.at[0], peer(*others[i]), c)

    def norm_move(i):
        return remote(nsend.at[1], nrecv.at[1, r], n_send.at[1, i], n_recv.at[1], (r + i) % n_row, nxt)

    def home(d):
        q = (c + n_col - d) % n_col
        return q // qpr, q % qpr

    last_slices = remote(mov.at[last, pl.ds(m, nv)], vfin, vsend_sem.at[last], varr_sem.at[ROUNDS], r, nxt)

    def to_owner(k, d):
        owner, j = home(d)
        if k is None:
            src = vfin.at[pl.ds((d - 1) * vr, vr)]
            dst = vo_ref.at[pl.ds(pl.multiple_of(j * width + r * vr, vr), vr), pl.ds(p, p)]
            send, sem = fin_send.at[d - 1], vf_recv.at[j]
        else:
            src = arr.at[k, pl.ds(m + d * vr, vr)]
            dst = va.at[k, j, pl.ds(pl.multiple_of(r * vr, vr), vr)]
            send, sem = fwd_send.at[k, d - 1], va_recv.at[k, j]
        return src, dst, send, sem, owner

    def send_to_owner(k, d):
        src, dst, send, sem, owner = to_owner(k, d)

        @pl.when(owner == r)
        def _():
            pltpu.make_async_copy(src, dst, sem).start()

        @pl.when((owner != r) & (owner // nx == y))
        def _():
            remote(src, dst, send, sem, owner, c).start()

    def sent_to_owner(k, d):
        src, dst, send, sem, owner = to_owner(k, d)

        @pl.when((owner != r) & (owner // nx == y))
        def _():
            remote(src, dst, send, sem, owner, c).wait_send()

    def across(k, d):
        owner, j = home(d)
        src = mov.at[k, pl.ds(m + d * vr, vr)]
        if isinstance(k, int) and k == last:
            dst = vo_ref.at[pl.ds(pl.multiple_of(j * width + r * vr, vr), vr), pl.ds(p, p)]
            sem = vf_recv.at[j]
        else:
            dst = va.at[k + 1, j, pl.ds(pl.multiple_of(r * vr, vr), vr)]
            sem = va_recv.at[k + 1, j]
        return odd & (owner // nx != y), remote(src, dst, x_send.at[k, d], sem, owner, nxt)

    def pass_block(k, j):
        return remote(vmov.at[k, j], va.at[k + 1, j], vm_send.at[k, j], va_recv.at[k + 1, j], r, nxt)

    def last_block(j):
        dst = vo_ref.at[pl.ds(j * width, width), pl.ds(p, p)]
        return remote(vmov.at[last, j], dst, vm_send.at[last, j], vf_recv.at[j], r, nxt)

    def lhs_rows(start, size):
        h = xh[pl.ds(start, size), :]
        return jnp.concatenate([h, xl[pl.ds(start, size), :], h], axis=1)

    def lhs_of(first, second):
        h1, l1 = split(first)
        h2, l2 = split(second)
        return jnp.concatenate([h1, h2, l1, l2, h1, h2], axis=1)

    def one_round(k, carry):
        s = stay[...]
        sh, slo = split(s)
        xh[:, pl.ds(0, p)] = sh
        xl[:, pl.ds(0, p)] = slo
        sth[...] = sh.T
        stl[...] = slo.T
        n1 = jnp.sum(s * s, axis=0, keepdims=True)
        n2 = jnp.zeros((1, p), F32)
        g = jnp.zeros((p, p), F32)
        for ch in range(NCH):
            rows = chunk(ch)
            await_bytes(arr.at[k, rows], arr_sem.at[k, ch])
            a = arr[k, rows]
            ah, al = split(a)
            xh[rows, pl.ds(p, p)] = ah
            xl[rows, pl.ds(p, p)] = al
            n2 = n2 + jnp.sum(a * a, axis=0, keepdims=True)
            th = sth[:, rows]
            g = g + mm3((th, stl[:, rows]), (ah, al))
        which = lax.broadcasted_iota(jnp.int32, (8, p), 0)
        norms = jnp.where(which == 0, n1, jnp.where(which == 1, n2, 0.0))
        for i in range(n_row):
            part[i, pl.ds(0, sl)] = g[i * sl:(i + 1) * sl]
            part[i, pl.ds(sl, 8)] = norms

        @pl.when(k == 0)
        def _():
            pl.semaphore_wait(barrier, len(others) + 2 * n_row)

        for i in range(len(others)):
            scatter(k, i).start()
        total = part[r]
        for i in range(len(others) - 1, -1, -1):
            scatter(k, i).wait_recv()
            total = total + rs[k, i]
        root = jnp.sqrt(total[sl:sl + 8] + 1e-06)
        root1, root2 = root[0:1], root[1:2]
        on_diag = lax.broadcasted_iota(jnp.int32, (sl, p), 1) == lax.broadcasted_iota(jnp.int32, (sl, p), 0) + r * sl
        root_col = jnp.sum(jnp.where(on_diag, root1, 0.0), axis=1, keepdims=True)
        ag[k, pl.ds(pl.multiple_of(r * sl, sl), sl)] = total[:sl] / (root_col * root2)
        for i in range(len(others)):
            gather(k, i).start()
        for d in range(1, ROUNDS):
            there, copy = across(k - 1, d - 1)

            @pl.when(there & (k >= d))
            def _():
                copy.start()

        for i in range(len(others) - 1, -1, -1):
            gather(k, i).wait_recv()

        @pl.when(k > 0)
        def _():
            await_bytes(arr.at[k, pl.ds(m + vr, 2 * vr)], varr_sem.at[k])

        for d in range(1, ROUNDS):
            @pl.when(even & (k >= d))
            def _():
                send_to_owner(k, d)

        coupling = ag[k]
        strength = jnp.sqrt(jnp.sum(coupling * coupling, keepdims=True))
        flipped = coupling.T
        p1, q12, q12t, p2 = turn_blocks(coupling / (1.0 + strength), flipped / (1.0 + strength), eye)
        chosen = jnp.full((1, p), plan_ref[0, k], jnp.int32) == 1
        for ref, top, bottom in (
            (qm, jnp.where(chosen, q12, p1), jnp.where(chosen, p2, -q12t)),
            (qs, jnp.where(chosen, p1, q12), jnp.where(chosen, -q12t, p2)),
        ):
            for at, piece in ((0, top), (p, bottom)):
                hi, lo = split(piece)
                ref[pl.ds(at, p)] = hi
                ref[pl.ds(2 * p + at, p)] = hi
                ref[pl.ds(4 * p + at, p)] = lo
        for ch in range(NCH):
            mov[k, chunk(ch)] = mm(lhs_rows(ch * rc, rc), qm[...])

        @pl.when(k < last)
        def _():
            for ch in range(NCH):
                move_x(k, ch).start()

        @pl.when(k == last)
        def _():
            t = mov[last, pl.ds(0, m)]
            nsend[1] = jnp.broadcast_to(jnp.sum(t * t, axis=0, keepdims=True), (8, p))
            for i in range(n_row):
                norm_move(i).start()

            @pl.when(odd)
            def _():
                mov[last, pl.ds(m, nv)] = mm(lhs_of(vst[last], arr[last, pl.ds(m, nv)]), qm[...])
                last_slices.start()
                for d in range(3):
                    there, copy = across(last, d)

                    @pl.when(there)
                    def _():
                        copy.start()

            for ch in range(NCH):
                move_x_last(ch).start()

        for ch in range(NCH):
            stay[chunk(ch)] = mm(lhs_rows(ch * rc, rc), qs[...])

        @pl.when(k < last)
        def _():
            v_lhs = lhs_of(vst[k], arr[k, pl.ds(m, nv)])
            mov[k, pl.ds(m, nv)] = mm(v_lhs, qm[...])
            vst[k + 1] = mm(v_lhs, qs[...])
            move_v(k).start()

        for j in range(qpr):
            @pl.when((lag[j] <= k) & (k < last))
            def _():
                @pl.when(lag[j] >= 1)
                def _():
                    await_bytes(va.at[k, j], va_recv.at[k, j])

                for ch in range(NCH):
                    rows = pl.ds(ch * wc, wc)
                    block = lhs_of(vs[j, rows], va[k, j, rows])
                    vmov[k, j, rows] = mm(block, qm[...])
                    vs[j, rows] = mm(block, qs[...])

                @pl.when(even)
                def _():
                    pass_block(k, j).start()

        for i in range(len(others)):
            scatter(k, i).wait_send()
            gather(k, i).wait_send()
        return carry

    lax.fori_loop(0, ROUNDS, one_round, 0)

    t = stay[...]
    nsend[0] = jnp.broadcast_to(jnp.sum(t * t, axis=0, keepdims=True), (8, p))
    for i in range(len(others)):
        norm_stay(i).start()
    pltpu.make_async_copy(nsend.at[0], nrecv.at[0, r], n_recv.at[0]).start()
    xo_ref[:, pl.ds(0, p)] = t

    for j in range(qpr):
        @pl.when((lag[j] >= 1) & (lag[j] <= 2))
        def _():
            await_bytes(va.at[last, j], va_recv.at[last, j])

        @pl.when((lag[j] <= 2) & even)
        def _():
            for ch in range(NCH):
                rows = pl.ds(ch * wc, wc)
                vmov[last, j, rows] = mm(lhs_of(vs[j, rows], va[last, j, rows]), qm[...])
            last_block(j).start()

    @pl.when(even)
    def _():
        await_bytes(vfin, varr_sem.at[ROUNDS])
        for d in range(1, 4):
            send_to_owner(None, d)

    for j in range(qpr):
        @pl.when(lag[j] <= 2)
        def _():
            for ch in range(NCH):
                rows = pl.ds(ch * wc, wc)
                vo_ref[pl.ds(j * width + ch * wc, wc), pl.ds(0, p)] = mm(
                    lhs_of(vs[j, rows], va[last, j, rows]), qs[...]
                )

    for panel in range(2):
        await_bytes(nrecv.at[panel], n_recv.at[panel])
        sums = nrecv[panel, 0]
        for i in range(1, n_row):
            sums = sums + nrecv[panel, i]
        so_ref[:, pl.ds(panel * p, p)] = jnp.sqrt(sums[0:1] / (m * n_row))

    for i in range(len(others)):
        norm_stay(i).wait_send()
    for i in range(n_row):
        norm_move(i).wait_send()
    for k in range(last):
        for ch in range(NCH):
            move_x(k, ch).wait_send()
        move_v(k).wait_send()
    @pl.when(odd)
    def _():
        last_slices.wait_send()

    for k in range(ROUNDS):
        for d in range(k + 1):
            there, copy = across(k, d)

            @pl.when(there)
            def _():
                copy.wait_send()

    @pl.when(even)
    def _():
        for k in range(1, ROUNDS):
            for d in range(1, k + 1):
                sent_to_owner(k, d)
        for d in range(1, 4):
            sent_to_owner(None, d)

    for k in range(last):
        for j in range(qpr):
            @pl.when(even & (lag[j] <= k))
            def _():
                pass_block(k, j).wait_send()

    for j in range(qpr):
        @pl.when((lag[j] <= 2) & even)
        def _():
            last_block(j).wait_send()

        @pl.when((lag[j] >= 1) & (lag[j] <= 3))
        def _():
            await_bytes(vo_ref.at[pl.ds(j * width, width), pl.ds(p, p)], vf_recv.at[j])

    for ch in range(NCH):
        move_x_last(ch).wait_send()
        move_x_last(ch).wait_recv()


def write_out(x_ref, v_ref, s_ref, xo_hbm, vo_hbm, so_ref, sem):
    copies = []
    step = x_ref.shape[0] // 4
    for src, dst in ((v_ref, vo_hbm), (x_ref, xo_hbm)):
        for start in range(0, src.shape[0], step):
            rows = pl.ds(start, step)
            copies.append(pltpu.make_async_copy(src.at[rows], dst.at[rows], sem.at[len(copies)]))
    for copy in copies:
        copy.start()
    so_ref[...] = s_ref[...]
    for copy in copies:
        copy.wait()


def per_device(activations, plan):
    n_row, n_col = lax.axis_size("row"), lax.axis_size("col")
    m, width = activations.shape
    p = width // 2
    sl = p // n_row
    vr = width // n_row
    rows = m + 3 * vr
    qpr = n_col // n_row
    dma = pltpu.SemaphoreType.DMA
    vmem = pl.BlockSpec(memory_space=pltpu.VMEM)
    shapes = (
        jax.ShapeDtypeStruct((m, width), F32),
        jax.ShapeDtypeStruct((qpr * width, width), F32),
        jax.ShapeDtypeStruct((1, width), F32),
    )
    results = pl.pallas_call(
        functools.partial(kernel, n_row, n_col),
        out_shape=shapes,
        in_specs=[pl.BlockSpec(memory_space=pltpu.SMEM), pl.BlockSpec(memory_space=pltpu.HBM)],
        out_specs=(vmem, vmem, vmem),
        scratch_shapes=[
            pltpu.VMEM((m, p), F32),
            pltpu.VMEM((ROUNDS, 3 * vr, p), F32),
            pltpu.VMEM((ROUNDS, rows, p), F32),
            pltpu.VMEM((ROUNDS, rows, p), F32),
            pltpu.VMEM((m, width), BF16),
            pltpu.VMEM((m, width), BF16),
            pltpu.VMEM((p, m), BF16),
            pltpu.VMEM((p, m), BF16),
            pltpu.VMEM((3 * width, p), BF16),
            pltpu.VMEM((3 * width, p), BF16),
            pltpu.VMEM((n_row, sl + 8, p), F32),
            pltpu.VMEM((ROUNDS, n_row - 1, sl + 8, p), F32),
            pltpu.VMEM((ROUNDS, p, p), F32),
            pltpu.VMEM((qpr, width, p), F32),
            pltpu.VMEM((ROUNDS, qpr, width, p), F32),
            pltpu.VMEM((ROUNDS, qpr, width, p), F32),
            pltpu.VMEM((3 * vr, p), F32),
            pltpu.VMEM((2, 8, p), F32),
            pltpu.VMEM((2, n_row, 8, p), F32),
            dma,
            dma((ROUNDS + 1, NCH)),
            dma((ROUNDS + 1,)),
            dma((ROUNDS, NCH)),
            dma((ROUNDS,)),
            dma((n_row - 1,)),
            dma((n_row - 1,)),
            dma((n_row - 1,)),
            dma((n_row - 1,)),
            dma((ROUNDS, 2)),
            dma((3,)),
            dma((ROUNDS, 3)),
            dma((ROUNDS, qpr)),
            dma((qpr,)),
            dma((ROUNDS, qpr)),
            dma((2, n_row)),
            dma((2,)),
        ],
        compiler_params=pltpu.CompilerParams(collective_id=0, has_side_effects=True, vmem_limit_bytes=48 * 2**20),
    )(pltpu.with_memory_space_constraint(plan.T, pltpu.HBM), pltpu.with_memory_space_constraint(activations, pltpu.HBM))
    hbm = pl.BlockSpec(memory_space=pltpu.HBM)
    anywhere = pl.BlockSpec(memory_space=pl.ANY)
    rotated, vectors, spread = pl.pallas_call(
        write_out,
        out_shape=shapes,
        in_specs=[anywhere, anywhere, vmem],
        out_specs=(hbm, hbm, vmem),
        scratch_shapes=[dma((4 * (qpr + 1),))],
        compiler_params=pltpu.CompilerParams(vmem_limit_bytes=2**20),
    )(*results)
    return rotated, vectors, spread.reshape(width)


def solution(mesh):
    in_specs = (P("row", "col"), P(None, "col"))
    out_specs = (P("row", "col"), P("row", "col"), P("col"))
    return jax.shard_map(
        per_device, mesh=mesh, in_specs=in_specs, out_specs=out_specs, check_vma=False
    )
```

```python
import functools

import jax
import jax.numpy as jnp
from jax import lax
from jax.experimental import pallas as pl
from jax.experimental.pallas import tpu as pltpu
from jax.sharding import PartitionSpec as P

ROUNDS = 3
NY = 2
NCH = 2
MESH = pl.DeviceIdType.MESH
F32 = jnp.float32
BF16 = jnp.bfloat16


def split(x):
    hi = x.astype(BF16)
    lo = (x - hi.astype(F32)).astype(BF16)
    return hi, lo


def mm(a, b):
    return lax.dot_general(a, b, (((1,), (0,)), ((), ())), preferred_element_type=F32)


def mm3(a, b):
    ah, al = a
    bh, bl = b
    return mm(
        jnp.concatenate([ah, al, ah], axis=1), jnp.concatenate([bh, bh, bl], axis=0)
    )


def turn_blocks(b, bt, eye):
    bs, bts = split(b), split(bt)
    a = mm3(bs, bts)
    a_s = split(a)
    f1 = 0.25 * mm3(a_s, a_s) - 0.75 * a
    f1s = split(f1)
    d1 = mm3(a_s, f1s)
    d1s = split(d1)
    g = 0.25 * mm3(d1s, d1s) - 0.75 * d1
    w = 0.5 * a + 0.5 * d1 - 0.25 * mm3(d1s, a_s)
    h = mm3(f1s, split(g))
    q = 0.25 * d1 - 0.5 * (eye + f1 + h - mm3(split(w), split(h)))
    q_s = split(q)
    t = split(mm3(q_s, bs))
    tt = split(mm3(bts, q_s))
    return eye + mm3(a_s, q_s), b + mm3(a_s, t), bt + mm3(tt, a_s), eye + mm3(bts, t)


def kernel(
    n_row, n_col, plan_ref, x_hbm, xo_ref, vo_ref, so_ref,
    stay, vst, arr, mov, xh, xl, sth, stl, qm, qs, part, rs, ag, vs, va, vmov, vfin, nsend, nrecv,
    load_sem, arr_sem, varr_sem, xsend_sem, vsend_sem,
    rs_send, rs_recv, ag_send, ag_recv,
    fwd_send, fin_send, x_send, va_recv, vf_recv, vm_send, n_send, n_recv,
):
    m, width = x_hbm.shape
    p = width // 2
    sl = p // n_row
    vr = width // n_row
    nv = 3 * vr
    qpr = n_col // n_row
    nx = n_row // NY
    rc, wc = m // NCH, width // NCH
    last = ROUNDS - 1
    r = lax.axis_index("row")
    c = lax.axis_index("col")
    y, x = r // nx, r % nx
    nxt, prv = (c + 1) % n_col, (c + n_col - 1) % n_col
    others = [(dy, dx) for dy in range(NY - 1, -1, -1) for dx in range(nx) if dy or dx]

    def peer(dy, dx):
        return ((y + dy) % NY) * nx + (x + dx) % nx

    def greet(row, col):
        pl.semaphore_signal(barrier, inc=1, device_id={"row": row, "col": col}, device_id_type=MESH)

    def remote(src, dst, send, recv, row, col):
        return pltpu.make_async_remote_copy(
            src_ref=src, dst_ref=dst, send_sem=send, recv_sem=recv,
            device_id={"row": row, "col": col}, device_id_type=MESH,
        )

    def await_bytes(ref, sem):
        pltpu.make_async_copy(ref, ref, sem).wait()

    barrier = pltpu.get_barrier_semaphore()
    for dy, dx in others:
        greet(peer(dy, dx), c)
    for rr in range(n_row):
        greet(rr, nxt)
        greet(rr, prv)

    load = pltpu.make_async_copy(x_hbm.at[:, pl.ds(0, p)], stay, load_sem)
    load.start()
    for ch in range(NCH):
        pltpu.make_async_copy(
            x_hbm.at[pl.ds(ch * rc, rc), pl.ds(p, p)],
            arr.at[0, pl.ds(ch * rc, rc)],
            arr_sem.at[0, ch],
        ).start()

    lane = lax.broadcasted_iota(jnp.int32, (vr, p), 1)
    row_id = lax.broadcasted_iota(jnp.int32, (vr, p), 0) + r * vr
    vst[0, pl.ds(0, vr)] = jnp.where(row_id == lane, 1.0, 0.0).astype(F32)
    arr[0, pl.ds(m, vr)] = jnp.where(row_id == lane + p, 1.0, 0.0).astype(F32)
    vst[0, pl.ds(vr, 2 * vr)] = jnp.zeros((2 * vr, p), F32)
    arr[0, pl.ds(m + vr, 2 * vr)] = jnp.zeros((2 * vr, p), F32)
    for k in range(1, ROUNDS):
        arr[k, pl.ds(m, vr)] = jnp.zeros((vr, p), F32)

    lag = [(c + n_col - (qpr * r + j)) % n_col for j in range(qpr)]
    for j in range(qpr):
        @pl.when(lag[j] > 2)
        def _():
            vo_ref[pl.ds(j * width, width), pl.ds(0, p)] = jnp.zeros((width, p), F32)

        @pl.when((lag[j] < 1) | (lag[j] > 3))
        def _():
            vo_ref[pl.ds(j * width, width), pl.ds(p, p)] = jnp.zeros((width, p), F32)

        @pl.when(lag[j] == 0)
        def _():
            col_id = lax.broadcasted_iota(jnp.int32, (width, p), 1)
            at = lax.broadcasted_iota(jnp.int32, (width, p), 0)
            vs[j] = jnp.where(at == col_id, 1.0, 0.0).astype(F32)
            va[0, j] = jnp.where(at == col_id + p, 1.0, 0.0).astype(F32)
            for k in range(1, ROUNDS):
                va[k, j] = jnp.zeros((width, p), F32)

        @pl.when((lag[j] >= 1) & (lag[j] <= 2))
        def _():
            vs[j] = jnp.zeros((width, p), F32)

    odd = c % 2 == 1
    even = c % 2 == 0
    eye = jnp.where(
        lax.broadcasted_iota(jnp.int32, (p, p), 0) == lax.broadcasted_iota(jnp.int32, (p, p), 1), 1.0, 0.0
    ).astype(F32)
    load.wait()

    def chunk(ch):
        return pl.ds(ch * rc, rc)

    def move_x(k, ch):
        return remote(
            mov.at[k, chunk(ch)], arr.at[k + 1, chunk(ch)], xsend_sem.at[k, ch], arr_sem.at[k + 1, ch], r, nxt
        )

    def move_x_last(part_id):
        rows = pl.ds(m // 4, m - m // 4) if part_id else pl.ds(0, m // 4)
        return remote(
            mov.at[last, rows], xo_ref.at[rows, pl.ds(p, p)], xsend_sem.at[last, part_id],
            arr_sem.at[ROUNDS, part_id], r, nxt,
        )

    def move_v(k):
        return remote(
            mov.at[k, pl.ds(m, 2 * vr)], arr.at[k + 1, pl.ds(m + vr, 2 * vr)],
            vsend_sem.at[k], varr_sem.at[k + 1], r, nxt,
        )

    def scatter(k, i):
        to = peer(*others[i])
        return remote(part.at[to], rs.at[k, i], rs_send.at[i], rs_recv.at[i], to, c)

    def gather(k, i):
        mine = ag.at[k, pl.ds(pl.multiple_of(r * sl, sl), sl)]
        return remote(mine, mine, ag_send.at[i], ag_recv.at[i], peer(*others[i]), c)

    def norm_stay(i):
        return remote(nsend.at[0], nrecv.at[0, r], n_send.at[0, i], n_recv.at[0], peer(*others[i]), c)

    def norm_move(i):
        return remote(nsend.at[1], nrecv.at[1, r], n_send.at[1, i], n_recv.at[1], (r + i) % n_row, nxt)

    def home(d):
        q = (c + n_col - d) % n_col
        return q // qpr, q % qpr

    last_slices = remote(mov.at[last, pl.ds(m, nv)], vfin, vsend_sem.at[last], varr_sem.at[ROUNDS], r, nxt)

    def to_owner(k, d):
        owner, j = home(d)
        if k is None:
            src = vfin.at[pl.ds((d - 1) * vr, vr)]
            dst = vo_ref.at[pl.ds(pl.multiple_of(j * width + r * vr, vr), vr), pl.ds(p, p)]
            send, sem = fin_send.at[d - 1], vf_recv.at[j]
        else:
            src = arr.at[k, pl.ds(m + d * vr, vr)]
            dst = va.at[k, j, pl.ds(pl.multiple_of(r * vr, vr), vr)]
            send, sem = fwd_send.at[k, d - 1], va_recv.at[k, j]
        return src, dst, send, sem, owner

    def send_to_owner(k, d):
        src, dst, send, sem, owner = to_owner(k, d)

        @pl.when(owner == r)
        def _():
            pltpu.make_async_copy(src, dst, sem).start()

        @pl.when((owner != r) & (owner // nx == y))
        def _():
            remote(src, dst, send, sem, owner, c).start()

    def sent_to_owner(k, d):
        src, dst, send, sem, owner = to_owner(k, d)

        @pl.when((owner != r) & (owner // nx == y))
        def _():
            remote(src, dst, send, sem, owner, c).wait_send()

    def across(k, d):
        owner, j = home(d)
        src = mov.at[k, pl.ds(m + d * vr, vr)]
        if isinstance(k, int) and k == last:
            dst = vo_ref.at[pl.ds(pl.multiple_of(j * width + r * vr, vr), vr), pl.ds(p, p)]
            sem = vf_recv.at[j]
        else:
            dst = va.at[k + 1, j, pl.ds(pl.multiple_of(r * vr, vr), vr)]
            sem = va_recv.at[k + 1, j]
        return odd & (owner // nx != y), remote(src, dst, x_send.at[k, d], sem, owner, nxt)

    def pass_block(k, j):
        return remote(vmov.at[k, j], va.at[k + 1, j], vm_send.at[k, j], va_recv.at[k + 1, j], r, nxt)

    def last_block(j):
        dst = vo_ref.at[pl.ds(j * width, width), pl.ds(p, p)]
        return remote(vmov.at[last, j], dst, vm_send.at[last, j], vf_recv.at[j], r, nxt)

    def lhs_rows(start, size):
        h = xh[pl.ds(start, size), :]
        return jnp.concatenate([h, xl[pl.ds(start, size), :], h], axis=1)

    def lhs_of(first, second):
        h1, l1 = split(first)
        h2, l2 = split(second)
        return jnp.concatenate([h1, h2, l1, l2, h1, h2], axis=1)

    def one_round(k, carry):
        s = stay[...]
        sh, slo = split(s)
        xh[:, pl.ds(0, p)] = sh
        xl[:, pl.ds(0, p)] = slo
        sth[...] = sh.T
        stl[...] = slo.T
        n1 = jnp.sum(s * s, axis=0, keepdims=True)
        n2 = jnp.zeros((1, p), F32)
        g = jnp.zeros((p, p), F32)
        for ch in range(NCH):
            rows = chunk(ch)
            await_bytes(arr.at[k, rows], arr_sem.at[k, ch])
            a = arr[k, rows]
            ah, al = split(a)
            xh[rows, pl.ds(p, p)] = ah
            xl[rows, pl.ds(p, p)] = al
            n2 = n2 + jnp.sum(a * a, axis=0, keepdims=True)
            th = sth[:, rows]
            g = g + mm3((th, stl[:, rows]), (ah, al))
        which = lax.broadcasted_iota(jnp.int32, (8, p), 0)
        norms = jnp.where(which == 0, n1, jnp.where(which == 1, n2, 0.0))
        for i in range(n_row):
            part[i, pl.ds(0, sl)] = g[i * sl:(i + 1) * sl]
            part[i, pl.ds(sl, 8)] = norms

        @pl.when(k == 0)
        def _():
            pl.semaphore_wait(barrier, len(others) + 2 * n_row)

        for i in range(len(others)):
            scatter(k, i).start()
        total = part[r]
        for i in range(len(others) - 1, -1, -1):
            scatter(k, i).wait_recv()
            total = total + rs[k, i]
        root = jnp.sqrt(total[sl:sl + 8] + 1e-06)
        root1, root2 = root[0:1], root[1:2]
        on_diag = lax.broadcasted_iota(jnp.int32, (sl, p), 1) == lax.broadcasted_iota(jnp.int32, (sl, p), 0) + r * sl
        root_col = jnp.sum(jnp.where(on_diag, root1, 0.0), axis=1, keepdims=True)
        ag[k, pl.ds(pl.multiple_of(r * sl, sl), sl)] = total[:sl] / (root_col * root2)
        for i in range(len(others)):
            gather(k, i).start()
        for d in range(1, ROUNDS):
            there, copy = across(k - 1, d - 1)

            @pl.when(there & (k >= d))
            def _():
                copy.start()

        for i in range(len(others) - 1, -1, -1):
            gather(k, i).wait_recv()

        @pl.when(k > 0)
        def _():
            await_bytes(arr.at[k, pl.ds(m + vr, 2 * vr)], varr_sem.at[k])

        for d in range(1, ROUNDS):
            @pl.when(even & (k >= d))
            def _():
                send_to_owner(k, d)

        coupling = ag[k]
        strength = jnp.sqrt(jnp.sum(coupling * coupling, keepdims=True))
        flipped = coupling.T
        p1, q12, q12t, p2 = turn_blocks(coupling / (1.0 + strength), flipped / (1.0 + strength), eye)
        chosen = jnp.full((1, p), plan_ref[0, k], jnp.int32) == 1
        for ref, top, bottom in (
            (qm, jnp.where(chosen, q12, p1), jnp.where(chosen, p2, -q12t)),
            (qs, jnp.where(chosen, p1, q12), jnp.where(chosen, -q12t, p2)),
        ):
            for at, piece in ((0, top), (p, bottom)):
                hi, lo = split(piece)
                ref[pl.ds(at, p)] = hi
                ref[pl.ds(2 * p + at, p)] = hi
                ref[pl.ds(4 * p + at, p)] = lo
        @pl.when(k < last)
        def _():
            for ch in range(NCH):
                mov[k, chunk(ch)] = mm(lhs_rows(ch * rc, rc), qm[...])
                move_x(k, ch).start()

        @pl.when(k == last)
        def _():
            quarter = m // 4
            mov[last, pl.ds(0, quarter)] = mm(lhs_rows(0, quarter), qm[...])
            move_x_last(0).start()
            mov[last, pl.ds(quarter, quarter)] = mm(lhs_rows(quarter, quarter), qm[...])
            mov[last, pl.ds(2 * quarter, 2 * quarter)] = mm(lhs_rows(2 * quarter, 2 * quarter), qm[...])
            t = mov[last, pl.ds(0, m)]
            nsend[1] = jnp.broadcast_to(jnp.sum(t * t, axis=0, keepdims=True), (8, p))
            for i in range(n_row):
                norm_move(i).start()

            @pl.when(odd)
            def _():
                mov[last, pl.ds(m, nv)] = mm(lhs_of(vst[last], arr[last, pl.ds(m, nv)]), qm[...])
                last_slices.start()
                for d in range(3):
                    there, copy = across(last, d)

                    @pl.when(there)
                    def _():
                        copy.start()

            move_x_last(1).start()

        for ch in range(NCH):
            stay[chunk(ch)] = mm(lhs_rows(ch * rc, rc), qs[...])

        @pl.when(k < last)
        def _():
            v_lhs = lhs_of(vst[k], arr[k, pl.ds(m, nv)])
            mov[k, pl.ds(m, nv)] = mm(v_lhs, qm[...])
            vst[k + 1] = mm(v_lhs, qs[...])
            move_v(k).start()

        for j in range(qpr):
            @pl.when((lag[j] <= k) & (k < last))
            def _():
                @pl.when(lag[j] >= 1)
                def _():
                    await_bytes(va.at[k, j], va_recv.at[k, j])

                for ch in range(NCH):
                    rows = pl.ds(ch * wc, wc)
                    block = lhs_of(vs[j, rows], va[k, j, rows])
                    vmov[k, j, rows] = mm(block, qm[...])
                    vs[j, rows] = mm(block, qs[...])

                @pl.when(even)
                def _():
                    pass_block(k, j).start()

        for i in range(len(others)):
            scatter(k, i).wait_send()
            gather(k, i).wait_send()
        return carry

    lax.fori_loop(0, ROUNDS, one_round, 0)

    t = stay[...]
    nsend[0] = jnp.broadcast_to(jnp.sum(t * t, axis=0, keepdims=True), (8, p))
    for i in range(len(others)):
        norm_stay(i).start()
    pltpu.make_async_copy(nsend.at[0], nrecv.at[0, r], n_recv.at[0]).start()
    xo_ref[:, pl.ds(0, p)] = t

    for j in range(qpr):
        @pl.when((lag[j] >= 1) & (lag[j] <= 2))
        def _():
            await_bytes(va.at[last, j], va_recv.at[last, j])

        @pl.when((lag[j] <= 2) & even)
        def _():
            for ch in range(NCH):
                rows = pl.ds(ch * wc, wc)
                vmov[last, j, rows] = mm(lhs_of(vs[j, rows], va[last, j, rows]), qm[...])
            last_block(j).start()

    @pl.when(even)
    def _():
        await_bytes(vfin, varr_sem.at[ROUNDS])
        for d in range(1, 4):
            send_to_owner(None, d)

    for j in range(qpr):
        @pl.when(lag[j] <= 2)
        def _():
            for ch in range(NCH):
                rows = pl.ds(ch * wc, wc)
                vo_ref[pl.ds(j * width + ch * wc, wc), pl.ds(0, p)] = mm(
                    lhs_of(vs[j, rows], va[last, j, rows]), qs[...]
                )

    for panel in range(2):
        await_bytes(nrecv.at[panel], n_recv.at[panel])
        sums = nrecv[panel, 0]
        for i in range(1, n_row):
            sums = sums + nrecv[panel, i]
        so_ref[:, pl.ds(panel * p, p)] = jnp.sqrt(sums[0:1] / (m * n_row))

    for i in range(len(others)):
        norm_stay(i).wait_send()
    for i in range(n_row):
        norm_move(i).wait_send()
    for k in range(last):
        for ch in range(NCH):
            move_x(k, ch).wait_send()
        move_v(k).wait_send()
    @pl.when(odd)
    def _():
        last_slices.wait_send()

    for k in range(ROUNDS):
        for d in range(k + 1):
            there, copy = across(k, d)

            @pl.when(there)
            def _():
                copy.wait_send()

    @pl.when(even)
    def _():
        for k in range(1, ROUNDS):
            for d in range(1, k + 1):
                sent_to_owner(k, d)
        for d in range(1, 4):
            sent_to_owner(None, d)

    for k in range(last):
        for j in range(qpr):
            @pl.when(even & (lag[j] <= k))
            def _():
                pass_block(k, j).wait_send()

    for j in range(qpr):
        @pl.when((lag[j] <= 2) & even)
        def _():
            last_block(j).wait_send()

        @pl.when((lag[j] >= 1) & (lag[j] <= 3))
        def _():
            await_bytes(vo_ref.at[pl.ds(j * width, width), pl.ds(p, p)], vf_recv.at[j])

    for ch in range(NCH):
        move_x_last(ch).wait_send()
        move_x_last(ch).wait_recv()


def write_out(x_ref, v_ref, s_ref, xo_hbm, vo_hbm, so_ref, sem):
    copies = []
    step = x_ref.shape[0] // 4
    for src, dst in ((v_ref, vo_hbm), (x_ref, xo_hbm)):
        for start in range(0, src.shape[0], step):
            rows = pl.ds(start, step)
            copies.append(pltpu.make_async_copy(src.at[rows], dst.at[rows], sem.at[len(copies)]))
    for copy in copies:
        copy.start()
    so_ref[...] = s_ref[...]
    for copy in copies:
        copy.wait()


def per_device(activations, plan):
    n_row, n_col = lax.axis_size("row"), lax.axis_size("col")
    m, width = activations.shape
    p = width // 2
    sl = p // n_row
    vr = width // n_row
    rows = m + 3 * vr
    qpr = n_col // n_row
    dma = pltpu.SemaphoreType.DMA
    vmem = pl.BlockSpec(memory_space=pltpu.VMEM)
    shapes = (
        jax.ShapeDtypeStruct((m, width), F32),
        jax.ShapeDtypeStruct((qpr * width, width), F32),
        jax.ShapeDtypeStruct((1, width), F32),
    )
    results = pl.pallas_call(
        functools.partial(kernel, n_row, n_col),
        out_shape=shapes,
        in_specs=[pl.BlockSpec(memory_space=pltpu.SMEM), pl.BlockSpec(memory_space=pltpu.HBM)],
        out_specs=(vmem, vmem, vmem),
        scratch_shapes=[
            pltpu.VMEM((m, p), F32),
            pltpu.VMEM((ROUNDS, 3 * vr, p), F32),
            pltpu.VMEM((ROUNDS, rows, p), F32),
            pltpu.VMEM((ROUNDS, rows, p), F32),
            pltpu.VMEM((m, width), BF16),
            pltpu.VMEM((m, width), BF16),
            pltpu.VMEM((p, m), BF16),
            pltpu.VMEM((p, m), BF16),
            pltpu.VMEM((3 * width, p), BF16),
            pltpu.VMEM((3 * width, p), BF16),
            pltpu.VMEM((n_row, sl + 8, p), F32),
            pltpu.VMEM((ROUNDS, n_row - 1, sl + 8, p), F32),
            pltpu.VMEM((ROUNDS, p, p), F32),
            pltpu.VMEM((qpr, width, p), F32),
            pltpu.VMEM((ROUNDS, qpr, width, p), F32),
            pltpu.VMEM((ROUNDS, qpr, width, p), F32),
            pltpu.VMEM((3 * vr, p), F32),
            pltpu.VMEM((2, 8, p), F32),
            pltpu.VMEM((2, n_row, 8, p), F32),
            dma,
            dma((ROUNDS + 1, NCH)),
            dma((ROUNDS + 1,)),
            dma((ROUNDS, NCH)),
            dma((ROUNDS,)),
            dma((n_row - 1,)),
            dma((n_row - 1,)),
            dma((n_row - 1,)),
            dma((n_row - 1,)),
            dma((ROUNDS, 2)),
            dma((3,)),
            dma((ROUNDS, 3)),
            dma((ROUNDS, qpr)),
            dma((qpr,)),
            dma((ROUNDS, qpr)),
            dma((2, n_row)),
            dma((2,)),
        ],
        compiler_params=pltpu.CompilerParams(collective_id=0, has_side_effects=True, vmem_limit_bytes=48 * 2**20),
    )(pltpu.with_memory_space_constraint(plan.T, pltpu.HBM), pltpu.with_memory_space_constraint(activations, pltpu.HBM))
    hbm = pl.BlockSpec(memory_space=pltpu.HBM)
    anywhere = pl.BlockSpec(memory_space=pl.ANY)
    rotated, vectors, spread = pl.pallas_call(
        write_out,
        out_shape=shapes,
        in_specs=[anywhere, anywhere, vmem],
        out_specs=(hbm, hbm, vmem),
        scratch_shapes=[dma((4 * (qpr + 1),))],
        compiler_params=pltpu.CompilerParams(vmem_limit_bytes=2**20),
    )(*results)
    return rotated, vectors, spread.reshape(width)


def solution(mesh):
    in_specs = (P("row", "col"), P(None, "col"))
    out_specs = (P("row", "col"), P("row", "col"), P("col"))
    return jax.shard_map(
        per_device, mesh=mesh, in_specs=in_specs, out_specs=out_specs, check_vma=False
    )
```

```python
import functools

import jax
import jax.numpy as jnp
from jax import lax
from jax.experimental import pallas as pl
from jax.experimental.pallas import tpu as pltpu
from jax.sharding import PartitionSpec as P

ROUNDS = 3
NY = 2
NCH = 2
MESH = pl.DeviceIdType.MESH
F32 = jnp.float32
BF16 = jnp.bfloat16


def split(x):
    hi = x.astype(BF16)
    lo = (x - hi.astype(F32)).astype(BF16)
    return hi, lo


def mm(a, b):
    return lax.dot_general(a, b, (((1,), (0,)), ((), ())), preferred_element_type=F32)


def mm3(a, b):
    ah, al = a
    bh, bl = b
    return mm(
        jnp.concatenate([ah, al, ah], axis=1), jnp.concatenate([bh, bh, bl], axis=0)
    )


def turn_blocks(b, bt, eye):
    bs, bts = split(b), split(bt)
    a = mm3(bs, bts)
    a_s = split(a)
    f1 = 0.25 * mm3(a_s, a_s) - 0.75 * a
    f1s = split(f1)
    d1 = mm3(a_s, f1s)
    d1s = split(d1)
    g = 0.25 * mm3(d1s, d1s) - 0.75 * d1
    w = 0.5 * a + 0.5 * d1 - 0.25 * mm3(d1s, a_s)
    h = mm3(f1s, split(g))
    q = 0.25 * d1 - 0.5 * (eye + f1 + h - mm3(split(w), split(h)))
    q_s = split(q)
    t = split(mm3(q_s, bs))
    tt = split(mm3(bts, q_s))
    return eye + mm3(a_s, q_s), b + mm3(a_s, t), bt + mm3(tt, a_s), eye + mm3(bts, t)


def kernel(
    n_row, n_col, plan_ref, x_hbm, xo_ref, vo_ref, so_ref,
    stay, vst, arr, mov, xh, xl, sth, stl, qm, qs, part, rs, ag, vs, va, vmov, vfin, nsend, nrecv,
    load_sem, arr_sem, varr_sem, xsend_sem, vsend_sem,
    rs_send, rs_recv, ag_send, ag_recv,
    fwd_send, fin_send, x_send, va_recv, vf_recv, vm_send, n_send, n_recv,
):
    m, width = x_hbm.shape
    p = width // 2
    sl = p // n_row
    vr = width // n_row
    nv = 3 * vr
    qpr = n_col // n_row
    nx = n_row // NY
    rc, wc = m // NCH, width // NCH
    last = ROUNDS - 1
    r = lax.axis_index("row")
    c = lax.axis_index("col")
    y, x = r // nx, r % nx
    nxt, prv = (c + 1) % n_col, (c + n_col - 1) % n_col
    others = [(dy, dx) for dy in range(NY) for dx in range(nx) if dy or dx]
    others.sort(key=lambda to: -2 * to[0] - min(to[1], nx - to[1]))

    def peer(dy, dx):
        return ((y + dy) % NY) * nx + (x + dx) % nx

    def greet(row, col):
        pl.semaphore_signal(barrier, inc=1, device_id={"row": row, "col": col}, device_id_type=MESH)

    def remote(src, dst, send, recv, row, col):
        return pltpu.make_async_remote_copy(
            src_ref=src, dst_ref=dst, send_sem=send, recv_sem=recv,
            device_id={"row": row, "col": col}, device_id_type=MESH,
        )

    def await_bytes(ref, sem):
        pltpu.make_async_copy(ref, ref, sem).wait()

    barrier = pltpu.get_barrier_semaphore()
    for dy, dx in others:
        greet(peer(dy, dx), c)
    for rr in range(n_row):
        greet(rr, nxt)
        greet(rr, prv)

    load = pltpu.make_async_copy(x_hbm.at[:, pl.ds(0, p)], stay, load_sem)
    load.start()
    for ch in range(NCH):
        pltpu.make_async_copy(
            x_hbm.at[pl.ds(ch * rc, rc), pl.ds(p, p)],
            arr.at[0, pl.ds(ch * rc, rc)],
            arr_sem.at[0, ch],
        ).start()

    lane = lax.broadcasted_iota(jnp.int32, (vr, p), 1)
    row_id = lax.broadcasted_iota(jnp.int32, (vr, p), 0) + r * vr
    vst[0, pl.ds(0, vr)] = jnp.where(row_id == lane, 1.0, 0.0).astype(F32)
    arr[0, pl.ds(m, vr)] = jnp.where(row_id == lane + p, 1.0, 0.0).astype(F32)
    vst[0, pl.ds(vr, 2 * vr)] = jnp.zeros((2 * vr, p), F32)
    arr[0, pl.ds(m + vr, 2 * vr)] = jnp.zeros((2 * vr, p), F32)
    for k in range(1, ROUNDS):
        arr[k, pl.ds(m, vr)] = jnp.zeros((vr, p), F32)

    lag = [(c + n_col - (qpr * r + j)) % n_col for j in range(qpr)]
    for j in range(qpr):
        @pl.when(lag[j] > 2)
        def _():
            vo_ref[pl.ds(j * width, width), pl.ds(0, p)] = jnp.zeros((width, p), F32)

        @pl.when((lag[j] < 1) | (lag[j] > 3))
        def _():
            vo_ref[pl.ds(j * width, width), pl.ds(p, p)] = jnp.zeros((width, p), F32)

        @pl.when(lag[j] == 0)
        def _():
            col_id = lax.broadcasted_iota(jnp.int32, (width, p), 1)
            at = lax.broadcasted_iota(jnp.int32, (width, p), 0)
            vs[j] = jnp.where(at == col_id, 1.0, 0.0).astype(F32)
            va[0, j] = jnp.where(at == col_id + p, 1.0, 0.0).astype(F32)
            for k in range(1, ROUNDS):
                va[k, j] = jnp.zeros((width, p), F32)

        @pl.when((lag[j] >= 1) & (lag[j] <= 2))
        def _():
            vs[j] = jnp.zeros((width, p), F32)

    odd = c % 2 == 1
    even = c % 2 == 0
    eye = jnp.where(
        lax.broadcasted_iota(jnp.int32, (p, p), 0) == lax.broadcasted_iota(jnp.int32, (p, p), 1), 1.0, 0.0
    ).astype(F32)
    load.wait()

    def chunk(ch):
        return pl.ds(ch * rc, rc)

    def move_x(k, ch):
        return remote(
            mov.at[k, chunk(ch)], arr.at[k + 1, chunk(ch)], xsend_sem.at[k, ch], arr_sem.at[k + 1, ch], r, nxt
        )

    def move_x_last(part_id):
        rows = pl.ds(m // 4, m - m // 4) if part_id else pl.ds(0, m // 4)
        return remote(
            mov.at[last, rows], xo_ref.at[rows, pl.ds(p, p)], xsend_sem.at[last, part_id],
            arr_sem.at[ROUNDS, part_id], r, nxt,
        )

    def move_v(k):
        return remote(
            mov.at[k, pl.ds(m, 2 * vr)], arr.at[k + 1, pl.ds(m + vr, 2 * vr)],
            vsend_sem.at[k], varr_sem.at[k + 1], r, nxt,
        )

    def scatter(k, i):
        to = peer(*others[i])
        return remote(part.at[to], rs.at[k, i], rs_send.at[i], rs_recv.at[i], to, c)

    def gather(k, i):
        mine = ag.at[k, pl.ds(pl.multiple_of(r * sl, sl), sl)]
        return remote(mine, mine, ag_send.at[i], ag_recv.at[i], peer(*others[i]), c)

    def norm_stay(i):
        return remote(nsend.at[0], nrecv.at[0, r], n_send.at[0, i], n_recv.at[0], peer(*others[i]), c)

    def norm_move(i):
        return remote(nsend.at[1], nrecv.at[1, r], n_send.at[1, i], n_recv.at[1], (r + i) % n_row, nxt)

    def home(d):
        q = (c + n_col - d) % n_col
        return q // qpr, q % qpr

    last_slices = remote(mov.at[last, pl.ds(m, nv)], vfin, vsend_sem.at[last], varr_sem.at[ROUNDS], r, nxt)

    def to_owner(k, d):
        owner, j = home(d)
        if k is None:
            src = vfin.at[pl.ds((d - 1) * vr, vr)]
            dst = vo_ref.at[pl.ds(pl.multiple_of(j * width + r * vr, vr), vr), pl.ds(p, p)]
            send, sem = fin_send.at[d - 1], vf_recv.at[j]
        else:
            src = arr.at[k, pl.ds(m + d * vr, vr)]
            dst = va.at[k, j, pl.ds(pl.multiple_of(r * vr, vr), vr)]
            send, sem = fwd_send.at[k, d - 1], va_recv.at[k, j]
        return src, dst, send, sem, owner

    def send_to_owner(k, d):
        src, dst, send, sem, owner = to_owner(k, d)

        @pl.when(owner == r)
        def _():
            pltpu.make_async_copy(src, dst, sem).start()

        @pl.when((owner != r) & (owner // nx == y))
        def _():
            remote(src, dst, send, sem, owner, c).start()

    def sent_to_owner(k, d):
        src, dst, send, sem, owner = to_owner(k, d)

        @pl.when((owner != r) & (owner // nx == y))
        def _():
            remote(src, dst, send, sem, owner, c).wait_send()

    def across(k, d):
        owner, j = home(d)
        src = mov.at[k, pl.ds(m + d * vr, vr)]
        if isinstance(k, int) and k == last:
            dst = vo_ref.at[pl.ds(pl.multiple_of(j * width + r * vr, vr), vr), pl.ds(p, p)]
            sem = vf_recv.at[j]
        else:
            dst = va.at[k + 1, j, pl.ds(pl.multiple_of(r * vr, vr), vr)]
            sem = va_recv.at[k + 1, j]
        return odd & (owner // nx != y), remote(src, dst, x_send.at[k, d], sem, owner, nxt)

    def pass_block(k, j):
        return remote(vmov.at[k, j], va.at[k + 1, j], vm_send.at[k, j], va_recv.at[k + 1, j], r, nxt)

    def last_block(j):
        dst = vo_ref.at[pl.ds(j * width, width), pl.ds(p, p)]
        return remote(vmov.at[last, j], dst, vm_send.at[last, j], vf_recv.at[j], r, nxt)

    def lhs_rows(start, size):
        h = xh[pl.ds(start, size), :]
        return jnp.concatenate([h, xl[pl.ds(start, size), :], h], axis=1)

    def lhs_of(first, second):
        h1, l1 = split(first)
        h2, l2 = split(second)
        return jnp.concatenate([h1, h2, l1, l2, h1, h2], axis=1)

    def one_round(k, carry):
        s = stay[...]
        sh, slo = split(s)
        xh[:, pl.ds(0, p)] = sh
        xl[:, pl.ds(0, p)] = slo
        sth[...] = sh.T
        stl[...] = slo.T
        n1 = jnp.sum(s * s, axis=0, keepdims=True)
        n2 = jnp.zeros((1, p), F32)
        g = jnp.zeros((p, p), F32)
        for ch in range(NCH):
            rows = chunk(ch)
            await_bytes(arr.at[k, rows], arr_sem.at[k, ch])
            a = arr[k, rows]
            ah, al = split(a)
            xh[rows, pl.ds(p, p)] = ah
            xl[rows, pl.ds(p, p)] = al
            n2 = n2 + jnp.sum(a * a, axis=0, keepdims=True)
            th = sth[:, rows]
            g = g + mm3((th, stl[:, rows]), (ah, al))
        which = lax.broadcasted_iota(jnp.int32, (8, p), 0)
        norms = jnp.where(which == 0, n1, jnp.where(which == 1, n2, 0.0))
        for i in range(n_row):
            part[i, pl.ds(0, sl)] = g[i * sl:(i + 1) * sl]
            part[i, pl.ds(sl, 8)] = norms

        @pl.when(k == 0)
        def _():
            pl.semaphore_wait(barrier, len(others) + 2 * n_row)

        for i in range(len(others)):
            scatter(k, i).start()
        total = part[r]
        for i in range(len(others) - 1, -1, -1):
            scatter(k, i).wait_recv()
            total = total + rs[k, i]
        root = jnp.sqrt(total[sl:sl + 8] + 1e-06)
        root1, root2 = root[0:1], root[1:2]
        on_diag = lax.broadcasted_iota(jnp.int32, (sl, p), 1) == lax.broadcasted_iota(jnp.int32, (sl, p), 0) + r * sl
        root_col = jnp.sum(jnp.where(on_diag, root1, 0.0), axis=1, keepdims=True)
        ag[k, pl.ds(pl.multiple_of(r * sl, sl), sl)] = total[:sl] / (root_col * root2)
        for i in range(len(others)):
            gather(k, i).start()
        for d in range(1, ROUNDS):
            there, copy = across(k - 1, d - 1)

            @pl.when(there & (k >= d))
            def _():
                copy.start()

        for i in range(len(others) - 1, -1, -1):
            gather(k, i).wait_recv()

        @pl.when(k > 0)
        def _():
            await_bytes(arr.at[k, pl.ds(m + vr, 2 * vr)], varr_sem.at[k])

        for d in range(1, ROUNDS):
            @pl.when(even & (k >= d))
            def _():
                send_to_owner(k, d)

        coupling = ag[k]
        strength = jnp.sqrt(jnp.sum(coupling * coupling, keepdims=True))
        flipped = coupling.T
        p1, q12, q12t, p2 = turn_blocks(coupling / (1.0 + strength), flipped / (1.0 + strength), eye)
        chosen = jnp.full((1, p), plan_ref[0, k], jnp.int32) == 1
        for ref, top, bottom in (
            (qm, jnp.where(chosen, q12, p1), jnp.where(chosen, p2, -q12t)),
            (qs, jnp.where(chosen, p1, q12), jnp.where(chosen, -q12t, p2)),
        ):
            for at, piece in ((0, top), (p, bottom)):
                hi, lo = split(piece)
                ref[pl.ds(at, p)] = hi
                ref[pl.ds(2 * p + at, p)] = hi
                ref[pl.ds(4 * p + at, p)] = lo
        @pl.when(k < last)
        def _():
            for ch in range(NCH):
                mov[k, chunk(ch)] = mm(lhs_rows(ch * rc, rc), qm[...])
                move_x(k, ch).start()

        @pl.when(k == last)
        def _():
            quarter = m // 4
            mov[last, pl.ds(0, quarter)] = mm(lhs_rows(0, quarter), qm[...])
            move_x_last(0).start()
            mov[last, pl.ds(quarter, quarter)] = mm(lhs_rows(quarter, quarter), qm[...])
            mov[last, pl.ds(2 * quarter, 2 * quarter)] = mm(lhs_rows(2 * quarter, 2 * quarter), qm[...])
            t = mov[last, pl.ds(0, m)]
            nsend[1] = jnp.broadcast_to(jnp.sum(t * t, axis=0, keepdims=True), (8, p))
            for i in range(n_row):
                norm_move(i).start()

            @pl.when(odd)
            def _():
                mov[last, pl.ds(m, nv)] = mm(lhs_of(vst[last], arr[last, pl.ds(m, nv)]), qm[...])
                last_slices.start()
                for d in range(3):
                    there, copy = across(last, d)

                    @pl.when(there)
                    def _():
                        copy.start()

            move_x_last(1).start()

        for ch in range(NCH):
            stay[chunk(ch)] = mm(lhs_rows(ch * rc, rc), qs[...])

        @pl.when(k < last)
        def _():
            v_lhs = lhs_of(vst[k], arr[k, pl.ds(m, nv)])
            mov[k, pl.ds(m, nv)] = mm(v_lhs, qm[...])
            vst[k + 1] = mm(v_lhs, qs[...])
            move_v(k).start()

        for j in range(qpr):
            @pl.when((lag[j] <= k) & (k < last))
            def _():
                @pl.when(lag[j] >= 1)
                def _():
                    await_bytes(va.at[k, j], va_recv.at[k, j])

                for ch in range(NCH):
                    rows = pl.ds(ch * wc, wc)
                    block = lhs_of(vs[j, rows], va[k, j, rows])
                    vmov[k, j, rows] = mm(block, qm[...])
                    vs[j, rows] = mm(block, qs[...])

                @pl.when(even)
                def _():
                    pass_block(k, j).start()

        for i in range(len(others)):
            scatter(k, i).wait_send()
            gather(k, i).wait_send()
        return carry

    lax.fori_loop(0, ROUNDS, one_round, 0)

    t = stay[...]
    nsend[0] = jnp.broadcast_to(jnp.sum(t * t, axis=0, keepdims=True), (8, p))
    for i in range(len(others)):
        norm_stay(i).start()
    pltpu.make_async_copy(nsend.at[0], nrecv.at[0, r], n_recv.at[0]).start()
    xo_ref[:, pl.ds(0, p)] = t

    for j in range(qpr):
        @pl.when((lag[j] >= 1) & (lag[j] <= 2))
        def _():
            await_bytes(va.at[last, j], va_recv.at[last, j])

        @pl.when((lag[j] <= 2) & even)
        def _():
            for ch in range(NCH):
                rows = pl.ds(ch * wc, wc)
                vmov[last, j, rows] = mm(lhs_of(vs[j, rows], va[last, j, rows]), qm[...])
            last_block(j).start()

    @pl.when(even)
    def _():
        await_bytes(vfin, varr_sem.at[ROUNDS])
        for d in range(1, 4):
            send_to_owner(None, d)

    for j in range(qpr):
        @pl.when(lag[j] <= 2)
        def _():
            for ch in range(NCH):
                rows = pl.ds(ch * wc, wc)
                vo_ref[pl.ds(j * width + ch * wc, wc), pl.ds(0, p)] = mm(
                    lhs_of(vs[j, rows], va[last, j, rows]), qs[...]
                )

    for panel in range(2):
        await_bytes(nrecv.at[panel], n_recv.at[panel])
        sums = nrecv[panel, 0]
        for i in range(1, n_row):
            sums = sums + nrecv[panel, i]
        so_ref[:, pl.ds(panel * p, p)] = jnp.sqrt(sums[0:1] / (m * n_row))

    for i in range(len(others)):
        norm_stay(i).wait_send()
    for i in range(n_row):
        norm_move(i).wait_send()
    for k in range(last):
        for ch in range(NCH):
            move_x(k, ch).wait_send()
        move_v(k).wait_send()
    @pl.when(odd)
    def _():
        last_slices.wait_send()

    for k in range(ROUNDS):
        for d in range(k + 1):
            there, copy = across(k, d)

            @pl.when(there)
            def _():
                copy.wait_send()

    @pl.when(even)
    def _():
        for k in range(1, ROUNDS):
            for d in range(1, k + 1):
                sent_to_owner(k, d)
        for d in range(1, 4):
            sent_to_owner(None, d)

    for k in range(last):
        for j in range(qpr):
            @pl.when(even & (lag[j] <= k))
            def _():
                pass_block(k, j).wait_send()

    for j in range(qpr):
        @pl.when((lag[j] <= 2) & even)
        def _():
            last_block(j).wait_send()

        @pl.when((lag[j] >= 1) & (lag[j] <= 3))
        def _():
            await_bytes(vo_ref.at[pl.ds(j * width, width), pl.ds(p, p)], vf_recv.at[j])

    for ch in range(NCH):
        move_x_last(ch).wait_send()
        move_x_last(ch).wait_recv()


def write_out(x_ref, v_ref, s_ref, xo_hbm, vo_hbm, so_ref, sem):
    copies = []
    step = x_ref.shape[0] // 4
    for src, dst in ((v_ref, vo_hbm), (x_ref, xo_hbm)):
        for start in range(0, src.shape[0], step):
            rows = pl.ds(start, step)
            copies.append(pltpu.make_async_copy(src.at[rows], dst.at[rows], sem.at[len(copies)]))
    for copy in copies:
        copy.start()
    so_ref[...] = s_ref[...]
    for copy in copies:
        copy.wait()


def per_device(activations, plan):
    n_row, n_col = lax.axis_size("row"), lax.axis_size("col")
    m, width = activations.shape
    p = width // 2
    sl = p // n_row
    vr = width // n_row
    rows = m + 3 * vr
    qpr = n_col // n_row
    dma = pltpu.SemaphoreType.DMA
    vmem = pl.BlockSpec(memory_space=pltpu.VMEM)
    shapes = (
        jax.ShapeDtypeStruct((m, width), F32),
        jax.ShapeDtypeStruct((qpr * width, width), F32),
        jax.ShapeDtypeStruct((1, width), F32),
    )
    results = pl.pallas_call(
        functools.partial(kernel, n_row, n_col),
        out_shape=shapes,
        in_specs=[pl.BlockSpec(memory_space=pltpu.SMEM), pl.BlockSpec(memory_space=pltpu.HBM)],
        out_specs=(vmem, vmem, vmem),
        scratch_shapes=[
            pltpu.VMEM((m, p), F32),
            pltpu.VMEM((ROUNDS, 3 * vr, p), F32),
            pltpu.VMEM((ROUNDS, rows, p), F32),
            pltpu.VMEM((ROUNDS, rows, p), F32),
            pltpu.VMEM((m, width), BF16),
            pltpu.VMEM((m, width), BF16),
            pltpu.VMEM((p, m), BF16),
            pltpu.VMEM((p, m), BF16),
            pltpu.VMEM((3 * width, p), BF16),
            pltpu.VMEM((3 * width, p), BF16),
            pltpu.VMEM((n_row, sl + 8, p), F32),
            pltpu.VMEM((ROUNDS, n_row - 1, sl + 8, p), F32),
            pltpu.VMEM((ROUNDS, p, p), F32),
            pltpu.VMEM((qpr, width, p), F32),
            pltpu.VMEM((ROUNDS, qpr, width, p), F32),
            pltpu.VMEM((ROUNDS, qpr, width, p), F32),
            pltpu.VMEM((3 * vr, p), F32),
            pltpu.VMEM((2, 8, p), F32),
            pltpu.VMEM((2, n_row, 8, p), F32),
            dma,
            dma((ROUNDS + 1, NCH)),
            dma((ROUNDS + 1,)),
            dma((ROUNDS, NCH)),
            dma((ROUNDS,)),
            dma((n_row - 1,)),
            dma((n_row - 1,)),
            dma((n_row - 1,)),
            dma((n_row - 1,)),
            dma((ROUNDS, 2)),
            dma((3,)),
            dma((ROUNDS, 3)),
            dma((ROUNDS, qpr)),
            dma((qpr,)),
            dma((ROUNDS, qpr)),
            dma((2, n_row)),
            dma((2,)),
        ],
        compiler_params=pltpu.CompilerParams(collective_id=0, has_side_effects=True, vmem_limit_bytes=48 * 2**20),
    )(pltpu.with_memory_space_constraint(plan.T, pltpu.HBM), pltpu.with_memory_space_constraint(activations, pltpu.HBM))
    hbm = pl.BlockSpec(memory_space=pltpu.HBM)
    anywhere = pl.BlockSpec(memory_space=pl.ANY)
    rotated, vectors, spread = pl.pallas_call(
        write_out,
        out_shape=shapes,
        in_specs=[anywhere, anywhere, vmem],
        out_specs=(hbm, hbm, vmem),
        scratch_shapes=[dma((4 * (qpr + 1),))],
        compiler_params=pltpu.CompilerParams(vmem_limit_bytes=2**20),
    )(*results)
    return rotated, vectors, spread.reshape(width)


def solution(mesh):
    in_specs = (P("row", "col"), P(None, "col"))
    out_specs = (P("row", "col"), P("row", "col"), P("col"))
    return jax.shard_map(
        per_device, mesh=mesh, in_specs=in_specs, out_specs=out_specs, check_vma=False
    )
```
